128 devices in a mesh: rel: 4 (over z), ent: 32 (over y, x, core).
Axes of the slice: x: 4, y: 4, z: 4, core: 2. Of those that a mesh axis runs over, the one named last changes fastest.
Arguments:
- features: bfloat16 [16384, 512], P('ent'), may hold values from -6 to 6
- w_self: bfloat16 [512, 512], replicated, may hold values from -0.25 to 0.25
- basis_mats: bfloat16 [16384, 512], replicated, may hold values from -0.046875 to 0.046875
- basis_coeffs: float32 [1000, 32], replicated, may hold values from -5 to 5
- group_rels: int32 [1000], P('rel'), may hold values from 0 to 999, each once
- rel_local: int32 [65536], P(('rel', 'ent')), may hold values from 0 to 249
- edge_src: int32 [65536], P(('rel', 'ent')), may hold values from 0 to 16383, as said below
- edge_dst: int32 [65536], P(('rel', 'ent')), may hold values from 0 to 16383, as said below
- block_counts: int32 [4, 32, 32], P('rel', 'ent'), may hold values from 1 to 16, as said below
- cotangent: bfloat16 [16384, 512], P('ent'), may hold values from -6 to 6
Outputs:
- activations: bfloat16 [16384, 512], P('ent')
- grad_features: bfloat16 [16384, 512], P('ent')
- grad_basis: float32 [16384, 512], P(('rel', 'ent'))
The draws below stay inside these ranges and needn't reach their ends.
Inputs may be any that keep to these rules, and one draw needn't show every extreme that they name: `edge_src`: slot i's source is owned by ent index (i // 512) % 32: it lies in [that index * 512, that index * 512 + 512). `edge_dst`: slot i's destination is owned by block index k = (i % 512) // 16: it lies in [k * 512, k * 512 + 512); within each aligned block of 16 slots the destinations are non-decreasing; the live slots of a block are its first block_counts ones. `block_counts`: one relation group, drawn from the seed, has every block full.
All inputs are finite; a program needn't handle non-finite values.
Results may differ from the reference program's by a relative error of at most 0.0059.
Values may be sent and summed in bfloat16 or wider, within the bound.
A program may use at most 192 MiB of HBM per device.

```python
import jax
import jax.numpy as jnp
from jax import lax

D = 512
B = 32
RELS = 1000
ENT_DEV = 512
SLOT_DEV = 512
ENTS = 16384
CAP = 16
RPG = 250
EDGE_SLOTS = 65536
N_REL = 4
N_ENT = 32


def draw_edge_src(key, part):
    total_slots = SLOT_DEV * N_REL * N_ENT
    positions = jnp.arange(total_slots, dtype=jnp.int32)
    owner = positions // SLOT_DEV % N_ENT
    offsets = jax.random.randint(jax.random.fold_in(key, 11), (total_slots,), 0, ENT_DEV)
    return (owner * ENT_DEV + offsets).astype(jnp.int32)


def draw_edge_dst(key, part):
    block_cap = SLOT_DEV // N_ENT
    offsets = jax.random.randint(jax.random.fold_in(key, 13), (N_REL * N_ENT, N_ENT, block_cap), 0, ENT_DEV)
    offsets = jnp.sort(offsets, axis=-1)
    owner = jnp.arange(N_ENT, dtype=jnp.int32)[None, :, None]
    return (owner * ENT_DEV + offsets).reshape(-1).astype(jnp.int32)


def draw_block_counts(key, part):
    block_cap = SLOT_DEV // N_ENT
    heavy = jax.random.randint(jax.random.fold_in(key, 7), (), 0, N_REL)
    others = jax.random.randint(jax.random.fold_in(key, 8), (N_REL, N_ENT, N_ENT), 1, block_cap + 1)
    groups = jnp.arange(N_REL, dtype=jnp.int32)[:, None, None]
    return jnp.where(groups == heavy, block_cap, others).astype(jnp.int32)


def with_ends(result, stream_key, low, high):
    place = [jax.random.randint(jax.random.fold_in(stream_key, axis), (), 0, length) for axis, length in enumerate(result.shape)]
    widest = result.shape.index(max(result.shape))
    neighbour = place[:widest] + [(place[widest] + 1) % result.shape[widest]] + place[widest + 1:]
    return result.at[tuple(place)].set(low).at[tuple(neighbour)].set(high)


def level_of(own_key, extent, shards, least, largest):
    def one(position, shards_of):
        steps = jax.random.uniform(jax.random.fold_in(jax.random.fold_in(own_key, 6), position), (shards_of,), jnp.float32, least / len(shards), largest / len(shards))
        return jnp.repeat(jnp.exp(steps), extent[position] // shards_of).reshape((-1,) + (1,) * (len(extent) - position - 1))

    gain = one(*shards[0])
    for cut in shards[1:]:
        gain = gain * one(*cut)
    return gain


def noise(key, extent, width, bound, pieces=(), held_as=jnp.bfloat16):
    entries = jax.random.normal(key, extent, jnp.float32) * width
    if len(pieces) > 0:
        entries = level_of(key, extent, pieces, -0.22, 0.18) * entries
    return jnp.clip(entries, min=-bound, max=bound).astype(held_as)


def setup_inputs(seed: int = 0) -> dict:
    key_list = jax.random.split(jax.random.key(seed), 11)
    features = noise(key_list[0], (ENTS, D), 1.0, 6.0, ((0, 32),))
    w_self = noise(key_list[1], (D, D), D ** -0.5, 0.25)
    basis_mats = noise(key_list[2], (B * D, D), (B * D) ** -0.5, 0.046875)
    basis_coeffs = noise(key_list[3], (RELS, B), 1.0, 5.0, (), jnp.float32)
    group_rels = jax.random.permutation(key_list[4], RELS).astype(jnp.int32)
    rel_local = with_ends(jax.random.randint(key_list[5], (EDGE_SLOTS,), 0, RPG), jax.random.fold_in(key_list[5], 1), 0, RPG - 1).astype(jnp.int32)
    edge_src = draw_edge_src(jax.random.fold_in(key_list[10], 71), 0)
    edge_dst = draw_edge_dst(jax.random.fold_in(key_list[10], 71), 0)
    block_counts = draw_block_counts(jax.random.fold_in(key_list[10], 71), 0)
    cotangent = noise(key_list[9], (ENTS, D), 1.0, 6.0, ((0, 32),))
    return dict(features=features, w_self=w_self, basis_mats=basis_mats, basis_coeffs=basis_coeffs, group_rels=group_rels, rel_local=rel_local, edge_src=edge_src, edge_dst=edge_dst, block_counts=block_counts, cotangent=cotangent)


def reference(features, w_self, basis_mats, basis_coeffs, group_rels, rel_local, edge_src, edge_dst, block_counts, cotangent):
    ent_total = features.shape[0]
    block_total = N_REL * N_ENT
    slot_pos = jnp.arange(SLOT_DEV, dtype=jnp.int32) % CAP

    def block_data(index):
        group = index // N_ENT
        sender = index % N_ENT
        row_start = index * SLOT_DEV
        local_rel = lax.dynamic_slice_in_dim(rel_local, row_start, SLOT_DEV)
        src_block = lax.dynamic_slice_in_dim(edge_src, row_start, SLOT_DEV)
        limits = jnp.repeat(block_counts[group, sender], CAP, total_repeat_length=SLOT_DEV)
        is_live = slot_pos < limits
        rel_coef = basis_coeffs[group_rels[group * RPG + local_rel]]
        src_rows = features[src_block].astype(jnp.float32)
        mixed = (rel_coef[:, :, None] * src_rows[:, None, :]).reshape(SLOT_DEV, B * D).astype(jnp.bfloat16)
        return mixed, rel_coef, is_live

    def forward_block(index):
        mixed, rel_coef, is_live = block_data(index)
        product = jnp.dot(mixed, basis_mats, preferred_element_type=jnp.float32)
        return (product * is_live.astype(jnp.float32)[:, None]).astype(jnp.bfloat16)

    block_ids = jnp.arange(block_total, dtype=jnp.int32)
    messages = lax.map(forward_block, block_ids).reshape(-1, D)
    all_pos = jnp.arange(EDGE_SLOTS, dtype=jnp.int32) % CAP
    live_all = all_pos < jnp.repeat(block_counts.reshape(-1), CAP, total_repeat_length=EDGE_SLOTS)
    targets = jnp.where(live_all, edge_dst, ent_total)
    sums = jax.ops.segment_sum(messages.astype(jnp.float32), targets, ent_total + 1)[:ent_total]
    in_degree = jax.ops.segment_sum(live_all.astype(jnp.float32), targets, ent_total + 1)[:ent_total]
    inverse = 1.0 / jnp.maximum(in_degree, 1.0)
    pre_act = jnp.dot(features, w_self, preferred_element_type=jnp.float32) + sums * inverse[:, None]
    sigmoid_pre = jax.nn.sigmoid(pre_act)
    activations = (pre_act * sigmoid_pre).astype(jnp.bfloat16)
    grad_pre = (cotangent.astype(jnp.float32) * (sigmoid_pre * (1.0 + pre_act * (1.0 - sigmoid_pre)))).astype(jnp.bfloat16)
    grad_scaled = (grad_pre.astype(jnp.float32) * inverse[:, None]).astype(jnp.bfloat16)
    grad_back = jnp.where(live_all[:, None], grad_scaled[edge_dst], jnp.zeros((), jnp.bfloat16))

    def backward_block(carry, index):
        mixed, rel_coef, is_live = block_data(index)
        grad_block = lax.dynamic_slice_in_dim(grad_back, index * SLOT_DEV, SLOT_DEV)
        grad_mixed = lax.dot_general(grad_block, basis_mats, (((1,), (1,)), ((), ())), preferred_element_type=jnp.float32)
        grad_rows = jnp.sum(grad_mixed.reshape(SLOT_DEV, B, D) * rel_coef[:, :, None], axis=1)
        carry = carry + lax.dot_general(mixed, grad_block, (((0,), (0,)), ((), ())), preferred_element_type=jnp.float32)
        return carry, grad_rows

    grad_basis, grad_rows = lax.scan(backward_block, jnp.zeros((B * D, D), jnp.float32), block_ids)
    grad_src = jax.ops.segment_sum(grad_rows.reshape(-1, D), edge_src, ent_total)
    self_part = lax.dot_general(grad_pre, w_self, (((1,), (1,)), ((), ())), preferred_element_type=jnp.float32)
    grad_features = (self_part + grad_src).astype(jnp.bfloat16)
    return activations, grad_features, grad_basis
```

```python
import jax
import jax.numpy as jnp
from jax import lax
from jax.sharding import PartitionSpec as P

BF = jnp.bfloat16
F32 = jnp.float32


def dot(a, b, dims=((1,), (0,)), precision=None):
    return lax.dot_general(
        a, b, (dims, ((), ())), preferred_element_type=F32, precision=precision
    )


def swap(x, axis):
    return lax.all_to_all(x, axis, split_axis=0, concat_axis=0, tiled=True)


def per_device(
    features,
    w_self,
    basis_mats,
    basis_coeffs,
    group_rels,
    rel_local,
    edge_src,
    edge_dst,
    block_counts,
    cotangent,
):
    n_ent, width = features.shape
    ent_count = lax.axis_size("ent")
    rel_count = lax.axis_size("rel")
    slots = rel_local.shape[0]
    cap = slots // ent_count
    bases = basis_coeffs.shape[1]
    rels = basis_coeffs.shape[0]
    part = width // rel_count
    q = lax.axis_index("rel")
    s = lax.axis_index("ent")
    all_slots = slots * rel_count

    pos = jnp.arange(slots, dtype=jnp.int32)
    limits = jnp.repeat(block_counts.reshape(ent_count), cap, total_repeat_length=slots)
    live = pos % cap < limits
    src_own = edge_src - s * n_ent
    dst_own = jnp.where(live, edge_dst - pos // cap * n_ent, n_ent)
    rel_own = group_rels[rel_local]
    meta = jnp.stack([src_own, dst_own, rel_own])
    meta = lax.all_gather(meta, "rel").reshape(rel_count, 3, ent_count, cap)
    meta = meta.transpose(2, 1, 0, 3)
    src = meta[:, 0].reshape(all_slots)
    arrived = swap(meta[:, 1:], "ent")
    dst = arrived[:, 0].reshape(all_slots)
    rel = arrived[:, 1].reshape(all_slots)

    ids = jnp.arange(n_ent, dtype=jnp.int32)[:, None]
    pick_src = (ids == src[None, :]).astype(BF)
    feat_part = lax.dynamic_slice_in_dim(features, q * part, part, 1)
    rows = dot(pick_src, feat_part, ((0,), (0,))).astype(BF)
    rows = swap(rows.reshape(ent_count, rel_count * cap, part), "ent").reshape(all_slots, part)

    pick_rel = (jnp.arange(rels, dtype=jnp.int32)[:, None] == rel[None, :]).astype(F32)
    coef_t = dot(basis_coeffs, pick_rel, ((0,), (0,)), lax.Precision.HIGHEST)
    pick = (ids == dst[None, :]).astype(BF)
    degree = jnp.sum(pick, axis=1, dtype=F32)
    inverse = (1.0 / jnp.maximum(degree, 1.0))[:, None]
    mixed_t = (
        (coef_t[:, None, :] * rows.T.astype(F32)[None])
        .reshape(bases * part, all_slots)
        .astype(BF)
    )
    agg = dot(pick, mixed_t, ((1,), (1,))).astype(BF)
    basis_part = lax.dynamic_slice_in_dim(
        basis_mats.reshape(bases, width, width), q * part, part, 1
    ).reshape(bases * part, width)
    partial = dot(agg, basis_part).astype(BF)
    partial = swap(partial.reshape(n_ent, rel_count, part).transpose(1, 0, 2), "rel")
    sums = jnp.sum(partial.astype(F32), axis=0)

    w_part = lax.dynamic_slice_in_dim(w_self, q * part, part, 1)
    cot = lax.dynamic_slice_in_dim(cotangent, q * part, part, 1).astype(F32)
    pre = dot(features, w_part) + sums * inverse
    sig = jax.nn.sigmoid(pre)
    act = (pre * sig).astype(BF)
    grad_pre = (cot * (sig * (1.0 + pre * (1.0 - sig)))).astype(BF)
    act = lax.all_gather(act, "rel", axis=1, tiled=True)
    grad_pre = lax.all_gather(grad_pre, "rel", axis=1, tiled=True)
    scaled = (grad_pre.astype(F32) * inverse).astype(BF)

    basis_terms = dot(agg, scaled, ((0,), (0,))).astype(BF)
    basis_terms = swap(basis_terms.reshape(ent_count, part, width), "ent")
    block = jnp.sum(basis_terms.astype(F32), axis=0)
    per_rel = bases // rel_count
    routes = [
        (r * ent_count + b, (b // per_rel) * ent_count + (b % per_rel) * rel_count + r)
        for r in range(rel_count)
        for b in range(bases)
    ]
    grad_basis = lax.ppermute(block, ("rel", "ent"), routes)

    back_t = dot(basis_part, scaled, ((1,), (1,))).astype(BF)
    spread = dot(back_t, pick).reshape(bases, part, all_slots)
    grad_rows = jnp.sum(spread * coef_t[:, None, :], axis=0).astype(BF).T
    grad_rows = swap(grad_rows.reshape(ent_count, rel_count * cap, part), "ent")
    w_rows = lax.dynamic_slice_in_dim(w_self, q * part, part, 0)
    grad_part = dot(grad_pre, w_rows, ((1,), (1,))) + dot(
        pick_src, grad_rows.reshape(all_slots, part)
    )
    grad_features = lax.all_gather(grad_part.astype(BF), "rel", axis=1, tiled=True)
    return act, grad_features, grad_basis


def solution(mesh):
    placed = (
        P("ent", None),
        P(),
        P(),
        P(),
        P("rel"),
        P(("rel", "ent")),
        P(("rel", "ent")),
        P(("rel", "ent")),
        P("rel", "ent", None),
        P("ent", None),
    )
    return jax.shard_map(
        per_device,
        mesh=mesh,
        in_specs=placed,
        out_specs=(P("ent", None), P("ent", None), P(("rel", "ent"), None)),
        check_vma=False,
    )
```

```python
import functools

import jax
import jax.numpy as jnp
from jax import lax
from jax.experimental import pallas as pl
from jax.experimental.pallas import tpu as pltpu
from jax.sharding import PartitionSpec as P

BF = jnp.bfloat16
F32 = jnp.float32
I32 = jnp.int32
MIB = 1 << 20


def dot(a, b, dims=((1,), (0,))):
    return lax.dot_general(a, b, (dims, ((), ())), preferred_element_type=F32)


def swap(x, axis):
    return lax.all_to_all(x, axis, split_axis=0, concat_axis=0, tiled=True)


def one_hot(count, row):
    ids = lax.broadcasted_iota(I32, (count, row.shape[1]), 0)
    return (ids == row).astype(F32).astype(BF)


def split3(x):
    hi = x.astype(BF)
    rest = x - hi.astype(F32)
    mid = rest.astype(BF)
    lo = (rest - mid.astype(F32)).astype(BF)
    return hi, mid, lo


def forward_kernel(
    group,
    dst_ref,
    rel_ref,
    rows_ref,
    coef_ref,
    basis_hbm,
    part_ref,
    agg_ref,
    inv_ref,
    coef_t_ref,
    basis,
    table,
    pick,
    rows_t,
    acc,
    sem,
):
    q = lax.axis_index("rel")
    bases, part, width = basis.shape
    rels = coef_ref.shape[0]
    n_ent = pick.shape[0]
    load = pltpu.make_async_copy(
        basis_hbm.at[:, pl.ds(pl.multiple_of(q * part, part), part), :], basis, sem
    )
    load.start()
    table[...] = jnp.zeros_like(table)
    table[:rels, :bases] = coef_ref[...]
    which = one_hot(table.shape[0], rel_ref[...])
    hi, mid, lo = split3(table[...])
    coef_t = dot(hi, which, ((0,), (0,))) + dot(mid, which, ((0,), (0,)))
    coef_t = coef_t + dot(lo, which, ((0,), (0,)))
    coef_t_ref[...] = coef_t[:bases, :]
    pick[...] = one_hot(n_ent, dst_ref[...])
    degree = dot(pick[...], jnp.ones((pick.shape[1], part), BF))
    inv_ref[...] = 1.0 / jnp.maximum(degree, 1.0)
    rows_t[...] = rows_ref[...].astype(F32).T
    acc[...] = jnp.zeros_like(acc)
    load.wait()

    def step(i, _):
        mixed = jnp.concatenate(
            [
                (rows_t[...] * coef_t_ref[pl.ds(i * group + g, 1), :]).astype(BF)
                for g in range(group)
            ],
            axis=0,
        )
        agg = dot(pick[...], mixed, ((1,), (1,)))
        agg_b = agg.astype(BF)
        weights = basis[pl.ds(i * group, group)].reshape(group * part, width)
        acc[...] += dot(agg_b, weights)
        agg_ref[pl.ds(i * group, group)] = agg.T.astype(BF).reshape(group, part, n_ent)
        return 0

    lax.fori_loop(0, bases // group, step, 0)
    for r in range(width // part):
        part_ref[r] = acc[:, r * part : (r + 1) * part].astype(BF)


def forward(dst, rel, rows, coeffs, basis_mats, n_ent):
    all_slots, part = rows.shape
    rels, bases = coeffs.shape
    width = basis_mats.shape[1]
    vm = pl.BlockSpec(memory_space=pltpu.VMEM)
    return pl.pallas_call(
        functools.partial(forward_kernel, 2),
        out_shape=(
            jax.ShapeDtypeStruct((width // part, n_ent, part), BF),
            jax.ShapeDtypeStruct((bases, part, n_ent), BF),
            jax.ShapeDtypeStruct((n_ent, part), F32),
            jax.ShapeDtypeStruct((bases, all_slots), F32),
        ),
        in_specs=[vm, vm, vm, vm, pl.BlockSpec(memory_space=pl.ANY)],
        out_specs=(vm, vm, vm, vm),
        scratch_shapes=[
            pltpu.VMEM((bases, part, width), BF),
            pltpu.VMEM((1024, 128), F32),
            pltpu.VMEM((n_ent, all_slots), BF),
            pltpu.VMEM((part, all_slots), F32),
            pltpu.VMEM((n_ent, width), F32),
            pltpu.SemaphoreType.DMA,
        ],
        compiler_params=pltpu.CompilerParams(vmem_limit_bytes=56 * MIB),
    )(dst, rel, rows, coeffs, basis_mats.reshape(bases, width, width))


def terms_kernel(agg_ref, scaled_ref, out_ref):
    group, part, n_ent = agg_ref.shape
    terms = dot(agg_ref[...].reshape(group * part, n_ent), scaled_ref[...])
    out_ref[...] = terms.astype(BF).reshape(out_ref.shape)


def basis_terms(agg, scaled):
    bases, part, n_ent = agg.shape
    width = scaled.shape[1]
    group = 8
    return pl.pallas_call(
        terms_kernel,
        out_shape=jax.ShapeDtypeStruct((bases, part, width), BF),
        grid=(bases // group,),
        in_specs=[
            pl.BlockSpec((group, part, n_ent), lambda i: (i, 0, 0)),
            pl.BlockSpec((n_ent, width), lambda i: (0, 0)),
        ],
        out_specs=pl.BlockSpec((group, part, width), lambda i: (i, 0, 0)),
        compiler_params=pltpu.CompilerParams(vmem_limit_bytes=32 * MIB),
    )(agg, scaled)


def backward_kernel(
    group, scaled_ref, dst_ref, coef_t_ref, basis_hbm, out_ref, basis, pick, acc, sem
):
    q = lax.axis_index("rel")
    bases, part, width = basis.shape
    load = pltpu.make_async_copy(
        basis_hbm.at[:, pl.ds(pl.multiple_of(q * part, part), part), :], basis, sem
    )
    load.start()
    pick[...] = one_hot(pick.shape[0], dst_ref[...])
    acc[...] = jnp.zeros_like(acc)
    load.wait()

    def step(i, _):
        weights = basis[pl.ds(i * group, group)].reshape(group * part, width)
        back = dot(weights, scaled_ref[...], ((1,), (1,))).astype(BF)
        spread = dot(back, pick[...])
        total = acc[...]
        for g in range(group):
            total += (
                spread[g * part : (g + 1) * part] * coef_t_ref[pl.ds(i * group + g, 1), :]
            )
        acc[...] = total
        return 0

    lax.fori_loop(0, bases // group, step, 0)
    out_ref[...] = acc[...].T.astype(BF)


def backward(scaled, dst, coef_t, basis_mats):
    bases, all_slots = coef_t.shape
    n_ent, width = scaled.shape
    part = 128
    vm = pl.BlockSpec(memory_space=pltpu.VMEM)
    return pl.pallas_call(
        functools.partial(backward_kernel, 4),
        out_shape=jax.ShapeDtypeStruct((all_slots, part), BF),
        in_specs=[vm, vm, vm, pl.BlockSpec(memory_space=pl.ANY)],
        out_specs=vm,
        scratch_shapes=[
            pltpu.VMEM((bases, part, width), BF),
            pltpu.VMEM((n_ent, all_slots), BF),
            pltpu.VMEM((part, all_slots), F32),
            pltpu.SemaphoreType.DMA,
        ],
        compiler_params=pltpu.CompilerParams(vmem_limit_bytes=56 * MIB),
    )(scaled, dst, coef_t, basis_mats.reshape(bases, width, width))


def per_device(
    features,
    w_self,
    basis_mats,
    basis_coeffs,
    group_rels,
    rel_local,
    edge_src,
    edge_dst,
    block_counts,
    cotangent,
):
    n_ent, width = features.shape
    ent_count = lax.axis_size("ent")
    rel_count = lax.axis_size("rel")
    slots = rel_local.shape[0]
    cap = slots // ent_count
    bases = basis_coeffs.shape[1]
    part = width // rel_count
    q = lax.axis_index("rel")
    s = lax.axis_index("ent")
    all_slots = slots * rel_count

    shape = (ent_count, cap)
    live = lax.broadcasted_iota(I32, shape, 1) < block_counts.reshape(ent_count, 1)
    src_own = edge_src.reshape(shape) - s * n_ent
    base = lax.broadcasted_iota(I32, shape, 0) * n_ent
    dst_own = jnp.where(live, edge_dst.reshape(shape) - base, n_ent)
    ids = jnp.arange(group_rels.shape[0], dtype=I32)
    rel_own = jnp.sum(
        jnp.where(rel_local[:, None] == ids[None, :], group_rels[None, :], 0), axis=1
    ).reshape(shape)
    meta = jnp.stack([src_own, dst_own, rel_own])
    meta = lax.all_gather(meta, "rel")
    meta = meta.transpose(2, 1, 0, 3)
    src = meta[:, 0].reshape(1, all_slots)
    arrived = swap(meta[:, 1:], "ent")
    dst = arrived[:, 0].reshape(1, all_slots)
    rel = arrived[:, 1].reshape(1, all_slots)

    pick_src = (jnp.arange(n_ent, dtype=I32)[:, None] == src).astype(BF)
    feat_part = lax.dynamic_slice_in_dim(features, q * part, part, 1)
    rows = dot(pick_src, feat_part, ((0,), (0,))).astype(BF)
    rows = swap(rows.reshape(ent_count, rel_count * cap, part), "ent").reshape(all_slots, part)

    partial, agg, inverse, coef_t = forward(dst, rel, rows, basis_coeffs, basis_mats, n_ent)
    partial = swap(partial, "rel")
    sums = jnp.sum(partial.astype(F32), axis=0)

    w_part = lax.dynamic_slice_in_dim(w_self, q * part, part, 1)
    cot = lax.dynamic_slice_in_dim(cotangent, q * part, part, 1).astype(F32)
    pre = dot(features, w_part) + sums * inverse
    sig = jax.nn.sigmoid(pre)
    act = (pre * sig).astype(BF)
    grad_pre = (cot * (sig * (1.0 + pre * (1.0 - sig)))).astype(BF)
    both = lax.all_gather(jnp.stack([act, grad_pre]), "rel")
    act = both[:, 0].transpose(1, 0, 2).reshape(n_ent, width)
    grad_pre = both[:, 1].transpose(1, 0, 2).reshape(n_ent, width)
    scaled = (grad_pre.astype(F32) * inverse[:, :1]).astype(BF)

    terms = swap(basis_terms(agg, scaled), "ent")
    block = jnp.sum(terms.astype(F32), axis=0)
    per_rel = bases // rel_count
    routes = [
        (r * ent_count + b, (b // per_rel) * ent_count + (b % per_rel) * rel_count + r)
        for r in range(rel_count)
        for b in range(bases)
    ]
    grad_basis = lax.ppermute(block, ("rel", "ent"), routes)

    grad_rows = backward(scaled, dst, coef_t, basis_mats)
    grad_rows = swap(grad_rows.reshape(ent_count, rel_count * cap, part), "ent")
    w_rows = lax.dynamic_slice_in_dim(w_self, q * part, part, 0)
    grad_part = dot(grad_pre, w_rows, ((1,), (1,))) + dot(
        pick_src, grad_rows.reshape(all_slots, part)
    )
    grad_features = lax.all_gather(grad_part.astype(BF), "rel", axis=1, tiled=True)
    return act, grad_features, grad_basis


def solution(mesh):
    placed = (
        P("ent", None),
        P(),
        P(),
        P(),
        P("rel"),
        P(("rel", "ent")),
        P(("rel", "ent")),
        P(("rel", "ent")),
        P("rel", "ent", None),
        P("ent", None),
    )
    return jax.shard_map(
        per_device,
        mesh=mesh,
        in_specs=placed,
        out_specs=(P("ent", None), P("ent", None), P(("rel", "ent"), None)),
        check_vma=False,
    )
```

```python
import functools

import jax
import jax.numpy as jnp
from jax import lax
from jax.experimental import pallas as pl
from jax.experimental.pallas import tpu as pltpu
from jax.sharding import PartitionSpec as P

BF = jnp.bfloat16
F32 = jnp.float32
I32 = jnp.int32
MIB = 1 << 20


def dot(a, b, dims=((1,), (0,))):
    return lax.dot_general(a, b, (dims, ((), ())), preferred_element_type=F32)


def swap(x, axis):
    return lax.all_to_all(x, axis, split_axis=0, concat_axis=0, tiled=True)


def one_hot(count, row):
    ids = lax.broadcasted_iota(I32, (count, row.shape[1]), 0)
    return (ids == row).astype(F32).astype(BF)


def split3(x):
    hi = x.astype(BF)
    rest = x - hi.astype(F32)
    mid = rest.astype(BF)
    lo = (rest - mid.astype(F32)).astype(BF)
    return hi, mid, lo


def forward_kernel(
    group,
    dst_ref,
    rel_ref,
    rows_ref,
    coef_ref,
    basis_hbm,
    part_ref,
    agg_ref,
    inv_ref,
    coef_t_ref,
    basis,
    table,
    pick,
    rows_t,
    acc,
    sem,
):
    q = lax.axis_index("rel")
    bases, part, width = basis.shape
    rels = coef_ref.shape[0]
    n_ent = pick.shape[0]
    load = pltpu.make_async_copy(
        basis_hbm.at[:, pl.ds(pl.multiple_of(q * part, part), part), :], basis, sem
    )
    load.start()
    table[...] = jnp.zeros_like(table)
    table[:rels, :bases] = coef_ref[...]
    which = one_hot(table.shape[0], rel_ref[...])
    hi, mid, lo = split3(table[...])
    coef_t = dot(hi, which, ((0,), (0,))) + dot(mid, which, ((0,), (0,)))
    coef_t = coef_t + dot(lo, which, ((0,), (0,)))
    coef_t_ref[...] = coef_t[:bases, :]
    pick[...] = one_hot(n_ent, dst_ref[...])
    degree = dot(pick[...], jnp.ones((pick.shape[1], part), BF))
    inv_ref[...] = 1.0 / jnp.maximum(degree, 1.0)
    rows_t[...] = rows_ref[...].astype(F32).T
    acc[...] = jnp.zeros_like(acc)
    load.wait()

    def step(i, _):
        mixed = jnp.concatenate(
            [
                (rows_t[...] * coef_t_ref[pl.ds(i * group + g, 1), :]).astype(BF)
                for g in range(group)
            ],
            axis=0,
        )
        agg = dot(pick[...], mixed, ((1,), (1,)))
        agg_b = agg.astype(BF)
        weights = basis[pl.ds(i * group, group)].reshape(group * part, width)
        acc[...] += dot(agg_b, weights)
        agg_ref[pl.ds(i * group, group)] = agg.T.astype(BF).reshape(group, part, n_ent)
        return 0

    lax.fori_loop(0, bases // group, step, 0)
    for r in range(width // part):
        part_ref[r] = acc[:, r * part : (r + 1) * part].astype(BF)


def forward(dst, rel, rows, coeffs, basis_mats, n_ent):
    all_slots, part = rows.shape
    rels, bases = coeffs.shape
    width = basis_mats.shape[1]
    vm = pl.BlockSpec(memory_space=pltpu.VMEM)
    return pl.pallas_call(
        functools.partial(forward_kernel, 2),
        out_shape=(
            jax.ShapeDtypeStruct((width // part, n_ent, part), BF),
            jax.ShapeDtypeStruct((bases, part, n_ent), BF),
            jax.ShapeDtypeStruct((n_ent, part), F32),
            jax.ShapeDtypeStruct((bases, all_slots), F32),
        ),
        in_specs=[vm, vm, vm, vm, pl.BlockSpec(memory_space=pl.ANY)],
        out_specs=(vm, vm, vm, vm),
        scratch_shapes=[
            pltpu.VMEM((bases, part, width), BF),
            pltpu.VMEM((1024, 128), F32),
            pltpu.VMEM((n_ent, all_slots), BF),
            pltpu.VMEM((part, all_slots), F32),
            pltpu.VMEM((n_ent, width), F32),
            pltpu.SemaphoreType.DMA,
        ],
        compiler_params=pltpu.CompilerParams(vmem_limit_bytes=56 * MIB),
    )(dst, rel, rows, coeffs, basis_mats.reshape(bases, width, width))


def remote(src, dst, send_sem, recv_sem, z, e):
    return pltpu.make_async_remote_copy(
        src_ref=src,
        dst_ref=dst,
        send_sem=send_sem,
        recv_sem=recv_sem,
        device_id=(z, e),
        device_id_type=pl.DeviceIdType.MESH,
    )


def finish_kernel(
    n_z,
    n_e,
    sums_ref,
    inv_ref,
    feat_ref,
    w_ref,
    cot_ref,
    src_ref,
    dst_ref,
    coef_t_ref,
    agg_hbm,
    basis_hbm,
    act_ref,
    gf_ref,
    gb_ref,
    sums_in,
    pre_in,
    scaled,
    scaled_sib,
    agg_own,
    agg_sib,
    basis,
    pick,
    pick_src,
    acc,
    term_out,
    term_in,
    row_out,
    row_in,
    load_sem,
    sums_send,
    sums_recv,
    act_send,
    act_recv,
    pre_send,
    pre_recv,
    agg_send,
    agg_recv,
    sib_send,
    sib_recv,
    term_send,
    term_recv,
    row_send,
    row_recv,
    gf_send,
    gf_recv,
):
    q = lax.axis_index("rel")
    e = lax.axis_index("ent")
    core = lax.rem(e, 2)
    chip = lax.div(e, 2)
    sib = e + 1 - 2 * core
    bases, part, width = basis.shape
    half = bases // 2
    n_chip = n_e // 2
    per_z = bases // n_z
    lanes = pl.ds(pl.multiple_of(q * part, part), part)

    def owner(b):
        return lax.div(b, per_z), lax.rem(b, per_z) * n_z + q

    my_b = q * per_z + lax.div(e, n_z)
    from_z = lax.rem(e, n_z)
    from_core = lax.div(my_b, half)
    self_owned = jnp.logical_and(from_z == q, from_core == core)

    barrier = pltpu.get_barrier_semaphore()

    def greet(z, peer):
        pl.semaphore_signal(
            barrier, inc=1, device_id=(z, peer), device_id_type=pl.DeviceIdType.MESH
        )

    for d in range(1, n_z):
        greet(lax.rem(q + d, n_z), e)

    def greet_plane(d, _):
        greet(q, lax.rem(e + d, n_e))
        return 0

    lax.fori_loop(1, n_e, greet_plane, 0)

    def greet_source(i, _):
        source = i * 2 + from_core

        @pl.when(jnp.logical_not(jnp.logical_and(from_z == q, source == e)))
        def _():
            greet(from_z, source)

        return 0

    lax.fori_loop(0, n_chip, greet_source, 0)

    load_basis = pltpu.make_async_copy(basis_hbm.at[:, lanes, :], basis, load_sem.at[0])
    load_basis.start()
    load_agg = pltpu.make_async_copy(
        agg_hbm.at[pl.ds(core * half, half)], agg_own, load_sem.at[1]
    )
    load_agg.start()
    w_part = w_ref[:, lanes]
    pre = dot(feat_ref[...], w_part)
    pl.semaphore_wait(barrier, n_z - 1 + n_e - 1 + half - self_owned.astype(I32))

    def sums_copy(d):
        z = lax.rem(q + d, n_z)
        return remote(
            sums_ref.at[z], sums_in.at[q], sums_send.at[d], sums_recv.at[q], z, e
        )

    def sums_wait(d):
        z = lax.rem(q + d, n_z)
        remote(
            sums_ref.at[z], sums_in.at[z], sums_send.at[d], sums_recv.at[z], z, e
        ).wait_recv()

    for d in range(1, n_z):
        sums_copy(d).start()
    agg_copy = remote(
        agg_hbm.at[pl.ds((1 - core) * half, half)],
        agg_sib,
        agg_send,
        agg_recv,
        q,
        sib,
    )
    agg_copy.start()
    pick[...] = one_hot(pick.shape[0], dst_ref[...])
    pick_src[...] = one_hot(pick.shape[0], src_ref[...])
    total = sums_ref[q].astype(F32)
    for d in range(1, n_z):
        sums_wait(d)
        total += sums_in[lax.rem(q + d, n_z)].astype(F32)
    inverse = inv_ref[...]
    pre = pre + total * inverse
    sig = jax.nn.sigmoid(pre)
    slope = sig * (1.0 + pre * (1.0 - sig))
    pre_in[q] = (cot_ref[:, lanes].astype(F32) * slope).astype(BF)

    def pre_copy(d, z_in):
        z = lax.rem(q + d, n_z)
        return remote(pre_in.at[q], pre_in.at[z_in], pre_send.at[d], pre_recv.at[z_in], z, e)

    def act_copy(d, z_in):
        z = lax.rem(q + d, n_z)
        at = pl.ds(pl.multiple_of(z_in * part, part), part)
        return remote(
            act_ref.at[:, lanes], act_ref.at[:, at], act_send.at[d], act_recv.at[z_in], z, e
        )

    for d in range(1, n_z):
        pre_copy(d, q).start()
    act_ref[:, lanes] = (pre * sig).astype(BF)
    for d in range(1, n_z):
        act_copy(d, q).start()
    for d in range(1, n_z):
        pre_copy(d, lax.rem(q + d, n_z)).wait_recv()
    for z in range(n_z):
        scaled[:, z * part : (z + 1) * part] = (pre_in[z].astype(F32) * inverse).astype(BF)
    sib_copy = remote(scaled, scaled_sib, sib_send, sib_recv, q, sib)
    sib_copy.start()
    w_rows = w_ref[lanes, :]
    grad = dot(pre_in[0], w_rows[:, :part], ((1,), (1,)))
    for z in range(1, n_z):
        grad += dot(pre_in[z], w_rows[:, z * part : (z + 1) * part], ((1,), (1,)))
    load_agg.wait()
    agg_copy.wait_recv()
    sib_copy.wait_recv()

    group = 4
    groups = half // group
    n_ent = agg_own.shape[2]

    def term_copy(i):
        z, peer = owner(core * half + i)
        return remote(
            term_out.at[i], term_in.at[chip], term_send.at[i], term_recv.at[chip], z, peer
        )

    def term_step(t, _):
        first = lax.rem(t + chip, groups) * group
        own = agg_own[pl.ds(first, group)].reshape(group * part, n_ent)
        other = agg_sib[pl.ds(first, group)].reshape(group * part, n_ent)
        terms = dot(own, scaled[...]) + dot(other, scaled_sib[...])
        term_out[pl.ds(first, group)] = terms.astype(BF).reshape(group, part, width)
        for g in range(group):
            i = first + g
            z, peer = owner(core * half + i)
            mine = jnp.logical_and(z == q, peer == e)

            @pl.when(mine)
            def _():
                term_in[chip] = term_out[i]

            @pl.when(jnp.logical_not(mine))
            def _():
                term_copy(i).start()

        return 0

    lax.fori_loop(0, groups, term_step, 0)
    acc[...] = jnp.zeros_like(acc)
    load_basis.wait()

    def step(i, _):
        weights = basis[pl.ds(i * group, group)].reshape(group * part, width)
        back = dot(weights, scaled[...], ((1,), (1,))).astype(BF)
        spread = dot(back, pick[...])
        rows = acc[...]
        for g in range(group):
            rows += spread[g * part : (g + 1) * part] * coef_t_ref[pl.ds(i * group + g, 1), :]
        acc[...] = rows
        return 0

    lax.fori_loop(0, bases // group, step, 0)
    row_out[...] = acc[...].T.astype(BF).reshape(row_out.shape)
    row_in[e] = row_out[e]

    def row_copy(peer, slot):
        return remote(
            row_out.at[peer], row_in.at[slot], row_send.at[peer], row_recv.at[slot], q, peer
        )

    def row_start(d, _):
        row_copy(lax.rem(e + d, n_e), e).start()
        return 0

    def row_wait(d, _):
        peer = lax.rem(e + d, n_e)
        row_copy(peer, peer).wait_recv()
        return 0

    lax.fori_loop(1, n_e, row_start, 0)
    lax.fori_loop(1, n_e, row_wait, 0)
    grad += dot(pick_src[...], row_in[...].reshape(pick_src.shape[1], part))
    gf_ref[:, lanes] = grad.astype(BF)

    def gf_copy(d, z_in):
        z = lax.rem(q + d, n_z)
        at = pl.ds(pl.multiple_of(z_in * part, part), part)
        return remote(
            gf_ref.at[:, lanes], gf_ref.at[:, at], gf_send.at[d], gf_recv.at[z_in], z, e
        )

    for d in range(1, n_z):
        gf_copy(d, q).start()

    def term_wait(i, _):
        source = i * 2 + from_core

        @pl.when(jnp.logical_not(jnp.logical_and(from_z == q, source == e)))
        def _():
            remote(
                term_out.at[0], term_in.at[i], term_send.at[0], term_recv.at[i], from_z, source
            ).wait_recv()

        return 0

    lax.fori_loop(0, n_chip, term_wait, 0)
    block = term_in[0].astype(F32)
    for i in range(1, n_chip):
        block += term_in[i].astype(F32)
    gb_ref[...] = block

    for d in range(1, n_z):
        z = lax.rem(q + d, n_z)
        act_copy(d, z).wait_recv()
        gf_copy(d, z).wait_recv()
        sums_copy(d).wait_send()
        pre_copy(d, q).wait_send()
        act_copy(d, q).wait_send()
        gf_copy(d, q).wait_send()
    agg_copy.wait_send()
    sib_copy.wait_send()

    def term_sent(i, _):
        z, peer = owner(core * half + i)

        @pl.when(jnp.logical_not(jnp.logical_and(z == q, peer == e)))
        def _():
            term_copy(i).wait_send()

        return 0

    lax.fori_loop(0, half, term_sent, 0)

    def row_sent(d, _):
        row_copy(lax.rem(e + d, n_e), e).wait_send()
        return 0

    lax.fori_loop(1, n_e, row_sent, 0)


def finish(sums, inverse, features, w_self, cotangent, src, dst, coef_t, agg, basis_mats):
    n_z = lax.axis_size("rel")
    n_e = lax.axis_size("ent")
    n_ent, width = features.shape
    bases, all_slots = coef_t.shape
    part = width // n_z
    half = bases // 2
    block = all_slots // n_e
    vm = pl.BlockSpec(memory_space=pltpu.VMEM)
    hbm = pl.BlockSpec(memory_space=pl.ANY)
    dma = pltpu.SemaphoreType.DMA
    return pl.pallas_call(
        functools.partial(finish_kernel, n_z, n_e),
        out_shape=(
            jax.ShapeDtypeStruct((n_ent, width), BF),
            jax.ShapeDtypeStruct((n_ent, width), BF),
            jax.ShapeDtypeStruct((part, width), F32),
        ),
        in_specs=[vm] * 8 + [hbm, hbm],
        out_specs=(vm, vm, vm),
        scratch_shapes=[
            pltpu.VMEM((n_z, n_ent, part), BF),
            pltpu.VMEM((n_z, n_ent, part), BF),
            pltpu.VMEM((n_ent, width), BF),
            pltpu.VMEM((n_ent, width), BF),
            pltpu.VMEM((half, part, n_ent), BF),
            pltpu.VMEM((half, part, n_ent), BF),
            pltpu.VMEM((bases, part, width), BF),
            pltpu.VMEM((n_ent, all_slots), BF),
            pltpu.VMEM((n_ent, all_slots), BF),
            pltpu.VMEM((part, all_slots), F32),
            pltpu.VMEM((half, part, width), BF),
            pltpu.VMEM((n_e // 2, part, width), BF),
            pltpu.VMEM((n_e, block, part), BF),
            pltpu.VMEM((n_e, block, part), BF),
            dma((2,)),
            dma((n_z,)),
            dma((n_z,)),
            dma((n_z,)),
            dma((n_z,)),
            dma((n_z,)),
            dma((n_z,)),
            dma,
            dma,
            dma,
            dma,
            dma((half,)),
            dma((n_e // 2,)),
            dma((n_e,)),
            dma((n_e,)),
            dma((n_z,)),
            dma((n_z,)),
        ],
        compiler_params=pltpu.CompilerParams(
            vmem_limit_bytes=56 * MIB, collective_id=0, has_side_effects=True
        ),
    )(
        sums,
        inverse,
        features,
        w_self,
        cotangent,
        src,
        dst,
        coef_t,
        agg,
        basis_mats.reshape(bases, width, width),
    )


def per_device(
    features,
    w_self,
    basis_mats,
    basis_coeffs,
    group_rels,
    rel_local,
    edge_src,
    edge_dst,
    block_counts,
    cotangent,
):
    n_ent, width = features.shape
    ent_count = lax.axis_size("ent")
    rel_count = lax.axis_size("rel")
    slots = rel_local.shape[0]
    cap = slots // ent_count
    bases = basis_coeffs.shape[1]
    part = width // rel_count
    q = lax.axis_index("rel")
    s = lax.axis_index("ent")
    all_slots = slots * rel_count

    shape = (ent_count, cap)
    live = lax.broadcasted_iota(I32, shape, 1) < block_counts.reshape(ent_count, 1)
    src_own = edge_src.reshape(shape) - s * n_ent
    base = lax.broadcasted_iota(I32, shape, 0) * n_ent
    dst_own = jnp.where(live, edge_dst.reshape(shape) - base, n_ent)
    ids = jnp.arange(group_rels.shape[0], dtype=I32)
    rel_own = jnp.sum(
        jnp.where(rel_local[:, None] == ids[None, :], group_rels[None, :], 0), axis=1
    ).reshape(shape)
    meta = jnp.stack([src_own, dst_own, rel_own])
    meta = lax.all_gather(meta, "rel")
    meta = meta.transpose(2, 1, 0, 3)
    src = meta[:, 0].reshape(1, all_slots)
    arrived = swap(meta[:, 1:], "ent")
    dst = arrived[:, 0].reshape(1, all_slots)
    rel = arrived[:, 1].reshape(1, all_slots)

    pick_src = (jnp.arange(n_ent, dtype=I32)[:, None] == src).astype(BF)
    feat_part = lax.dynamic_slice_in_dim(features, q * part, part, 1)
    rows = dot(pick_src, feat_part, ((0,), (0,))).astype(BF)
    rows = swap(rows.reshape(ent_count, rel_count * cap, part), "ent").reshape(all_slots, part)

    partial, agg, inverse, coef_t = forward(dst, rel, rows, basis_coeffs, basis_mats, n_ent)
    return finish(
        partial, inverse, features, w_self, cotangent, src, dst, coef_t, agg, basis_mats
    )


def solution(mesh):
    placed = (
        P("ent", None),
        P(),
        P(),
        P(),
        P("rel"),
        P(("rel", "ent")),
        P(("rel", "ent")),
        P(("rel", "ent")),
        P("rel", "ent", None),
        P("ent", None),
    )
    return jax.shard_map(
        per_device,
        mesh=mesh,
        in_specs=placed,
        out_specs=(P("ent", None), P("ent", None), P(("rel", "ent"), None)),
        check_vma=False,
    )
```

```python
import functools

import jax
import jax.numpy as jnp
from jax import lax
from jax.experimental import pallas as pl
from jax.experimental.pallas import tpu as pltpu
from jax.sharding import PartitionSpec as P

BF = jnp.bfloat16
F32 = jnp.float32
I32 = jnp.int32
MIB = 1 << 20


def dot(a, b, dims=((1,), (0,))):
    return lax.dot_general(a, b, (dims, ((), ())), preferred_element_type=F32)


def swap(x, axis):
    return lax.all_to_all(x, axis, split_axis=0, concat_axis=0, tiled=True)


def one_hot(count, row):
    ids = lax.broadcasted_iota(I32, (count, row.shape[1]), 0)
    return (ids == row).astype(F32).astype(BF)


def split3(x):
    hi = x.astype(BF)
    rest = x - hi.astype(F32)
    mid = rest.astype(BF)
    lo = (rest - mid.astype(F32)).astype(BF)
    return hi, mid, lo


def slot_order(bases):
    half = bases // 2
    return [
        c * half + (x % 2) * 8 + y * 2 + x // 2
        for c in range(2)
        for x in range(4)
        for y in range(half // 4)
    ]


def basis_loads(basis_hbm, basis, sems, q):
    part = basis.shape[1]
    lanes = pl.ds(pl.multiple_of(q * part, part), part)
    loads = []
    for c in range(2):
        for x in range(4):
            at = c * 4 + x
            loads.append(
                pltpu.make_async_copy(
                    basis_hbm.at[c, x % 2, :, x // 2, lanes, :],
                    basis.at[pl.ds(at * 4, 4)],
                    sems.at[at],
                )
            )
    return loads


def forward_kernel(
    group,
    dst_ref,
    rel_ref,
    rows_ref,
    coef_ref,
    basis_hbm,
    part_ref,
    agg_ref,
    inv_ref,
    coef_t_ref,
    basis,
    table,
    pick,
    rows_t,
    acc,
    sem,
):
    q = lax.axis_index("rel")
    bases, part, width = basis.shape
    rels = coef_ref.shape[0]
    n_ent = pick.shape[0]
    loads = basis_loads(basis_hbm, basis, sem, q)
    for load in loads:
        load.start()
    table[...] = jnp.zeros_like(table)
    table[:rels, :bases] = coef_ref[...]
    which = one_hot(table.shape[0], rel_ref[...])
    hi, mid, lo = split3(table[...])
    coef_t = dot(hi, which, ((0,), (0,))) + dot(mid, which, ((0,), (0,)))
    coef_t = coef_t + dot(lo, which, ((0,), (0,)))
    for p, b in enumerate(slot_order(bases)):
        coef_t_ref[p : p + 1, :] = coef_t[b : b + 1, :]
    pick[...] = one_hot(n_ent, dst_ref[...])
    degree = dot(pick[...], jnp.ones((pick.shape[1], part), BF))
    inv_ref[...] = 1.0 / jnp.maximum(degree, 1.0)
    rows_t[...] = rows_ref[...].astype(F32).T
    acc[...] = jnp.zeros_like(acc)
    for load in loads:
        load.wait()

    def step(i, _):
        mixed = jnp.concatenate(
            [
                (rows_t[...] * coef_t_ref[pl.ds(i * group + g, 1), :]).astype(BF)
                for g in range(group)
            ],
            axis=0,
        )
        agg = dot(pick[...], mixed, ((1,), (1,)))
        agg_b = agg.astype(BF)
        weights = basis[pl.ds(i * group, group)].reshape(group * part, width)
        acc[...] += dot(agg_b, weights)
        agg_ref[pl.ds(i * group, group)] = agg.T.astype(BF).reshape(group, part, n_ent)
        return 0

    lax.fori_loop(0, bases // group, step, 0)
    for r in range(width // part):
        part_ref[r] = acc[:, r * part : (r + 1) * part].astype(BF)


def forward(dst, rel, rows, coeffs, basis_mats, n_ent):
    all_slots, part = rows.shape
    rels, bases = coeffs.shape
    width = basis_mats.shape[1]
    vm = pl.BlockSpec(memory_space=pltpu.VMEM)
    return pl.pallas_call(
        functools.partial(forward_kernel, 2),
        out_shape=(
            jax.ShapeDtypeStruct((width // part, n_ent, part), BF),
            jax.ShapeDtypeStruct((bases, part, n_ent), BF),
            jax.ShapeDtypeStruct((n_ent, part), F32),
            jax.ShapeDtypeStruct((bases, all_slots), F32),
        ),
        in_specs=[vm, vm, vm, vm, pl.BlockSpec(memory_space=pl.ANY)],
        out_specs=(vm, vm, vm, vm),
        scratch_shapes=[
            pltpu.VMEM((bases, part, width), BF),
            pltpu.VMEM((1024, 128), F32),
            pltpu.VMEM((n_ent, all_slots), BF),
            pltpu.VMEM((part, all_slots), F32),
            pltpu.VMEM((n_ent, width), F32),
            pltpu.SemaphoreType.DMA((bases // 4,)),
        ],
        compiler_params=pltpu.CompilerParams(vmem_limit_bytes=56 * MIB),
    )(dst, rel, rows, coeffs, basis_mats.reshape(2, 2, 4, 2, width, width))


def remote(src, dst, send_sem, recv_sem, z, e):
    return pltpu.make_async_remote_copy(
        src_ref=src,
        dst_ref=dst,
        send_sem=send_sem,
        recv_sem=recv_sem,
        device_id=(z, e),
        device_id_type=pl.DeviceIdType.MESH,
    )


def finish_kernel(
    n_z,
    n_e,
    sums_ref,
    inv_ref,
    feat_ref,
    w_ref,
    cot_ref,
    src_ref,
    dst_ref,
    coef_t_ref,
    agg_hbm,
    basis_hbm,
    act_ref,
    gf_ref,
    gb_ref,
    sums_in,
    pre_in,
    scaled,
    scaled_sib,
    agg_own,
    agg_sib,
    basis,
    pick,
    pick_src,
    acc,
    back,
    term_x,
    term_y,
    x_in,
    y_in,
    half_x,
    half_y,
    xy_in,
    yx_in,
    done,
    row_out,
    row_in,
    basis_sem,
    load_sem,
    sums_send,
    sums_recv,
    act_send,
    act_recv,
    pre_send,
    pre_recv,
    agg_send,
    agg_recv,
    sib_send,
    sib_recv,
    x_send,
    x_recv,
    y_send,
    y_recv,
    xy_send,
    xy_recv,
    yx_send,
    yx_recv,
    move_send,
    move_recv,
    row_send,
    row_recv,
    gf_send,
    gf_recv,
):
    q = lax.axis_index("rel")
    e = lax.axis_index("ent")
    core = lax.rem(e, 2)
    chip = lax.div(e, 2)
    sib = e + 1 - 2 * core
    bases, part, width = basis.shape
    half = bases // 2
    lanes = pl.ds(pl.multiple_of(q * part, part), part)
    x = lax.rem(chip, 4)
    y = lax.div(chip, 4)

    def at_chip(y_at, x_at):
        return (y_at * 4 + x_at) * 2 + core

    to_z = 2 * core + lax.rem(x, 2)
    to_e = (y * 4 + lax.div(x, 2) * 2 + lax.div(q, 2)) * 2 + lax.rem(q, 2)
    from_z = lax.rem(x, 2) * 2 + core
    from_e = (y * 4 + lax.div(x, 2) * 2 + lax.rem(q, 2)) * 2 + lax.div(q, 2)
    keeps = jnp.logical_and(to_z == q, to_e == e)
    moves = jnp.logical_not(keeps)

    barrier = pltpu.get_barrier_semaphore()

    def greet(z, peer):
        pl.semaphore_signal(
            barrier, inc=1, device_id=(z, peer), device_id_type=pl.DeviceIdType.MESH
        )

    for d in range(1, n_z):
        greet(lax.rem(q + d, n_z), e)

    def greet_plane(d, _):
        greet(q, lax.rem(e + d, n_e))
        return 0

    lax.fori_loop(1, n_e, greet_plane, 0)

    @pl.when(moves)
    def _():
        greet(from_z, from_e)

    loads = basis_loads(basis_hbm, basis, basis_sem, q)
    for load in loads:
        load.start()
    load_agg = pltpu.make_async_copy(
        agg_hbm.at[pl.ds(core * half, half)], agg_own, load_sem
    )
    load_agg.start()
    w_part = w_ref[:, lanes]
    pre = dot(feat_ref[...], w_part)
    pl.semaphore_wait(barrier, n_z - 1 + n_e - 1 + moves.astype(I32))

    def sums_copy(d):
        z = lax.rem(q + d, n_z)
        return remote(
            sums_ref.at[z], sums_in.at[q], sums_send.at[d], sums_recv.at[q], z, e
        )

    def sums_wait(d):
        z = lax.rem(q + d, n_z)
        remote(
            sums_ref.at[z], sums_in.at[z], sums_send.at[d], sums_recv.at[z], z, e
        ).wait_recv()

    for d in range(1, n_z):
        sums_copy(d).start()
    agg_copy = remote(
        agg_hbm.at[pl.ds((1 - core) * half, half)],
        agg_sib,
        agg_send,
        agg_recv,
        q,
        sib,
    )
    agg_copy.start()
    pick[...] = one_hot(pick.shape[0], dst_ref[...])
    pick_src[...] = one_hot(pick.shape[0], src_ref[...])
    total = sums_ref[q].astype(F32)
    for d in range(1, n_z):
        sums_wait(d)
        total += sums_in[lax.rem(q + d, n_z)].astype(F32)
    inverse = inv_ref[...]
    pre = pre + total * inverse
    sig = jax.nn.sigmoid(pre)
    slope = sig * (1.0 + pre * (1.0 - sig))
    pre_in[q] = (cot_ref[:, lanes].astype(F32) * slope).astype(BF)

    def pre_copy(d, z_in):
        z = lax.rem(q + d, n_z)
        return remote(pre_in.at[q], pre_in.at[z_in], pre_send.at[d], pre_recv.at[z_in], z, e)

    def act_copy(d, z_in):
        z = lax.rem(q + d, n_z)
        at = pl.ds(pl.multiple_of(z_in * part, part), part)
        return remote(
            act_ref.at[:, lanes], act_ref.at[:, at], act_send.at[d], act_recv.at[z_in], z, e
        )

    for d in range(1, n_z):
        pre_copy(d, q).start()
    act_ref[:, lanes] = (pre * sig).astype(BF)
    for d in range(1, n_z):
        pre_copy(d, lax.rem(q + d, n_z)).wait_recv()
    for z in range(n_z):
        scaled[:, z * part : (z + 1) * part] = (pre_in[z].astype(F32) * inverse).astype(BF)
    sib_copy = remote(scaled, scaled_sib, sib_send, sib_recv, q, sib)
    sib_copy.start()
    w_rows = w_ref[lanes, :]
    grad = dot(pre_in[0], w_rows[:, :part], ((1,), (1,)))
    for z in range(1, n_z):
        grad += dot(pre_in[z], w_rows[:, z * part : (z + 1) * part], ((1,), (1,)))
    load_agg.wait()
    agg_copy.wait_recv()
    sib_copy.wait_recv()

    group = 4
    n_ent = agg_own.shape[2]
    wide = width // 2

    def x_first(d, slot):
        peer = lax.rem(x + d, 4)
        return remote(
            term_x.at[peer], x_in.at[slot], x_send.at[d], x_recv.at[slot], q, at_chip(y, peer)
        )

    def y_first(d, slot):
        peer = lax.rem(y + d, 4)
        return remote(
            term_y.at[peer], y_in.at[slot], y_send.at[d], y_recv.at[slot], q, at_chip(peer, x)
        )

    def x_then_y(d, slot):
        peer = lax.rem(y + d, 4)
        return remote(
            half_x.at[peer], xy_in.at[slot], xy_send.at[d], xy_recv.at[slot], q, at_chip(peer, x)
        )

    def y_then_x(d, slot):
        peer = lax.rem(x + d, 4)
        return remote(
            half_y.at[peer], yx_in.at[slot], yx_send.at[d], yx_recv.at[slot], q, at_chip(y, peer)
        )

    for d in (2, 1, 3, 0):
        at = lax.rem(x + d, 4)
        own = agg_own[pl.ds(at * group, group)].reshape(group * part, n_ent)
        other = agg_sib[pl.ds(at * group, group)].reshape(group * part, n_ent)
        terms = dot(own, scaled[...]) + dot(other, scaled_sib[...])
        terms = terms.astype(BF)
        term_x[at] = terms[:, :wide].reshape(group, part, wide)
        for g in range(group):
            term_y[g, at] = terms[g * part : (g + 1) * part, wide:]
        if d:
            x_first(d, x).start()
    for d in (2, 1, 3):
        y_first(d, y).start()
    for d in range(1, n_z):
        act_copy(d, q).start()
    for load in loads:
        load.wait()
    seg = acc.shape[1]

    def back_step(i, _):
        weights = basis[pl.ds(i * group, group)].reshape(group * part, width)
        back[i] = dot(weights, scaled[...], ((1,), (1,))).astype(BF)
        return 0

    lax.fori_loop(0, bases // group, back_step, 0)

    def spread(first):
        acc[...] = jnp.zeros_like(acc)

        def step(i, _):
            out = dot(back[i], pick[:, first : first + seg])
            rows = acc[...]
            for g in range(group):
                coef = coef_t_ref[pl.ds(i * group + g, 1), first : first + seg]
                rows += out[g * part : (g + 1) * part] * coef
            acc[...] = rows
            return 0

        lax.fori_loop(0, bases // group, step, 0)
        block = row_out.shape[1]
        rows = acc[...].T.astype(BF).reshape(seg // block, block, part)
        row_out[first // block : (first + seg) // block] = rows

    def row_copy(peer, slot):
        return remote(
            row_out.at[peer], row_in.at[slot], row_send.at[peer], row_recv.at[slot], q, peer
        )

    def row_start(peer, _):
        @pl.when(peer != e)
        def _():
            row_copy(peer, e).start()

        return 0

    def row_wait(d, _):
        peer = lax.rem(e + d, n_e)
        row_copy(peer, peer).wait_recv()
        return 0

    per_seg = n_e * seg // pick.shape[1]
    for n in range(n_e // per_seg):
        spread(n * seg)
        lax.fori_loop(n * per_seg, (n + 1) * per_seg, row_start, 0)
    row_in[e] = row_out[e]

    def add_up(own, arrived, recv, me):
        total = own.astype(F32)
        for d in (1, 3, 2):
            slot = lax.rem(me + d, 4)
            recv(d, slot).wait_recv()
            total += arrived[slot].astype(F32)
        return total

    half_x[...] = add_up(term_x[x], x_in, x_first, x).astype(BF)
    for d in (2, 1, 3):
        x_then_y(d, y).start()
    half_y[...] = add_up(term_y[y], y_in, y_first, y).astype(BF)
    for d in (2, 1, 3):
        y_then_x(d, x).start()
    lax.fori_loop(1, n_e, row_wait, 0)
    grad += dot(pick_src[...], row_in[...].reshape(pick_src.shape[1], part))
    gf_ref[:, lanes] = grad.astype(BF)

    def gf_copy(d, z_in):
        z = lax.rem(q + d, n_z)
        at = pl.ds(pl.multiple_of(z_in * part, part), part)
        return remote(
            gf_ref.at[:, lanes], gf_ref.at[:, at], gf_send.at[d], gf_recv.at[z_in], z, e
        )

    for d in range(1, n_z):
        gf_copy(d, q).start()

    done[:, :wide] = add_up(half_x[y], xy_in, x_then_y, y)
    done[:, wide:] = add_up(half_y[x], yx_in, y_then_x, x)
    move = remote(done, gb_ref, move_send, move_recv, to_z, to_e)

    @pl.when(keeps)
    def _():
        gb_ref[...] = done[...]

    @pl.when(moves)
    def _():
        move.start()
        move.wait_send()
        remote(done, gb_ref, move_send, move_recv, from_z, from_e).wait_recv()

    for d in range(1, n_z):
        z = lax.rem(q + d, n_z)
        act_copy(d, z).wait_recv()
        gf_copy(d, z).wait_recv()
        sums_copy(d).wait_send()
        pre_copy(d, q).wait_send()
        act_copy(d, q).wait_send()
        gf_copy(d, q).wait_send()
    agg_copy.wait_send()
    sib_copy.wait_send()

    for d in (1, 2, 3):
        x_first(d, x).wait_send()
        y_first(d, y).wait_send()
        x_then_y(d, y).wait_send()
        y_then_x(d, x).wait_send()

    def row_sent(d, _):
        row_copy(lax.rem(e + d, n_e), e).wait_send()
        return 0

    lax.fori_loop(1, n_e, row_sent, 0)


def finish(sums, inverse, features, w_self, cotangent, src, dst, coef_t, agg, basis_mats):
    n_z = lax.axis_size("rel")
    n_e = lax.axis_size("ent")
    n_ent, width = features.shape
    bases, all_slots = coef_t.shape
    part = width // n_z
    half = bases // 2
    block = all_slots // n_e
    vm = pl.BlockSpec(memory_space=pltpu.VMEM)
    hbm = pl.BlockSpec(memory_space=pl.ANY)
    dma = pltpu.SemaphoreType.DMA
    return pl.pallas_call(
        functools.partial(finish_kernel, n_z, n_e),
        out_shape=(
            jax.ShapeDtypeStruct((n_ent, width), BF),
            jax.ShapeDtypeStruct((n_ent, width), BF),
            jax.ShapeDtypeStruct((part, width), F32),
        ),
        in_specs=[vm] * 8 + [hbm, hbm],
        out_specs=(vm, vm, vm),
        scratch_shapes=[
            pltpu.VMEM((n_z, n_ent, part), BF),
            pltpu.VMEM((n_z, n_ent, part), BF),
            pltpu.VMEM((n_ent, width), BF),
            pltpu.VMEM((n_ent, width), BF),
            pltpu.VMEM((half, part, n_ent), BF),
            pltpu.VMEM((half, part, n_ent), BF),
            pltpu.VMEM((bases, part, width), BF),
            pltpu.VMEM((n_ent, all_slots), BF),
            pltpu.VMEM((n_ent, all_slots), BF),
            pltpu.VMEM((part, all_slots // 2), F32),
            pltpu.VMEM((bases // 4, 4 * part, n_ent), BF),
            pltpu.VMEM((4, 4, part, width // 2), BF),
            pltpu.VMEM((4, 4, part, width // 2), BF),
            pltpu.VMEM((4, 4, part, width // 2), BF),
            pltpu.VMEM((4, 4, part, width // 2), BF),
            pltpu.VMEM((4, part, width // 2), BF),
            pltpu.VMEM((4, part, width // 2), BF),
            pltpu.VMEM((4, part, width // 2), BF),
            pltpu.VMEM((4, part, width // 2), BF),
            pltpu.VMEM((part, width), F32),
            pltpu.VMEM((n_e, block, part), BF),
            pltpu.VMEM((n_e, block, part), BF),
            dma((bases // 4,)),
            dma,
            dma((n_z,)),
            dma((n_z,)),
            dma((n_z,)),
            dma((n_z,)),
            dma((n_z,)),
            dma((n_z,)),
            dma,
            dma,
            dma,
            dma,
            dma((4,)),
            dma((4,)),
            dma((4,)),
            dma((4,)),
            dma((4,)),
            dma((4,)),
            dma((4,)),
            dma((4,)),
            dma,
            dma,
            dma((n_e,)),
            dma((n_e,)),
            dma((n_z,)),
            dma((n_z,)),
        ],
        compiler_params=pltpu.CompilerParams(
            vmem_limit_bytes=56 * MIB, collective_id=0, has_side_effects=True
        ),
    )(
        sums,
        inverse,
        features,
        w_self,
        cotangent,
        src,
        dst,
        coef_t,
        agg,
        basis_mats.reshape(2, 2, 4, 2, width, width),
    )


def per_device(
    features,
    w_self,
    basis_mats,
    basis_coeffs,
    group_rels,
    rel_local,
    edge_src,
    edge_dst,
    block_counts,
    cotangent,
):
    n_ent, width = features.shape
    ent_count = lax.axis_size("ent")
    rel_count = lax.axis_size("rel")
    slots = rel_local.shape[0]
    cap = slots // ent_count
    bases = basis_coeffs.shape[1]
    part = width // rel_count
    q = lax.axis_index("rel")
    s = lax.axis_index("ent")
    all_slots = slots * rel_count

    shape = (ent_count, cap)
    live = lax.broadcasted_iota(I32, shape, 1) < block_counts.reshape(ent_count, 1)
    src_own = edge_src.reshape(shape) - s * n_ent
    base = lax.broadcasted_iota(I32, shape, 0) * n_ent
    dst_own = jnp.where(live, edge_dst.reshape(shape) - base, n_ent)
    ids = jnp.arange(group_rels.shape[0], dtype=I32)
    rel_own = jnp.sum(
        jnp.where(rel_local[:, None] == ids[None, :], group_rels[None, :], 0), axis=1
    ).reshape(shape)
    meta = jnp.stack([src_own, dst_own, rel_own])
    meta = lax.all_gather(meta, "rel")
    meta = meta.transpose(2, 1, 0, 3)
    src = meta[:, 0].reshape(1, all_slots)
    arrived = swap(meta[:, 1:], "ent")
    dst = arrived[:, 0].reshape(1, all_slots)
    rel = arrived[:, 1].reshape(1, all_slots)

    pick_src = (jnp.arange(n_ent, dtype=I32)[:, None] == src).astype(BF)
    feat_part = lax.dynamic_slice_in_dim(features, q * part, part, 1)
    rows = dot(pick_src, feat_part, ((0,), (0,))).astype(BF)
    rows = swap(rows.reshape(ent_count, rel_count * cap, part), "ent").reshape(all_slots, part)

    partial, agg, inverse, coef_t = forward(dst, rel, rows, basis_coeffs, basis_mats, n_ent)
    return finish(
        partial, inverse, features, w_self, cotangent, src, dst, coef_t, agg, basis_mats
    )


def solution(mesh):
    placed = (
        P("ent", None),
        P(),
        P(),
        P(),
        P("rel"),
        P(("rel", "ent")),
        P(("rel", "ent")),
        P(("rel", "ent")),
        P("rel", "ent", None),
        P("ent", None),
    )
    return jax.shard_map(
        per_device,
        mesh=mesh,
        in_specs=placed,
        out_specs=(P("ent", None), P("ent", None), P(("rel", "ent"), None)),
        check_vma=False,
    )
```

```python
import functools

import jax
import jax.numpy as jnp
from jax import lax
from jax.experimental import pallas as pl
from jax.experimental.pallas import tpu as pltpu
from jax.sharding import PartitionSpec as P

BF = jnp.bfloat16
F32 = jnp.float32
I32 = jnp.int32
MIB = 1 << 20


def dot(a, b, dims=((1,), (0,))):
    return lax.dot_general(a, b, (dims, ((), ())), preferred_element_type=F32)


def one_hot(count, row):
    ids = lax.broadcasted_iota(I32, (count, row.shape[1]), 0)
    return (ids == row).astype(F32).astype(BF)


def split3(x):
    hi = x.astype(BF)
    rest = x - hi.astype(F32)
    mid = rest.astype(BF)
    lo = (rest - mid.astype(F32)).astype(BF)
    return hi, mid, lo


def slot_order(bases):
    half = bases // 2
    return [
        c * half + (x % 2) * 8 + y * 2 + x // 2
        for c in range(2)
        for x in range(4)
        for y in range(half // 4)
    ]


def basis_loads(basis_hbm, basis, sems, q):
    part = basis.shape[1]
    lanes = pl.ds(pl.multiple_of(q * part, part), part)
    loads = []
    for c in range(2):
        for x in range(4):
            at = c * 4 + x
            loads.append(
                pltpu.make_async_copy(
                    basis_hbm.at[c, x % 2, :, x // 2, lanes, :],
                    basis.at[pl.ds(at * 4, 4)],
                    sems.at[at],
                )
            )
    return loads


def remote(src, dst, send_sem, recv_sem, z, e):
    return pltpu.make_async_remote_copy(
        src_ref=src,
        dst_ref=dst,
        send_sem=send_sem,
        recv_sem=recv_sem,
        device_id=(z, e),
        device_id_type=pl.DeviceIdType.MESH,
    )


def step_kernel(
    n_z,
    n_e,
    meta_ref,
    feat_ref,
    w_ref,
    cot_ref,
    coef_ref,
    basis_hbm,
    act_ref,
    gf_ref,
    gb_ref,
    meta_z,
    meta_all,
    tags,
    line,
    line_rel,
    table,
    feed_out,
    feed_in,
    rows_t,
    coef_t_ref,
    inv_ref,
    pre_self,
    sums_acc,
    sums_ref,
    agg,
    sums_in,
    pre_in,
    scaled,
    scaled_sib,
    agg_sib,
    basis,
    pick,
    pick_src,
    acc,
    back,
    term_x,
    term_y,
    x_in,
    y_in,
    half_x,
    half_y,
    xy_in,
    yx_in,
    done,
    row_out,
    row_in,
    basis_sem,
    sums_send,
    sums_recv,
    act_send,
    act_recv,
    pre_send,
    pre_recv,
    agg_send,
    agg_recv,
    sib_send,
    sib_recv,
    x_send,
    x_recv,
    y_send,
    y_recv,
    xy_send,
    xy_recv,
    yx_send,
    yx_recv,
    move_send,
    move_recv,
    row_send,
    row_recv,
    gf_send,
    gf_recv,
    meta_send,
    meta_recv,
    tag_send,
    tag_recv,
    feed_send,
    feed_recv,
):
    q = lax.axis_index("rel")
    e = lax.axis_index("ent")
    core = lax.rem(e, 2)
    chip = lax.div(e, 2)
    sib = e + 1 - 2 * core
    bases, part, width = basis.shape
    half = bases // 2
    lanes = pl.ds(pl.multiple_of(q * part, part), part)
    x = lax.rem(chip, 4)
    y = lax.div(chip, 4)

    def at_chip(y_at, x_at):
        return (y_at * 4 + x_at) * 2 + core

    to_z = 2 * core + lax.rem(x, 2)
    to_e = (y * 4 + lax.div(x, 2) * 2 + lax.div(q, 2)) * 2 + lax.rem(q, 2)
    from_z = lax.rem(x, 2) * 2 + core
    from_e = (y * 4 + lax.div(x, 2) * 2 + lax.rem(q, 2)) * 2 + lax.div(q, 2)
    keeps = jnp.logical_and(to_z == q, to_e == e)
    moves = jnp.logical_not(keeps)

    barrier = pltpu.get_barrier_semaphore()

    def greet(z, peer):
        pl.semaphore_signal(
            barrier, inc=1, device_id=(z, peer), device_id_type=pl.DeviceIdType.MESH
        )

    for d in range(1, n_z):
        greet(lax.rem(q + d, n_z), e)

    def greet_plane(d, _):
        greet(q, lax.rem(e + d, n_e))
        return 0

    lax.fori_loop(1, n_e, greet_plane, 0)

    @pl.when(moves)
    def _():
        greet(from_z, from_e)

    loads = basis_loads(basis_hbm, basis, basis_sem, q)
    for load in loads:
        load.start()
    table[...] = jnp.zeros_like(table)
    table[: coef_ref.shape[0], :bases] = coef_ref[...]
    pre_self[...] = dot(feat_ref[...], w_ref[:, lanes])
    pl.semaphore_wait(barrier, n_z - 1 + n_e - 1 + moves.astype(I32))

    def meta_copy(d, slot):
        z = lax.rem(q + d, n_z)
        return remote(meta_ref, meta_z.at[slot], meta_send.at[d], meta_recv.at[slot], z, e)

    def tag_copy(peer, slot):
        return remote(
            meta_all.at[lax.div(peer, 2)],
            tags.at[slot],
            tag_send.at[peer],
            tag_recv.at[slot],
            q,
            peer,
        )

    def feed_copy(peer, slot):
        return remote(
            feed_out.at[peer], feed_in.at[slot], feed_send.at[peer], feed_recv.at[slot], q, peer
        )

    def start_all(copy):
        def go(d, _):
            copy(lax.rem(e + d, n_e), e).start()
            return 0

        lax.fori_loop(1, n_e, go, 0)

    def wait_all(copy):
        def go(d, _):
            peer = lax.rem(e + d, n_e)
            copy(peer, peer).wait_recv()
            return 0

        lax.fori_loop(1, n_e, go, 0)

    def sent_all(copy):
        def go(d, _):
            copy(lax.rem(e + d, n_e), e).wait_send()
            return 0

        lax.fori_loop(1, n_e, go, 0)

    for d in range(1, n_z):
        meta_copy(d, q).start()
    feat_t = feat_ref[:, lanes].T
    meta = meta_ref[...]
    for d in range(1, n_z):
        slot = lax.rem(q + d, n_z)
        meta_copy(d, slot).wait_recv()
        meta += meta_z[slot]
    meta_all[...] = meta
    start_all(tag_copy)
    tags[e] = meta_all[lax.div(e, 2)]
    n_ent = pick.shape[0]
    pairs = n_e // 2
    wide_lanes = meta_ref.shape[3]
    for t in range(pairs):
        line[:, t * wide_lanes : (t + 1) * wide_lanes] = meta_all[t, 0]
    pick_src[...] = one_hot(n_ent, line[...])
    feed = dot(feat_t, pick_src[...])
    feed_out[...] = feed.T.astype(BF).reshape(feed_out.shape)
    start_all(feed_copy)
    feed_in[e] = feed_out[e]
    wait_all(tag_copy)
    left = lax.broadcasted_iota(I32, (1, wide_lanes), 1) < wide_lanes // 2
    for f, out in ((1, line), (2, line_rel)):
        for t in range(pairs):
            even = tags[2 * t, f]
            odd = tags[2 * t + 1, f]
            even = jnp.where(core == 0, even, pltpu.roll(even, wide_lanes // 2, 1))
            odd = jnp.where(core == 0, pltpu.roll(odd, wide_lanes // 2, 1), odd)
            out[:, t * wide_lanes : (t + 1) * wide_lanes] = jnp.where(left, even, odd)
    which = one_hot(table.shape[0], line_rel[...])
    hi, mid, lo = split3(table[...])
    coef_t = dot(hi, which, ((0,), (0,))) + dot(mid, which, ((0,), (0,)))
    coef_t = coef_t + dot(lo, which, ((0,), (0,)))
    for p, b in enumerate(slot_order(bases)):
        coef_t_ref[p : p + 1, :] = coef_t[b : b + 1, :]
    pick[...] = one_hot(n_ent, line[...])
    degree = dot(pick[...], jnp.ones((pick.shape[1], part), BF))
    inv_ref[...] = 1.0 / jnp.maximum(degree, 1.0)
    sums_acc[...] = jnp.zeros_like(sums_acc)
    wait_all(feed_copy)
    rows_t[...] = feed_in[...].reshape(pick.shape[1], part).astype(F32).T
    for load in loads:
        load.wait()
    pair = 2

    def forward_step(i, _):
        at = i * pair
        mixed = jnp.concatenate(
            [
                (rows_t[...] * coef_t_ref[pl.ds(at + g, 1), :]).astype(BF)
                for g in range(pair)
            ],
            axis=0,
        )
        out = dot(pick[...], mixed, ((1,), (1,)))
        weights = basis[pl.ds(at, pair)].reshape(pair * part, width)
        sums_acc[...] += dot(out.astype(BF), weights)
        agg[pl.ds(at, pair)] = out.T.astype(BF).reshape(pair, part, n_ent)
        return 0

    agg_copy = remote(
        agg.at[pl.ds((1 - core) * half, half)], agg_sib, agg_send, agg_recv, q, sib
    )
    steps = half // pair
    lax.fori_loop((1 - core) * steps, (2 - core) * steps, forward_step, 0)
    agg_copy.start()
    lax.fori_loop(core * steps, (1 + core) * steps, forward_step, 0)
    for r in range(n_z):
        sums_ref[r] = sums_acc[:, r * part : (r + 1) * part].astype(BF)

    def sums_copy(d):
        z = lax.rem(q + d, n_z)
        return remote(
            sums_ref.at[z], sums_in.at[q], sums_send.at[d], sums_recv.at[q], z, e
        )

    def sums_wait(d):
        z = lax.rem(q + d, n_z)
        remote(
            sums_ref.at[z], sums_in.at[z], sums_send.at[d], sums_recv.at[z], z, e
        ).wait_recv()

    for d in range(1, n_z):
        sums_copy(d).start()
    total = sums_ref[q].astype(F32)
    for d in range(1, n_z):
        sums_wait(d)
        total += sums_in[lax.rem(q + d, n_z)].astype(F32)
    inverse = inv_ref[...]
    pre = pre_self[...] + total * inverse
    sig = jax.nn.sigmoid(pre)
    slope = sig * (1.0 + pre * (1.0 - sig))
    pre_in[q] = (cot_ref[:, lanes].astype(F32) * slope).astype(BF)

    def pre_copy(d, z_in):
        z = lax.rem(q + d, n_z)
        return remote(pre_in.at[q], pre_in.at[z_in], pre_send.at[d], pre_recv.at[z_in], z, e)

    def act_copy(d, z_in):
        z = lax.rem(q + d, n_z)
        at = pl.ds(pl.multiple_of(z_in * part, part), part)
        return remote(
            act_ref.at[:, lanes], act_ref.at[:, at], act_send.at[d], act_recv.at[z_in], z, e
        )

    for d in range(1, n_z):
        pre_copy(d, q).start()
    act_ref[:, lanes] = (pre * sig).astype(BF)
    for d in range(1, n_z):
        pre_copy(d, lax.rem(q + d, n_z)).wait_recv()
    for z in range(n_z):
        scaled[:, z * part : (z + 1) * part] = (pre_in[z].astype(F32) * inverse).astype(BF)
    sib_copy = remote(scaled, scaled_sib, sib_send, sib_recv, q, sib)
    sib_copy.start()
    w_rows = w_ref[lanes, :]
    grad = dot(pre_in[0], w_rows[:, :part], ((1,), (1,)))
    for z in range(1, n_z):
        grad += dot(pre_in[z], w_rows[:, z * part : (z + 1) * part], ((1,), (1,)))
    agg_copy.wait_recv()
    sib_copy.wait_recv()

    group = 4
    wide = width // 2

    def x_first(d, slot):
        peer = lax.rem(x + d, 4)
        return remote(
            term_x.at[peer], x_in.at[slot], x_send.at[d], x_recv.at[slot], q, at_chip(y, peer)
        )

    def y_first(d, slot):
        peer = lax.rem(y + d, 4)
        return remote(
            term_y.at[peer], y_in.at[slot], y_send.at[d], y_recv.at[slot], q, at_chip(peer, x)
        )

    def x_then_y(d, slot):
        peer = lax.rem(y + d, 4)
        return remote(
            half_x.at[peer], xy_in.at[slot], xy_send.at[d], xy_recv.at[slot], q, at_chip(peer, x)
        )

    def y_then_x(d, slot):
        peer = lax.rem(x + d, 4)
        return remote(
            half_y.at[peer], yx_in.at[slot], yx_send.at[d], yx_recv.at[slot], q, at_chip(y, peer)
        )

    for d in (2, 1, 3, 0):
        at = lax.rem(x + d, 4)
        own = agg[pl.ds(core * half + at * group, group)].reshape(group * part, n_ent)
        other = agg_sib[pl.ds(at * group, group)].reshape(group * part, n_ent)
        terms = dot(own, scaled[...]) + dot(other, scaled_sib[...])
        terms = terms.astype(BF)
        term_x[at] = terms[:, :wide].reshape(group, part, wide)
        for g in range(group):
            term_y[g, at] = terms[g * part : (g + 1) * part, wide:]
        if d:
            x_first(d, x).start()
    for d in (2, 1, 3):
        y_first(d, y).start()
    for d in range(1, n_z):
        act_copy(d, q).start()
    seg = acc.shape[1]

    def back_step(i, _):
        weights = basis[pl.ds(i * group, group)].reshape(group * part, width)
        back[i] = dot(weights, scaled[...], ((1,), (1,))).astype(BF)
        return 0

    lax.fori_loop(0, bases // group, back_step, 0)

    def spread(first):
        acc[...] = jnp.zeros_like(acc)

        def step(i, _):
            out = dot(back[i], pick[:, first : first + seg])
            rows = acc[...]
            for g in range(group):
                coef = coef_t_ref[pl.ds(i * group + g, 1), first : first + seg]
                rows += out[g * part : (g + 1) * part] * coef
            acc[...] = rows
            return 0

        lax.fori_loop(0, bases // group, step, 0)
        block = row_out.shape[1]
        rows = acc[...].T.astype(BF).reshape(seg // block, block, part)
        row_out[first // block : (first + seg) // block] = rows

    def row_copy(peer, slot):
        return remote(
            row_out.at[peer], row_in.at[slot], row_send.at[peer], row_recv.at[slot], q, peer
        )

    def row_start(peer, _):
        @pl.when(peer != e)
        def _():
            row_copy(peer, e).start()

        return 0

    per_seg = n_e * seg // pick.shape[1]
    for n in range(n_e // per_seg):
        spread(n * seg)
        lax.fori_loop(n * per_seg, (n + 1) * per_seg, row_start, 0)
    row_in[e] = row_out[e]

    def add_up(own, arrived, recv, me):
        total = own.astype(F32)
        for d in (1, 3, 2):
            slot = lax.rem(me + d, 4)
            recv(d, slot).wait_recv()
            total += arrived[slot].astype(F32)
        return total

    half_x[...] = add_up(term_x[x], x_in, x_first, x).astype(BF)
    for d in (2, 1, 3):
        x_then_y(d, y).start()
    half_y[...] = add_up(term_y[y], y_in, y_first, y).astype(BF)
    for d in (2, 1, 3):
        y_then_x(d, x).start()
    wait_all(row_copy)
    grad += dot(pick_src[...], row_in[...].reshape(pick_src.shape[1], part))
    gf_ref[:, lanes] = grad.astype(BF)

    def gf_copy(d, z_in):
        z = lax.rem(q + d, n_z)
        at = pl.ds(pl.multiple_of(z_in * part, part), part)
        return remote(
            gf_ref.at[:, lanes], gf_ref.at[:, at], gf_send.at[d], gf_recv.at[z_in], z, e
        )

    for d in range(1, n_z):
        gf_copy(d, q).start()

    done[:, :wide] = add_up(half_x[y], xy_in, x_then_y, y)
    done[:, wide:] = add_up(half_y[x], yx_in, y_then_x, x)
    move = remote(done, gb_ref, move_send, move_recv, to_z, to_e)

    @pl.when(keeps)
    def _():
        gb_ref[...] = done[...]

    @pl.when(moves)
    def _():
        move.start()
        move.wait_send()
        remote(done, gb_ref, move_send, move_recv, from_z, from_e).wait_recv()

    for d in range(1, n_z):
        z = lax.rem(q + d, n_z)
        act_copy(d, z).wait_recv()
        gf_copy(d, z).wait_recv()
        sums_copy(d).wait_send()
        pre_copy(d, q).wait_send()
        act_copy(d, q).wait_send()
        gf_copy(d, q).wait_send()
    agg_copy.wait_send()
    sib_copy.wait_send()

    for d in (1, 2, 3):
        x_first(d, x).wait_send()
        y_first(d, y).wait_send()
        x_then_y(d, y).wait_send()
        y_then_x(d, x).wait_send()

    for d in range(1, n_z):
        meta_copy(d, q).wait_send()
    sent_all(tag_copy)
    sent_all(feed_copy)
    sent_all(row_copy)


def run_step(meta, features, w_self, cotangent, coeffs, basis_mats):
    n_z = lax.axis_size("rel")
    n_e = lax.axis_size("ent")
    n_ent, width = features.shape
    bases = coeffs.shape[1]
    all_slots = meta.shape[0] * meta.shape[3]
    part = width // n_z
    half = bases // 2
    block = all_slots // n_e
    vm = pl.BlockSpec(memory_space=pltpu.VMEM)
    dma = pltpu.SemaphoreType.DMA
    return pl.pallas_call(
        functools.partial(step_kernel, n_z, n_e),
        out_shape=(
            jax.ShapeDtypeStruct((n_ent, width), BF),
            jax.ShapeDtypeStruct((n_ent, width), BF),
            jax.ShapeDtypeStruct((part, width), F32),
        ),
        in_specs=[vm] * 5 + [pl.BlockSpec(memory_space=pl.ANY)],
        out_specs=(vm, vm, vm),
        scratch_shapes=[
            pltpu.VMEM((n_z,) + meta.shape, I32),
            pltpu.VMEM(meta.shape, I32),
            pltpu.VMEM((n_e,) + meta.shape[1:], I32),
            pltpu.VMEM((1, all_slots), I32),
            pltpu.VMEM((1, all_slots), I32),
            pltpu.VMEM((1024, 128), F32),
            pltpu.VMEM((n_e, block, part), BF),
            pltpu.VMEM((n_e, block, part), BF),
            pltpu.VMEM((part, all_slots), F32),
            pltpu.VMEM((bases, all_slots), F32),
            pltpu.VMEM((n_ent, part), F32),
            pltpu.VMEM((n_ent, part), F32),
            pltpu.VMEM((n_ent, width), F32),
            pltpu.VMEM((n_z, n_ent, part), BF),
            pltpu.VMEM((bases, part, n_ent), BF),
            pltpu.VMEM((n_z, n_ent, part), BF),
            pltpu.VMEM((n_z, n_ent, part), BF),
            pltpu.VMEM((n_ent, width), BF),
            pltpu.VMEM((n_ent, width), BF),
            pltpu.VMEM((half, part, n_ent), BF),
            pltpu.VMEM((bases, part, width), BF),
            pltpu.VMEM((n_ent, all_slots), BF),
            pltpu.VMEM((n_ent, all_slots), BF),
            pltpu.VMEM((part, all_slots // 2), F32),
            pltpu.VMEM((bases // 4, 4 * part, n_ent), BF),
            pltpu.VMEM((4, 4, part, width // 2), BF),
            pltpu.VMEM((4, 4, part, width // 2), BF),
            pltpu.VMEM((4, 4, part, width // 2), BF),
            pltpu.VMEM((4, 4, part, width // 2), BF),
            pltpu.VMEM((4, part, width // 2), BF),
            pltpu.VMEM((4, part, width // 2), BF),
            pltpu.VMEM((4, part, width // 2), BF),
            pltpu.VMEM((4, part, width // 2), BF),
            pltpu.VMEM((part, width), F32),
            pltpu.VMEM((n_e, block, part), BF),
            pltpu.VMEM((n_e, block, part), BF),
            dma((bases // 4,)),
            dma((n_z,)),
            dma((n_z,)),
            dma((n_z,)),
            dma((n_z,)),
            dma((n_z,)),
            dma((n_z,)),
            dma,
            dma,
            dma,
            dma,
            dma((4,)),
            dma((4,)),
            dma((4,)),
            dma((4,)),
            dma((4,)),
            dma((4,)),
            dma((4,)),
            dma((4,)),
            dma,
            dma,
            dma((n_e,)),
            dma((n_e,)),
            dma((n_z,)),
            dma((n_z,)),
            dma((n_z,)),
            dma((n_z,)),
            dma((n_e,)),
            dma((n_e,)),
            dma((n_e,)),
            dma((n_e,)),
        ],
        compiler_params=pltpu.CompilerParams(
            vmem_limit_bytes=56 * MIB, collective_id=0, has_side_effects=True
        ),
    )(
        meta,
        features,
        w_self,
        cotangent,
        coeffs,
        basis_mats.reshape(2, 2, 4, 2, width, width),
    )


def per_device(
    features,
    w_self,
    basis_mats,
    basis_coeffs,
    group_rels,
    rel_local,
    edge_src,
    edge_dst,
    block_counts,
    cotangent,
):
    n_ent, width = features.shape
    ent_count = lax.axis_size("ent")
    rel_count = lax.axis_size("rel")
    slots = rel_local.shape[0]
    cap = slots // ent_count
    q = lax.axis_index("rel")
    s = lax.axis_index("ent")

    shape = (ent_count, cap)
    live = lax.broadcasted_iota(I32, shape, 1) < block_counts.reshape(ent_count, 1)
    src_own = edge_src.reshape(shape) - s * n_ent
    base = lax.broadcasted_iota(I32, shape, 0) * n_ent
    dst_own = jnp.where(live, edge_dst.reshape(shape) - base, n_ent)
    ids = jnp.arange(group_rels.shape[0], dtype=I32)
    rel_own = jnp.sum(
        jnp.where(rel_local[:, None] == ids[None, :], group_rels[None, :], 0), axis=1
    ).reshape(shape)
    meta = jnp.stack([src_own, dst_own, rel_own]).reshape(3, ent_count // 2, 2, 1, cap)
    mine = jnp.arange(rel_count, dtype=I32)[:, None] == q
    meta = jnp.where(mine, meta, 0).transpose(1, 0, 2, 3, 4)
    meta = meta.reshape(ent_count // 2, 3, 1, 2 * rel_count * cap)
    return run_step(meta, features, w_self, cotangent, basis_coeffs, basis_mats)


def solution(mesh):
    placed = (
        P("ent", None),
        P(),
        P(),
        P(),
        P("rel"),
        P(("rel", "ent")),
        P(("rel", "ent")),
        P(("rel", "ent")),
        P("rel", "ent", None),
        P("ent", None),
    )
    return jax.shard_map(
        per_device,
        mesh=mesh,
        in_specs=placed,
        out_specs=(P("ent", None), P("ent", None), P(("rel", "ent"), None)),
        check_vma=False,
    )
```

```python
import functools

import jax
import jax.numpy as jnp
from jax import lax
from jax.experimental import pallas as pl
from jax.experimental.pallas import tpu as pltpu
from jax.sharding import PartitionSpec as P

BF = jnp.bfloat16
F32 = jnp.float32
I32 = jnp.int32
MIB = 1 << 20


def dot(a, b, dims=((1,), (0,))):
    return lax.dot_general(a, b, (dims, ((), ())), preferred_element_type=F32)


def one_hot(count, row):
    ids = lax.broadcasted_iota(I32, (count, row.shape[1]), 0)
    return (ids == row).astype(F32).astype(BF)


def split3(x):
    hi = x.astype(BF)
    rest = x - hi.astype(F32)
    mid = rest.astype(BF)
    lo = (rest - mid.astype(F32)).astype(BF)
    return hi, mid, lo


def slot_order(bases):
    half = bases // 2
    return [
        c * half + (x % 2) * 8 + y * 2 + x // 2
        for c in range(2)
        for x in range(4)
        for y in range(half // 4)
    ]


def basis_loads(basis_hbm, basis, sems, q):
    part = basis.shape[1]
    lanes = pl.ds(pl.multiple_of(q * part, part), part)
    loads = []
    for c in range(2):
        for x in range(4):
            at = c * 4 + x
            loads.append(
                pltpu.make_async_copy(
                    basis_hbm.at[c, x % 2, :, x // 2, lanes, :],
                    basis.at[pl.ds(at * 4, 4)],
                    sems.at[at],
                )
            )
    return loads


def remote(src, dst, send_sem, recv_sem, z, e):
    return pltpu.make_async_remote_copy(
        src_ref=src,
        dst_ref=dst,
        send_sem=send_sem,
        recv_sem=recv_sem,
        device_id=(z, e),
        device_id_type=pl.DeviceIdType.MESH,
    )


def place_metadata(q, e, src_ref, dst_ref, rel_ref, group_row, counts_ref, meta_ref, n_ent):
    slots = src_ref.shape[1]
    n_e = counts_ref.shape[1]
    pairs, fields, _, lanes = meta_ref.shape
    cap = slots // n_e
    spot = lax.broadcasted_iota(I32, (1, slots), 1)
    peer = lax.div(spot, cap)
    rows16 = lax.broadcasted_iota(I32, (pairs, slots), 0)

    def digits(v):
        return lax.div(v, 32).astype(F32), lax.rem(v, 32).astype(F32)

    hi, lo = digits(group_row[...])
    level = lax.broadcasted_iota(I32, (pairs, group_row.shape[1]), 0)
    table = jnp.where(level == 0, hi, jnp.where(level == 1, lo, 0.0)).astype(BF)
    rel_digits = dot(table, one_hot(group_row.shape[1], rel_ref[...]))
    counts = jnp.broadcast_to(counts_ref[...].astype(F32), (pairs, n_e)).astype(BF)
    limit = dot(counts, one_hot(n_e, peer))[:1]
    live = lax.rem(spot, cap).astype(F32) < limit
    dst = jnp.where(live, dst_ref[...] - peer * n_ent, n_ent)
    values = digits(src_ref[...] - e * n_ent) + digits(dst)
    values = values + (rel_digits[:1], rel_digits[1:2])
    here = rows16 == lax.div(peer, 2)
    stacked = jnp.concatenate([jnp.where(here, v, 0.0) for v in values], axis=0).astype(BF)
    index = lax.broadcasted_iota(I32, (slots, lanes), 0)
    lane = lax.broadcasted_iota(I32, (slots, lanes), 1)
    half = lax.rem(lax.div(index, cap), 2)
    target = half * (lanes // 2) + q * cap + lax.rem(index, cap)
    moved = dot(stacked, (target == lane).astype(F32).astype(BF))
    for f in range(fields):
        hi = moved[2 * f * pairs : (2 * f + 1) * pairs]
        lo = moved[(2 * f + 1) * pairs : (2 * f + 2) * pairs]
        field = (hi * 32.0 + lo + 0.5).astype(I32)
        for t in range(pairs):
            meta_ref[t, f] = field[t : t + 1, :]


def step_kernel(
    n_z,
    n_e,
    src_ref,
    dst_ref,
    rel_ref,
    groups_ref,
    counts_ref,
    feat_ref,
    w_ref,
    cot_ref,
    coef_ref,
    basis_hbm,
    act_ref,
    gf_ref,
    gb_ref,
    group_row,
    meta_ref,
    meta_z,
    meta_all,
    tags,
    line,
    line_rel,
    table,
    feed_out,
    feed_in,
    rows_t,
    coef_t_ref,
    inv_ref,
    pre_self,
    sums_acc,
    sums_ref,
    agg,
    sums_in,
    pre_in,
    scaled,
    scaled_sib,
    agg_sib,
    basis,
    pick,
    pick_src,
    acc,
    back,
    term_x,
    term_y,
    x_in,
    y_in,
    half_x,
    half_y,
    xy_in,
    yx_in,
    done,
    row_out,
    row_in,
    basis_sem,
    sums_send,
    sums_recv,
    act_send,
    act_recv,
    pre_send,
    pre_recv,
    agg_send,
    agg_recv,
    sib_send,
    sib_recv,
    x_send,
    x_recv,
    y_send,
    y_recv,
    xy_send,
    xy_recv,
    yx_send,
    yx_recv,
    move_send,
    move_recv,
    row_send,
    row_recv,
    gf_send,
    gf_recv,
    meta_send,
    meta_recv,
    tag_send,
    tag_recv,
    feed_send,
    feed_recv,
):
    q = lax.axis_index("rel")
    e = lax.axis_index("ent")
    core = lax.rem(e, 2)
    chip = lax.div(e, 2)
    sib = e + 1 - 2 * core
    bases, part, width = basis.shape
    half = bases // 2
    lanes = pl.ds(pl.multiple_of(q * part, part), part)
    x = lax.rem(chip, 4)
    y = lax.div(chip, 4)

    def at_chip(y_at, x_at):
        return (y_at * 4 + x_at) * 2 + core

    to_z = 2 * core + lax.rem(x, 2)
    to_e = (y * 4 + lax.div(x, 2) * 2 + lax.div(q, 2)) * 2 + lax.rem(q, 2)
    from_z = lax.rem(x, 2) * 2 + core
    from_e = (y * 4 + lax.div(x, 2) * 2 + lax.rem(q, 2)) * 2 + lax.div(q, 2)
    keeps = jnp.logical_and(to_z == q, to_e == e)
    moves = jnp.logical_not(keeps)

    barrier = pltpu.get_barrier_semaphore()

    def greet(z, peer):
        pl.semaphore_signal(
            barrier, inc=1, device_id=(z, peer), device_id_type=pl.DeviceIdType.MESH
        )

    for d in range(1, n_z):
        greet(lax.rem(q + d, n_z), e)

    def greet_plane(d, _):
        greet(q, lax.rem(e + d, n_e))
        return 0

    lax.fori_loop(1, n_e, greet_plane, 0)

    @pl.when(moves)
    def _():
        greet(from_z, from_e)

    loads = basis_loads(basis_hbm, basis, basis_sem, q)
    for load in loads:
        load.start()
    table[...] = jnp.zeros_like(table)
    table[:, : coef_ref.shape[1]] = coef_ref[...]
    group_row[...] = jnp.zeros_like(group_row)
    group_row[:, : groups_ref.shape[1]] = groups_ref[...]
    place_metadata(
        q, e, src_ref, dst_ref, rel_ref, group_row, counts_ref, meta_ref, feat_ref.shape[0]
    )
    pre_self[...] = dot(feat_ref[...], w_ref[:, lanes])
    pl.semaphore_wait(barrier, n_z - 1 + n_e - 1 + moves.astype(I32))

    def meta_copy(d, slot):
        z = lax.rem(q + d, n_z)
        return remote(meta_ref, meta_z.at[slot], meta_send.at[d], meta_recv.at[slot], z, e)

    def tag_copy(peer, slot):
        return remote(
            meta_all.at[lax.div(peer, 2)],
            tags.at[slot],
            tag_send.at[peer],
            tag_recv.at[slot],
            q,
            peer,
        )

    def feed_copy(peer, slot):
        return remote(
            feed_out.at[peer], feed_in.at[slot], feed_send.at[peer], feed_recv.at[slot], q, peer
        )

    def start_all(copy):
        def go(d, _):
            copy(lax.rem(e + d, n_e), e).start()
            return 0

        lax.fori_loop(1, n_e, go, 0)

    def wait_all(copy):
        def go(d, _):
            peer = lax.rem(e + d, n_e)
            copy(peer, peer).wait_recv()
            return 0

        lax.fori_loop(1, n_e, go, 0)

    def sent_all(copy):
        def go(d, _):
            copy(lax.rem(e + d, n_e), e).wait_send()
            return 0

        lax.fori_loop(1, n_e, go, 0)

    for d in range(1, n_z):
        meta_copy(d, q).start()
    feat_t = feat_ref[:, lanes].T
    meta = meta_ref[...]
    for d in range(1, n_z):
        slot = lax.rem(q + d, n_z)
        meta_copy(d, slot).wait_recv()
        meta += meta_z[slot]
    meta_all[...] = meta
    start_all(tag_copy)
    tags[e] = meta_all[lax.div(e, 2)]
    n_ent = pick.shape[0]
    pairs = n_e // 2
    wide_lanes = meta_ref.shape[3]
    for t in range(pairs):
        line[:, t * wide_lanes : (t + 1) * wide_lanes] = meta_all[t, 0]
    pick_src[...] = one_hot(n_ent, line[...])
    feed = dot(feat_t, pick_src[...])
    feed_out[...] = feed.T.astype(BF).reshape(feed_out.shape)
    start_all(feed_copy)
    feed_in[e] = feed_out[e]
    wait_all(tag_copy)
    left = lax.broadcasted_iota(I32, (1, wide_lanes), 1) < wide_lanes // 2
    for f, out in ((1, line), (2, line_rel)):
        for t in range(pairs):
            even = tags[2 * t, f]
            odd = tags[2 * t + 1, f]
            even = jnp.where(core == 0, even, pltpu.roll(even, wide_lanes // 2, 1))
            odd = jnp.where(core == 0, pltpu.roll(odd, wide_lanes // 2, 1), odd)
            out[:, t * wide_lanes : (t + 1) * wide_lanes] = jnp.where(left, even, odd)
    which = one_hot(table.shape[1], line_rel[...])
    hi, mid, lo = split3(table[...])
    coef_t = dot(jnp.concatenate([hi, mid, lo], axis=0), which)
    coef_t = coef_t[:bases] + coef_t[bases : 2 * bases] + coef_t[2 * bases : 3 * bases]
    for p, b in enumerate(slot_order(bases)):
        coef_t_ref[p : p + 1, :] = coef_t[b : b + 1, :]
    pick[...] = one_hot(n_ent, line[...])
    degree = dot(pick[...], jnp.ones((pick.shape[1], part), BF))
    inv_ref[...] = 1.0 / jnp.maximum(degree, 1.0)
    sums_acc[...] = jnp.zeros_like(sums_acc)
    wait_all(feed_copy)
    rows_t[...] = feed_in[...].reshape(pick.shape[1], part).astype(F32).T
    for load in loads:
        load.wait()
    pair = 2

    def forward_step(i, _):
        at = i * pair
        mixed = jnp.concatenate(
            [
                (rows_t[...] * coef_t_ref[pl.ds(at + g, 1), :]).astype(BF)
                for g in range(pair)
            ],
            axis=0,
        )
        out = dot(pick[...], mixed, ((1,), (1,)))
        weights = basis[pl.ds(at, pair)].reshape(pair * part, width)
        sums_acc[...] += dot(out.astype(BF), weights)
        agg[pl.ds(at, pair)] = out.T.astype(BF).reshape(pair, part, n_ent)
        return 0

    agg_copy = remote(
        agg.at[pl.ds((1 - core) * half, half)], agg_sib, agg_send, agg_recv, q, sib
    )
    steps = half // pair
    lax.fori_loop((1 - core) * steps, (2 - core) * steps, forward_step, 0)
    agg_copy.start()
    lax.fori_loop(core * steps, (1 + core) * steps, forward_step, 0)
    for r in range(n_z):
        sums_ref[r] = sums_acc[:, r * part : (r + 1) * part].astype(BF)

    def sums_copy(d):
        z = lax.rem(q + d, n_z)
        return remote(
            sums_ref.at[z], sums_in.at[q], sums_send.at[d], sums_recv.at[q], z, e
        )

    def sums_wait(d):
        z = lax.rem(q + d, n_z)
        remote(
            sums_ref.at[z], sums_in.at[z], sums_send.at[d], sums_recv.at[z], z, e
        ).wait_recv()

    for d in range(1, n_z):
        sums_copy(d).start()
    total = sums_ref[q].astype(F32)
    for d in range(1, n_z):
        sums_wait(d)
        total += sums_in[lax.rem(q + d, n_z)].astype(F32)
    inverse = inv_ref[...]
    pre = pre_self[...] + total * inverse
    sig = jax.nn.sigmoid(pre)
    slope = sig * (1.0 + pre * (1.0 - sig))
    pre_in[q] = (cot_ref[:, lanes].astype(F32) * slope).astype(BF)

    def pre_copy(d, z_in):
        z = lax.rem(q + d, n_z)
        return remote(pre_in.at[q], pre_in.at[z_in], pre_send.at[d], pre_recv.at[z_in], z, e)

    def act_copy(d, z_in):
        z = lax.rem(q + d, n_z)
        at = pl.ds(pl.multiple_of(z_in * part, part), part)
        return remote(
            act_ref.at[:, lanes], act_ref.at[:, at], act_send.at[d], act_recv.at[z_in], z, e
        )

    for d in range(1, n_z):
        pre_copy(d, q).start()
    act_ref[:, lanes] = (pre * sig).astype(BF)
    for d in range(1, n_z):
        pre_copy(d, lax.rem(q + d, n_z)).wait_recv()
    for z in range(n_z):
        scaled[:, z * part : (z + 1) * part] = (pre_in[z].astype(F32) * inverse).astype(BF)
    sib_copy = remote(scaled, scaled_sib, sib_send, sib_recv, q, sib)
    sib_copy.start()
    w_rows = w_ref[lanes, :]
    grad = dot(pre_in[0], w_rows[:, :part], ((1,), (1,)))
    for z in range(1, n_z):
        grad += dot(pre_in[z], w_rows[:, z * part : (z + 1) * part], ((1,), (1,)))
    agg_copy.wait_recv()
    sib_copy.wait_recv()

    group = 4
    wide = width // 2

    def x_first(d, slot):
        peer = lax.rem(x + d, 4)
        return remote(
            term_x.at[peer], x_in.at[slot], x_send.at[d], x_recv.at[slot], q, at_chip(y, peer)
        )

    def y_first(d, slot):
        peer = lax.rem(y + d, 4)
        return remote(
            term_y.at[peer], y_in.at[slot], y_send.at[d], y_recv.at[slot], q, at_chip(peer, x)
        )

    def x_then_y(d, slot):
        peer = lax.rem(y + d, 4)
        return remote(
            half_x.at[peer], xy_in.at[slot], xy_send.at[d], xy_recv.at[slot], q, at_chip(peer, x)
        )

    def y_then_x(d, slot):
        peer = lax.rem(x + d, 4)
        return remote(
            half_y.at[peer], yx_in.at[slot], yx_send.at[d], yx_recv.at[slot], q, at_chip(y, peer)
        )

    for d in (2, 1, 3, 0):
        at = lax.rem(x + d, 4)
        own = agg[pl.ds(core * half + at * group, group)].reshape(group * part, n_ent)
        other = agg_sib[pl.ds(at * group, group)].reshape(group * part, n_ent)
        terms = dot(own, scaled[...]) + dot(other, scaled_sib[...])
        terms = terms.astype(BF)
        term_x[at] = terms[:, :wide].reshape(group, part, wide)
        for g in range(group):
            term_y[g, at] = terms[g * part : (g + 1) * part, wide:]
        if d:
            x_first(d, x).start()
    for d in (2, 1, 3):
        y_first(d, y).start()
    for d in range(1, n_z):
        act_copy(d, q).start()
    seg = acc.shape[1]

    def back_step(i, _):
        weights = basis[pl.ds(i * group, group)].reshape(group * part, width)
        back[i] = dot(weights, scaled[...], ((1,), (1,))).astype(BF)
        return 0

    lax.fori_loop(0, bases // group, back_step, 0)

    def spread(first):
        acc[...] = jnp.zeros_like(acc)

        def step(i, _):
            out = dot(back[i], pick[:, first : first + seg])
            rows = acc[...]
            for g in range(group):
                coef = coef_t_ref[pl.ds(i * group + g, 1), first : first + seg]
                rows += out[g * part : (g + 1) * part] * coef
            acc[...] = rows
            return 0

        lax.fori_loop(0, bases // group, step, 0)
        block = row_out.shape[1]
        rows = acc[...].T.astype(BF).reshape(seg // block, block, part)
        row_out[first // block : (first + seg) // block] = rows

    def row_copy(peer, slot):
        return remote(
            row_out.at[peer], row_in.at[slot], row_send.at[peer], row_recv.at[slot], q, peer
        )

    def row_start(peer, _):
        @pl.when(peer != e)
        def _():
            row_copy(peer, e).start()

        return 0

    per_seg = n_e * seg // pick.shape[1]
    for n in range(n_e // per_seg):
        spread(n * seg)
        lax.fori_loop(n * per_seg, (n + 1) * per_seg, row_start, 0)
    row_in[e] = row_out[e]

    def add_up(own, arrived, recv, me):
        total = own.astype(F32)
        for d in (1, 3, 2):
            slot = lax.rem(me + d, 4)
            recv(d, slot).wait_recv()
            total += arrived[slot].astype(F32)
        return total

    half_x[...] = add_up(term_x[x], x_in, x_first, x).astype(BF)
    for d in (2, 1, 3):
        x_then_y(d, y).start()
    half_y[...] = add_up(term_y[y], y_in, y_first, y).astype(BF)
    for d in (2, 1, 3):
        y_then_x(d, x).start()
    wait_all(row_copy)
    grad += dot(pick_src[...], row_in[...].reshape(pick_src.shape[1], part))
    gf_ref[:, lanes] = grad.astype(BF)

    def gf_copy(d, z_in):
        z = lax.rem(q + d, n_z)
        at = pl.ds(pl.multiple_of(z_in * part, part), part)
        return remote(
            gf_ref.at[:, lanes], gf_ref.at[:, at], gf_send.at[d], gf_recv.at[z_in], z, e
        )

    for d in range(1, n_z):
        gf_copy(d, q).start()

    done[:, :wide] = add_up(half_x[y], xy_in, x_then_y, y)
    done[:, wide:] = add_up(half_y[x], yx_in, y_then_x, x)
    move = remote(done, gb_ref, move_send, move_recv, to_z, to_e)

    @pl.when(keeps)
    def _():
        gb_ref[...] = done[...]

    @pl.when(moves)
    def _():
        move.start()
        move.wait_send()
        remote(done, gb_ref, move_send, move_recv, from_z, from_e).wait_recv()

    for d in range(1, n_z):
        z = lax.rem(q + d, n_z)
        act_copy(d, z).wait_recv()
        gf_copy(d, z).wait_recv()
        sums_copy(d).wait_send()
        pre_copy(d, q).wait_send()
        act_copy(d, q).wait_send()
        gf_copy(d, q).wait_send()
    agg_copy.wait_send()
    sib_copy.wait_send()

    for d in (1, 2, 3):
        x_first(d, x).wait_send()
        y_first(d, y).wait_send()
        x_then_y(d, y).wait_send()
        y_then_x(d, x).wait_send()

    for d in range(1, n_z):
        meta_copy(d, q).wait_send()
    sent_all(tag_copy)
    sent_all(feed_copy)
    sent_all(row_copy)


def run_step(src, dst, rel, groups, counts, features, w_self, cotangent, coeffs, basis_mats):
    n_z = lax.axis_size("rel")
    n_e = lax.axis_size("ent")
    n_ent, width = features.shape
    bases = coeffs.shape[0]
    all_slots = src.shape[1] * n_z
    part = width // n_z
    half = bases // 2
    block = all_slots // n_e
    vm = pl.BlockSpec(memory_space=pltpu.VMEM)
    dma = pltpu.SemaphoreType.DMA
    return pl.pallas_call(
        functools.partial(step_kernel, n_z, n_e),
        out_shape=(
            jax.ShapeDtypeStruct((n_ent, width), BF),
            jax.ShapeDtypeStruct((n_ent, width), BF),
            jax.ShapeDtypeStruct((part, width), F32),
        ),
        in_specs=[vm] * 9 + [pl.BlockSpec(memory_space=pl.ANY)],
        out_specs=(vm, vm, vm),
        scratch_shapes=[
            pltpu.VMEM((1, 256), I32),
            pltpu.VMEM((n_e // 2, 3, 1, 128), I32),
            pltpu.VMEM((n_z, n_e // 2, 3, 1, 128), I32),
            pltpu.VMEM((n_e // 2, 3, 1, 128), I32),
            pltpu.VMEM((n_e, 3, 1, 128), I32),
            pltpu.VMEM((1, all_slots), I32),
            pltpu.VMEM((1, all_slots), I32),
            pltpu.VMEM((bases, 1024), F32),
            pltpu.VMEM((n_e, block, part), BF),
            pltpu.VMEM((n_e, block, part), BF),
            pltpu.VMEM((part, all_slots), F32),
            pltpu.VMEM((bases, all_slots), F32),
            pltpu.VMEM((n_ent, part), F32),
            pltpu.VMEM((n_ent, part), F32),
            pltpu.VMEM((n_ent, width), F32),
            pltpu.VMEM((n_z, n_ent, part), BF),
            pltpu.VMEM((bases, part, n_ent), BF),
            pltpu.VMEM((n_z, n_ent, part), BF),
            pltpu.VMEM((n_z, n_ent, part), BF),
            pltpu.VMEM((n_ent, width), BF),
            pltpu.VMEM((n_ent, width), BF),
            pltpu.VMEM((half, part, n_ent), BF),
            pltpu.VMEM((bases, part, width), BF),
            pltpu.VMEM((n_ent, all_slots), BF),
            pltpu.VMEM((n_ent, all_slots), BF),
            pltpu.VMEM((part, all_slots // 2), F32),
            pltpu.VMEM((bases // 4, 4 * part, n_ent), BF),
            pltpu.VMEM((4, 4, part, width // 2), BF),
            pltpu.VMEM((4, 4, part, width // 2), BF),
            pltpu.VMEM((4, 4, part, width // 2), BF),
            pltpu.VMEM((4, 4, part, width // 2), BF),
            pltpu.VMEM((4, part, width // 2), BF),
            pltpu.VMEM((4, part, width // 2), BF),
            pltpu.VMEM((4, part, width // 2), BF),
            pltpu.VMEM((4, part, width // 2), BF),
            pltpu.VMEM((part, width), F32),
            pltpu.VMEM((n_e, block, part), BF),
            pltpu.VMEM((n_e, block, part), BF),
            dma((bases // 4,)),
            dma((n_z,)),
            dma((n_z,)),
            dma((n_z,)),
            dma((n_z,)),
            dma((n_z,)),
            dma((n_z,)),
            dma,
            dma,
            dma,
            dma,
            dma((4,)),
            dma((4,)),
            dma((4,)),
            dma((4,)),
            dma((4,)),
            dma((4,)),
            dma((4,)),
            dma((4,)),
            dma,
            dma,
            dma((n_e,)),
            dma((n_e,)),
            dma((n_z,)),
            dma((n_z,)),
            dma((n_z,)),
            dma((n_z,)),
            dma((n_e,)),
            dma((n_e,)),
            dma((n_e,)),
            dma((n_e,)),
        ],
        compiler_params=pltpu.CompilerParams(
            vmem_limit_bytes=56 * MIB, collective_id=0, has_side_effects=True
        ),
    )(
        src,
        dst,
        rel,
        groups,
        counts,
        features,
        w_self,
        cotangent,
        coeffs,
        basis_mats.reshape(2, 2, 4, 2, width, width),
    )


def store_kernel(a_in, b_in, c_in, a_out, b_out, c_out, sems):
    copies = [
        pltpu.make_async_copy(i, o, sems.at[n])
        for n, (i, o) in enumerate(((a_in, a_out), (b_in, b_out), (c_in, c_out)))
    ]
    for copy in copies:
        copy.start()
    for copy in copies:
        copy.wait()


def store(arrays):
    hbm = pl.BlockSpec(memory_space=pl.ANY)
    return pl.pallas_call(
        store_kernel,
        out_shape=tuple(jax.ShapeDtypeStruct(a.shape, a.dtype) for a in arrays),
        in_specs=[hbm] * 3,
        out_specs=(hbm,) * 3,
        scratch_shapes=[pltpu.SemaphoreType.DMA((3,))],
    )(*arrays)


def per_device(
    features,
    w_self,
    basis_mats,
    basis_coeffs,
    group_rels,
    rel_local,
    edge_src,
    edge_dst,
    block_counts,
    cotangent,
):
    outs = run_step(
        edge_src[None],
        edge_dst[None],
        rel_local[None],
        group_rels[None],
        block_counts[0],
        features,
        w_self,
        cotangent,
        basis_coeffs.T,
        basis_mats,
    )
    return store(outs)


def solution(mesh):
    placed = (
        P("ent", None),
        P(),
        P(),
        P(),
        P("rel"),
        P(("rel", "ent")),
        P(("rel", "ent")),
        P(("rel", "ent")),
        P("rel", "ent", None),
        P("ent", None),
    )
    return jax.shard_map(
        per_device,
        mesh=mesh,
        in_specs=placed,
        out_specs=(P("ent", None), P("ent", None), P(("rel", "ent"), None)),
        check_vma=False,
    )
```

```python
import functools

import jax
import jax.numpy as jnp
from jax import lax
from jax.experimental import pallas as pl
from jax.experimental.pallas import tpu as pltpu
from jax.sharding import PartitionSpec as P

BF = jnp.bfloat16
F32 = jnp.float32
I32 = jnp.int32
MIB = 1 << 20


def dot(a, b, dims=((1,), (0,))):
    return lax.dot_general(a, b, (dims, ((), ())), preferred_element_type=F32)


def one_hot(count, row):
    ids = lax.broadcasted_iota(I32, (count, row.shape[1]), 0)
    return (ids == row).astype(F32).astype(BF)


def split3(x):
    hi = x.astype(BF)
    rest = x - hi.astype(F32)
    mid = rest.astype(BF)
    lo = (rest - mid.astype(F32)).astype(BF)
    return hi, mid, lo


def slot_order(bases):
    half = bases // 2
    return [
        c * half + (x % 2) * 8 + y * 2 + x // 2
        for c in range(2)
        for x in range(4)
        for y in range(half // 4)
    ]


def basis_loads(basis_hbm, basis, sems, q):
    part = basis.shape[1]
    lanes = pl.ds(pl.multiple_of(q * part, part), part)
    loads = []
    for c in range(2):
        for x in range(4):
            at = c * 4 + x
            loads.append(
                pltpu.make_async_copy(
                    basis_hbm.at[c, x % 2, :, x // 2, lanes, :],
                    basis.at[pl.ds(at * 4, 4)],
                    sems.at[at],
                )
            )
    return loads


def remote(src, dst, send_sem, recv_sem, z, e):
    return pltpu.make_async_remote_copy(
        src_ref=src,
        dst_ref=dst,
        send_sem=send_sem,
        recv_sem=recv_sem,
        device_id=(z, e),
        device_id_type=pl.DeviceIdType.MESH,
    )


def place_metadata(q, e, src_ref, dst_ref, rel_ref, group_row, counts_ref, meta_ref, n_ent):
    slots = src_ref.shape[1]
    n_e = counts_ref.shape[1]
    pairs, fields, _, lanes = meta_ref.shape
    cap = slots // n_e
    spot = lax.broadcasted_iota(I32, (1, slots), 1)
    peer = lax.div(spot, cap)
    rows16 = lax.broadcasted_iota(I32, (pairs, slots), 0)

    def digits(v):
        return lax.div(v, 32).astype(F32), lax.rem(v, 32).astype(F32)

    hi, lo = digits(group_row[...])
    level = lax.broadcasted_iota(I32, (pairs, group_row.shape[1]), 0)
    table = jnp.where(level == 0, hi, jnp.where(level == 1, lo, 0.0)).astype(BF)
    rel_digits = dot(table, one_hot(group_row.shape[1], rel_ref[...]))
    counts = jnp.broadcast_to(counts_ref[...].astype(F32), (pairs, n_e)).astype(BF)
    limit = dot(counts, one_hot(n_e, peer))[:1]
    live = lax.rem(spot, cap).astype(F32) < limit
    dst = jnp.where(live, dst_ref[...] - peer * n_ent, n_ent)
    values = digits(src_ref[...] - e * n_ent) + digits(dst)
    values = values + (rel_digits[:1], rel_digits[1:2])
    here = rows16 == lax.div(peer, 2)
    stacked = jnp.concatenate([jnp.where(here, v, 0.0) for v in values], axis=0).astype(BF)
    index = lax.broadcasted_iota(I32, (slots, lanes), 0)
    lane = lax.broadcasted_iota(I32, (slots, lanes), 1)
    half = lax.rem(lax.div(index, cap), 2)
    target = half * (lanes // 2) + q * cap + lax.rem(index, cap)
    moved = dot(stacked, (target == lane).astype(F32).astype(BF))
    for f in range(fields):
        hi = moved[2 * f * pairs : (2 * f + 1) * pairs]
        lo = moved[(2 * f + 1) * pairs : (2 * f + 2) * pairs]
        field = (hi * 32.0 + lo + 0.5).astype(I32)
        for t in range(pairs):
            meta_ref[t, f] = field[t : t + 1, :]


def step_kernel(
    n_z,
    n_e,
    src_ref,
    dst_ref,
    rel_ref,
    groups_ref,
    counts_ref,
    feat_ref,
    w_ref,
    cot_ref,
    coef_ref,
    basis_hbm,
    act_ref,
    gf_ref,
    gb_ref,
    group_row,
    meta_ref,
    meta_z,
    meta_all,
    tags,
    line,
    line_rel,
    table,
    feed_out,
    feed_in,
    rows_t,
    coef_t_ref,
    inv_ref,
    pre_self,
    sums_acc,
    sums_ref,
    agg,
    sums_in,
    pre_in,
    scaled,
    scaled_sib,
    agg_sib,
    basis,
    pick,
    pick_src,
    acc,
    back,
    term_x,
    term_y,
    x_in,
    y_in,
    half_x,
    half_y,
    xy_in,
    yx_in,
    done,
    row_out,
    row_in,
    basis_sem,
    sums_send,
    sums_recv,
    act_send,
    act_recv,
    pre_send,
    pre_recv,
    agg_send,
    agg_recv,
    sib_send,
    sib_recv,
    x_send,
    x_recv,
    y_send,
    y_recv,
    xy_send,
    xy_recv,
    yx_send,
    yx_recv,
    move_send,
    move_recv,
    row_send,
    row_recv,
    gf_send,
    gf_recv,
    meta_send,
    meta_recv,
    tag_send,
    tag_recv,
    feed_send,
    feed_recv,
):
    q = lax.axis_index("rel")
    e = lax.axis_index("ent")
    core = lax.rem(e, 2)
    chip = lax.div(e, 2)
    sib = e + 1 - 2 * core
    bases, part, width = basis.shape
    half = bases // 2
    lanes = pl.ds(pl.multiple_of(q * part, part), part)
    x = lax.rem(chip, 4)
    y = lax.div(chip, 4)

    def at_chip(y_at, x_at):
        return (y_at * 4 + x_at) * 2 + core

    to_z = 2 * core + lax.rem(x, 2)
    to_e = (y * 4 + lax.div(x, 2) * 2 + lax.div(q, 2)) * 2 + lax.rem(q, 2)
    from_z = lax.rem(x, 2) * 2 + core
    from_e = (y * 4 + lax.div(x, 2) * 2 + lax.rem(q, 2)) * 2 + lax.div(q, 2)
    keeps = jnp.logical_and(to_z == q, to_e == e)
    moves = jnp.logical_not(keeps)

    barrier = pltpu.get_barrier_semaphore()

    def greet(z, peer):
        pl.semaphore_signal(
            barrier, inc=1, device_id=(z, peer), device_id_type=pl.DeviceIdType.MESH
        )

    for d in range(1, n_z):
        greet(lax.rem(q + d, n_z), e)

    def greet_plane(d, _):
        greet(q, lax.rem(e + d, n_e))
        return 0

    lax.fori_loop(1, n_e, greet_plane, 0)

    @pl.when(moves)
    def _():
        greet(from_z, from_e)

    loads = basis_loads(basis_hbm, basis, basis_sem, q)
    for load in loads:
        load.start()
    table[...] = jnp.zeros_like(table)
    table[:, : coef_ref.shape[1]] = coef_ref[...]
    group_row[...] = jnp.zeros_like(group_row)
    group_row[:, : groups_ref.shape[1]] = groups_ref[...]
    place_metadata(
        q, e, src_ref, dst_ref, rel_ref, group_row, counts_ref, meta_ref, feat_ref.shape[0]
    )
    pre_self[...] = dot(feat_ref[...], w_ref[:, lanes])
    pl.semaphore_wait(barrier, n_z - 1 + n_e - 1 + moves.astype(I32))

    def meta_copy(d, slot):
        z = lax.rem(q + d, n_z)
        return remote(meta_ref, meta_z.at[slot], meta_send.at[d], meta_recv.at[slot], z, e)

    def tag_copy(peer, slot):
        return remote(
            meta_all.at[lax.div(peer, 2)],
            tags.at[slot],
            tag_send.at[peer],
            tag_recv.at[slot],
            q,
            peer,
        )

    def feed_copy(peer, slot):
        return remote(
            feed_out.at[peer], feed_in.at[slot], feed_send.at[peer], feed_recv.at[slot], q, peer
        )

    def start_all(copy):
        def go(d, _):
            copy(lax.rem(e + d, n_e), e).start()
            return 0

        lax.fori_loop(1, n_e, go, 0)

    def wait_all(copy):
        def go(d, _):
            peer = lax.rem(e + d, n_e)
            copy(peer, peer).wait_recv()
            return 0

        lax.fori_loop(1, n_e, go, 0)

    def sent_all(copy):
        def go(d, _):
            copy(lax.rem(e + d, n_e), e).wait_send()
            return 0

        lax.fori_loop(1, n_e, go, 0)

    for d in range(1, n_z):
        meta_copy(d, q).start()
    feat_t = feat_ref[:, lanes].T
    meta = meta_ref[...]
    for d in range(1, n_z):
        slot = lax.rem(q + d, n_z)
        meta_copy(d, slot).wait_recv()
        meta += meta_z[slot]
    meta_all[...] = meta
    start_all(tag_copy)
    tags[e] = meta_all[lax.div(e, 2)]
    n_ent = pick.shape[0]
    pairs = n_e // 2
    wide_lanes = meta_ref.shape[3]
    for t in range(pairs):
        line[:, t * wide_lanes : (t + 1) * wide_lanes] = meta_all[t, 0]
    pick_src[...] = one_hot(n_ent, line[...])
    feed = dot(feat_t, pick_src[...])
    feed_out[...] = feed.T.astype(BF).reshape(feed_out.shape)
    start_all(feed_copy)
    feed_in[e] = feed_out[e]
    wait_all(tag_copy)
    left = lax.broadcasted_iota(I32, (1, wide_lanes), 1) < wide_lanes // 2
    for f, out in ((1, line), (2, line_rel)):
        for t in range(pairs):
            even = tags[2 * t, f]
            odd = tags[2 * t + 1, f]
            even = jnp.where(core == 0, even, pltpu.roll(even, wide_lanes // 2, 1))
            odd = jnp.where(core == 0, pltpu.roll(odd, wide_lanes // 2, 1), odd)
            out[:, t * wide_lanes : (t + 1) * wide_lanes] = jnp.where(left, even, odd)
    which = one_hot(table.shape[1], line_rel[...])
    hi, mid, lo = split3(table[...])
    coef_t = dot(jnp.concatenate([hi, mid, lo], axis=0), which)
    coef_t = coef_t[:bases] + coef_t[bases : 2 * bases] + coef_t[2 * bases : 3 * bases]
    for p, b in enumerate(slot_order(bases)):
        coef_t_ref[p : p + 1, :] = coef_t[b : b + 1, :]
    pick[...] = one_hot(n_ent, line[...])
    degree = dot(pick[...], jnp.ones((pick.shape[1], part), BF))
    inv_ref[...] = 1.0 / jnp.maximum(degree, 1.0)
    sums_acc[...] = jnp.zeros_like(sums_acc)
    wait_all(feed_copy)
    rows_t[...] = feed_in[...].reshape(pick.shape[1], part).astype(F32).T
    for load in loads:
        load.wait()
    pair = 8

    def forward_step(i, _):
        at = i * pair
        mixed = jnp.concatenate(
            [
                (rows_t[...] * coef_t_ref[pl.ds(at + g, 1), :]).astype(BF)
                for g in range(pair)
            ],
            axis=0,
        )
        out = dot(pick[...], mixed, ((1,), (1,)))
        weights = basis[pl.ds(at, pair)].reshape(pair * part, width)
        sums_acc[...] += dot(out.astype(BF), weights)
        agg[pl.ds(at, pair)] = out.T.astype(BF).reshape(pair, part, n_ent)
        return 0

    agg_copy = remote(
        agg.at[pl.ds((1 - core) * half, half)], agg_sib, agg_send, agg_recv, q, sib
    )
    steps = half // pair
    lax.fori_loop((1 - core) * steps, (2 - core) * steps, forward_step, 0)
    agg_copy.start()
    lax.fori_loop(core * steps, (1 + core) * steps, forward_step, 0)
    for r in range(n_z):
        sums_ref[r] = sums_acc[:, r * part : (r + 1) * part].astype(BF)

    def sums_copy(d):
        z = lax.rem(q + d, n_z)
        return remote(
            sums_ref.at[z], sums_in.at[q], sums_send.at[d], sums_recv.at[q], z, e
        )

    def sums_wait(d):
        z = lax.rem(q + d, n_z)
        remote(
            sums_ref.at[z], sums_in.at[z], sums_send.at[d], sums_recv.at[z], z, e
        ).wait_recv()

    for d in range(1, n_z):
        sums_copy(d).start()
    total = sums_ref[q].astype(F32)
    for d in range(1, n_z):
        sums_wait(d)
        total += sums_in[lax.rem(q + d, n_z)].astype(F32)
    inverse = inv_ref[...]
    pre = pre_self[...] + total * inverse
    sig = jax.nn.sigmoid(pre)
    slope = sig * (1.0 + pre * (1.0 - sig))
    pre_in[q] = (cot_ref[:, lanes].astype(F32) * slope).astype(BF)

    def pre_copy(d, z_in):
        z = lax.rem(q + d, n_z)
        return remote(pre_in.at[q], pre_in.at[z_in], pre_send.at[d], pre_recv.at[z_in], z, e)

    def act_copy(d, z_in):
        z = lax.rem(q + d, n_z)
        at = pl.ds(pl.multiple_of(z_in * part, part), part)
        return remote(
            act_ref.at[:, lanes], act_ref.at[:, at], act_send.at[d], act_recv.at[z_in], z, e
        )

    for d in range(1, n_z):
        pre_copy(d, q).start()
    act_ref[:, lanes] = (pre * sig).astype(BF)
    for d in range(1, n_z):
        pre_copy(d, lax.rem(q + d, n_z)).wait_recv()
    for z in range(n_z):
        scaled[:, z * part : (z + 1) * part] = (pre_in[z].astype(F32) * inverse).astype(BF)
    sib_copy = remote(scaled, scaled_sib, sib_send, sib_recv, q, sib)
    sib_copy.start()
    w_rows = w_ref[lanes, :]
    grad = dot(pre_in[0], w_rows[:, :part], ((1,), (1,)))
    for z in range(1, n_z):
        grad += dot(pre_in[z], w_rows[:, z * part : (z + 1) * part], ((1,), (1,)))
    agg_copy.wait_recv()
    sib_copy.wait_recv()

    group = 4
    wide = width // 2

    def x_first(d, slot):
        peer = lax.rem(x + d, 4)
        return remote(
            term_x.at[peer], x_in.at[slot], x_send.at[d], x_recv.at[slot], q, at_chip(y, peer)
        )

    def y_first(d, slot):
        peer = lax.rem(y + d, 4)
        return remote(
            term_y.at[peer], y_in.at[slot], y_send.at[d], y_recv.at[slot], q, at_chip(peer, x)
        )

    def x_then_y(d, slot):
        peer = lax.rem(y + d, 4)
        return remote(
            half_x.at[peer], xy_in.at[slot], xy_send.at[d], xy_recv.at[slot], q, at_chip(peer, x)
        )

    def y_then_x(d, slot):
        peer = lax.rem(x + d, 4)
        return remote(
            half_y.at[peer], yx_in.at[slot], yx_send.at[d], yx_recv.at[slot], q, at_chip(y, peer)
        )

    for d in (2, 1, 3, 0):
        at = lax.rem(x + d, 4)
        own = agg[pl.ds(core * half + at * group, group)].reshape(group * part, n_ent)
        other = agg_sib[pl.ds(at * group, group)].reshape(group * part, n_ent)
        terms = dot(own, scaled[...]) + dot(other, scaled_sib[...])
        terms = terms.astype(BF)
        term_x[at] = terms[:, :wide].reshape(group, part, wide)
        for g in range(group):
            term_y[g, at] = terms[g * part : (g + 1) * part, wide:]
        if d:
            x_first(d, x).start()
    for d in (2, 1, 3):
        y_first(d, y).start()
    for d in range(1, n_z):
        act_copy(d, q).start()
    seg = acc.shape[1]

    def back_step(i, _):
        weights = basis[pl.ds(i * group, group)].reshape(group * part, width)
        back[i] = dot(weights, scaled[...], ((1,), (1,))).astype(BF)
        return 0

    lax.fori_loop(0, bases // group, back_step, 0)

    def spread(first):
        acc[...] = jnp.zeros_like(acc)

        def step(i, _):
            out = dot(back[i], pick[:, first : first + seg])
            rows = acc[...]
            for g in range(group):
                coef = coef_t_ref[pl.ds(i * group + g, 1), first : first + seg]
                rows += out[g * part : (g + 1) * part] * coef
            acc[...] = rows
            return 0

        lax.fori_loop(0, bases // group, step, 0)
        block = row_out.shape[1]
        rows = acc[...].T.astype(BF).reshape(seg // block, block, part)
        row_out[first // block : (first + seg) // block] = rows

    def row_copy(peer, slot):
        return remote(
            row_out.at[peer], row_in.at[slot], row_send.at[peer], row_recv.at[slot], q, peer
        )

    def row_start(peer, _):
        @pl.when(peer != e)
        def _():
            row_copy(peer, e).start()

        return 0

    per_seg = n_e * seg // pick.shape[1]
    for n in range(n_e // per_seg):
        spread(n * seg)
        lax.fori_loop(n * per_seg, (n + 1) * per_seg, row_start, 0)
    row_in[e] = row_out[e]

    def add_up(own, arrived, recv, me):
        total = own.astype(F32)
        for d in (1, 3, 2):
            slot = lax.rem(me + d, 4)
            recv(d, slot).wait_recv()
            total += arrived[slot].astype(F32)
        return total

    half_x[...] = add_up(term_x[x], x_in, x_first, x).astype(BF)
    for d in (2, 1, 3):
        x_then_y(d, y).start()
    half_y[...] = add_up(term_y[y], y_in, y_first, y).astype(BF)
    for d in (2, 1, 3):
        y_then_x(d, x).start()
    wait_all(row_copy)
    grad += dot(pick_src[...], row_in[...].reshape(pick_src.shape[1], part))
    gf_ref[:, lanes] = grad.astype(BF)

    def gf_copy(d, z_in):
        z = lax.rem(q + d, n_z)
        at = pl.ds(pl.multiple_of(z_in * part, part), part)
        return remote(
            gf_ref.at[:, lanes], gf_ref.at[:, at], gf_send.at[d], gf_recv.at[z_in], z, e
        )

    for d in range(1, n_z):
        gf_copy(d, q).start()

    done[:, :wide] = add_up(half_x[y], xy_in, x_then_y, y)
    done[:, wide:] = add_up(half_y[x], yx_in, y_then_x, x)
    move = remote(done, gb_ref, move_send, move_recv, to_z, to_e)

    @pl.when(keeps)
    def _():
        gb_ref[...] = done[...]

    @pl.when(moves)
    def _():
        move.start()
        move.wait_send()
        remote(done, gb_ref, move_send, move_recv, from_z, from_e).wait_recv()

    for d in range(1, n_z):
        z = lax.rem(q + d, n_z)
        act_copy(d, z).wait_recv()
        gf_copy(d, z).wait_recv()
        sums_copy(d).wait_send()
        pre_copy(d, q).wait_send()
        act_copy(d, q).wait_send()
        gf_copy(d, q).wait_send()
    agg_copy.wait_send()
    sib_copy.wait_send()

    for d in (1, 2, 3):
        x_first(d, x).wait_send()
        y_first(d, y).wait_send()
        x_then_y(d, y).wait_send()
        y_then_x(d, x).wait_send()

    for d in range(1, n_z):
        meta_copy(d, q).wait_send()
    sent_all(tag_copy)
    sent_all(feed_copy)
    sent_all(row_copy)


def run_step(src, dst, rel, groups, counts, features, w_self, cotangent, coeffs, basis_mats):
    n_z = lax.axis_size("rel")
    n_e = lax.axis_size("ent")
    n_ent, width = features.shape
    bases = coeffs.shape[0]
    all_slots = src.shape[1] * n_z
    part = width // n_z
    half = bases // 2
    block = all_slots // n_e
    vm = pl.BlockSpec(memory_space=pltpu.VMEM)
    dma = pltpu.SemaphoreType.DMA
    return pl.pallas_call(
        functools.partial(step_kernel, n_z, n_e),
        out_shape=(
            jax.ShapeDtypeStruct((n_ent, width), BF),
            jax.ShapeDtypeStruct((n_ent, width), BF),
            jax.ShapeDtypeStruct((part, width), F32),
        ),
        in_specs=[vm] * 9 + [pl.BlockSpec(memory_space=pl.ANY)],
        out_specs=(vm, vm, vm),
        scratch_shapes=[
            pltpu.VMEM((1, 256), I32),
            pltpu.VMEM((n_e // 2, 3, 1, 128), I32),
            pltpu.VMEM((n_z, n_e // 2, 3, 1, 128), I32),
            pltpu.VMEM((n_e // 2, 3, 1, 128), I32),
            pltpu.VMEM((n_e, 3, 1, 128), I32),
            pltpu.VMEM((1, all_slots), I32),
            pltpu.VMEM((1, all_slots), I32),
            pltpu.VMEM((bases, 1024), F32),
            pltpu.VMEM((n_e, block, part), BF),
            pltpu.VMEM((n_e, block, part), BF),
            pltpu.VMEM((part, all_slots), F32),
            pltpu.VMEM((bases, all_slots), F32),
            pltpu.VMEM((n_ent, part), F32),
            pltpu.VMEM((n_ent, part), F32),
            pltpu.VMEM((n_ent, width), F32),
            pltpu.VMEM((n_z, n_ent, part), BF),
            pltpu.VMEM((bases, part, n_ent), BF),
            pltpu.VMEM((n_z, n_ent, part), BF),
            pltpu.VMEM((n_z, n_ent, part), BF),
            pltpu.VMEM((n_ent, width), BF),
            pltpu.VMEM((n_ent, width), BF),
            pltpu.VMEM((half, part, n_ent), BF),
            pltpu.VMEM((bases, part, width), BF),
            pltpu.VMEM((n_ent, all_slots), BF),
            pltpu.VMEM((n_ent, all_slots), BF),
            pltpu.VMEM((part, all_slots // 2), F32),
            pltpu.VMEM((bases // 4, 4 * part, n_ent), BF),
            pltpu.VMEM((4, 4, part, width // 2), BF),
            pltpu.VMEM((4, 4, part, width // 2), BF),
            pltpu.VMEM((4, 4, part, width // 2), BF),
            pltpu.VMEM((4, 4, part, width // 2), BF),
            pltpu.VMEM((4, part, width // 2), BF),
            pltpu.VMEM((4, part, width // 2), BF),
            pltpu.VMEM((4, part, width // 2), BF),
            pltpu.VMEM((4, part, width // 2), BF),
            pltpu.VMEM((part, width), F32),
            pltpu.VMEM((n_e, block, part), BF),
            pltpu.VMEM((n_e, block, part), BF),
            dma((bases // 4,)),
            dma((n_z,)),
            dma((n_z,)),
            dma((n_z,)),
            dma((n_z,)),
            dma((n_z,)),
            dma((n_z,)),
            dma,
            dma,
            dma,
            dma,
            dma((4,)),
            dma((4,)),
            dma((4,)),
            dma((4,)),
            dma((4,)),
            dma((4,)),
            dma((4,)),
            dma((4,)),
            dma,
            dma,
            dma((n_e,)),
            dma((n_e,)),
            dma((n_z,)),
            dma((n_z,)),
            dma((n_z,)),
            dma((n_z,)),
            dma((n_e,)),
            dma((n_e,)),
            dma((n_e,)),
            dma((n_e,)),
        ],
        compiler_params=pltpu.CompilerParams(
            vmem_limit_bytes=56 * MIB, collective_id=0, has_side_effects=True
        ),
    )(
        src,
        dst,
        rel,
        groups,
        counts,
        features,
        w_self,
        cotangent,
        coeffs,
        basis_mats.reshape(2, 2, 4, 2, width, width),
    )


def store_kernel(a_in, b_in, c_in, a_out, b_out, c_out, sems):
    copies = [
        pltpu.make_async_copy(i, o, sems.at[n])
        for n, (i, o) in enumerate(((a_in, a_out), (b_in, b_out), (c_in, c_out)))
    ]
    for copy in copies:
        copy.start()
    for copy in copies:
        copy.wait()


def store(arrays):
    hbm = pl.BlockSpec(memory_space=pl.ANY)
    return pl.pallas_call(
        store_kernel,
        out_shape=tuple(jax.ShapeDtypeStruct(a.shape, a.dtype) for a in arrays),
        in_specs=[pl.BlockSpec(memory_space=pltpu.VMEM)] * 3,
        out_specs=(hbm,) * 3,
        scratch_shapes=[pltpu.SemaphoreType.DMA((3,))],
    )(*arrays)


def per_device(
    features,
    w_self,
    basis_mats,
    basis_coeffs,
    group_rels,
    rel_local,
    edge_src,
    edge_dst,
    block_counts,
    cotangent,
):
    outs = run_step(
        edge_src[None],
        edge_dst[None],
        rel_local[None],
        group_rels[None],
        block_counts[0],
        features,
        w_self,
        cotangent,
        basis_coeffs.T,
        basis_mats,
    )
    return store(outs)


def solution(mesh):
    placed = (
        P("ent", None),
        P(),
        P(),
        P(),
        P("rel"),
        P(("rel", "ent")),
        P(("rel", "ent")),
        P(("rel", "ent")),
        P("rel", "ent", None),
        P("ent", None),
    )
    return jax.shard_map(
        per_device,
        mesh=mesh,
        in_specs=placed,
        out_specs=(P("ent", None), P("ent", None), P(("rel", "ent"), None)),
        check_vma=False,
    )
```

```python
import functools

import jax
import jax.numpy as jnp
from jax import lax
from jax.experimental import pallas as pl
from jax.experimental.pallas import tpu as pltpu
from jax.sharding import PartitionSpec as P

BF = jnp.bfloat16
F32 = jnp.float32
I32 = jnp.int32
MIB = 1 << 20


def dot(a, b, dims=((1,), (0,))):
    return lax.dot_general(a, b, (dims, ((), ())), preferred_element_type=F32)


def one_hot(count, row):
    ids = lax.broadcasted_iota(I32, (count, row.shape[1]), 0)
    return (ids == row).astype(F32).astype(BF)


def split3(x):
    hi = x.astype(BF)
    rest = x - hi.astype(F32)
    mid = rest.astype(BF)
    lo = (rest - mid.astype(F32)).astype(BF)
    return hi, mid, lo


def slot_order(bases):
    half = bases // 2
    return [
        c * half + (x % 2) * 8 + y * 2 + x // 2
        for c in range(2)
        for x in range(4)
        for y in range(half // 4)
    ]


def basis_loads(basis_hbm, basis, sems, q):
    part = basis.shape[1]
    lanes = pl.ds(pl.multiple_of(q * part, part), part)
    loads = []
    for c in range(2):
        for x in range(4):
            at = c * 4 + x
            loads.append(
                pltpu.make_async_copy(
                    basis_hbm.at[c, x % 2, :, x // 2, lanes, :],
                    basis.at[pl.ds(at * 4, 4)],
                    sems.at[at],
                )
            )
    return loads


def remote(src, dst, send_sem, recv_sem, z, e):
    return pltpu.make_async_remote_copy(
        src_ref=src,
        dst_ref=dst,
        send_sem=send_sem,
        recv_sem=recv_sem,
        device_id=(z, e),
        device_id_type=pl.DeviceIdType.MESH,
    )


def place_metadata(q, e, src_ref, dst_ref, rel_ref, group_row, counts_ref, meta_ref, n_ent):
    slots = src_ref.shape[1]
    n_e = counts_ref.shape[1]
    pairs, fields, _, lanes = meta_ref.shape
    cap = slots // n_e
    spot = lax.broadcasted_iota(I32, (1, slots), 1)
    peer = lax.div(spot, cap)
    rows16 = lax.broadcasted_iota(I32, (pairs, slots), 0)

    def digits(v):
        return lax.div(v, 32).astype(F32), lax.rem(v, 32).astype(F32)

    hi, lo = digits(group_row[...])
    level = lax.broadcasted_iota(I32, (pairs, group_row.shape[1]), 0)
    table = jnp.where(level == 0, hi, jnp.where(level == 1, lo, 0.0)).astype(BF)
    rel_digits = dot(table, one_hot(group_row.shape[1], rel_ref[...]))
    counts = jnp.broadcast_to(counts_ref[...].astype(F32), (pairs, n_e)).astype(BF)
    limit = dot(counts, one_hot(n_e, peer))[:1]
    live = lax.rem(spot, cap).astype(F32) < limit
    dst = jnp.where(live, dst_ref[...] - peer * n_ent, n_ent)
    values = digits(src_ref[...] - e * n_ent) + digits(dst)
    values = values + (rel_digits[:1], rel_digits[1:2])
    here = rows16 == lax.div(peer, 2)
    stacked = jnp.concatenate([jnp.where(here, v, 0.0) for v in values], axis=0).astype(BF)
    index = lax.broadcasted_iota(I32, (slots, lanes), 0)
    lane = lax.broadcasted_iota(I32, (slots, lanes), 1)
    half = lax.rem(lax.div(index, cap), 2)
    target = half * (lanes // 2) + q * cap + lax.rem(index, cap)
    moved = dot(stacked, (target == lane).astype(F32).astype(BF))
    for f in range(fields):
        hi = moved[2 * f * pairs : (2 * f + 1) * pairs]
        lo = moved[(2 * f + 1) * pairs : (2 * f + 2) * pairs]
        field = (hi * 32.0 + lo + 0.5).astype(I32)
        for t in range(pairs):
            meta_ref[t, f] = field[t : t + 1, :]


def step_kernel(
    n_z,
    n_e,
    src_ref,
    dst_ref,
    rel_ref,
    groups_ref,
    counts_ref,
    feat_ref,
    w_ref,
    cot_ref,
    coef_ref,
    basis_hbm,
    act_ref,
    gf_ref,
    gb_ref,
    group_row,
    meta_ref,
    meta_z,
    meta_all,
    tags,
    line,
    line_rel,
    table,
    feed_out,
    feed_in,
    rows_t,
    coef_t_ref,
    inv_ref,
    pre_self,
    sums_acc,
    sums_ref,
    agg,
    sums_in,
    pre_in,
    scaled,
    scaled_sib,
    agg_sib,
    basis,
    pick,
    pick_src,
    acc,
    back,
    term_x,
    term_y,
    x_in,
    y_in,
    half_x,
    half_y,
    xy_in,
    yx_in,
    done,
    done_in,
    row_out,
    row_in,
    basis_sem,
    sums_send,
    sums_recv,
    act_send,
    act_recv,
    pre_send,
    pre_recv,
    agg_send,
    agg_recv,
    sib_send,
    sib_recv,
    x_send,
    x_recv,
    y_send,
    y_recv,
    xy_send,
    xy_recv,
    yx_send,
    yx_recv,
    move_send,
    move_recv,
    row_send,
    row_recv,
    gf_send,
    gf_recv,
    meta_send,
    meta_recv,
    tag_send,
    tag_recv,
    feed_send,
    feed_recv,
):
    q = lax.axis_index("rel")
    e = lax.axis_index("ent")
    core = lax.rem(e, 2)
    chip = lax.div(e, 2)
    sib = e + 1 - 2 * core
    bases, part, width = basis.shape
    half = bases // 2
    lanes = pl.ds(pl.multiple_of(q * part, part), part)
    x = lax.rem(chip, 4)
    y = lax.div(chip, 4)

    def at_chip(y_at, x_at):
        return (y_at * 4 + x_at) * 2 + core

    to_z = 2 * core + lax.rem(x, 2)
    to_e = (y * 4 + lax.div(x, 2) * 2 + lax.div(q, 2)) * 2 + lax.rem(q, 2)
    from_z = lax.rem(x, 2) * 2 + core
    from_e = (y * 4 + lax.div(x, 2) * 2 + lax.rem(q, 2)) * 2 + lax.div(q, 2)
    keeps = jnp.logical_and(to_z == q, to_e == e)
    moves = jnp.logical_not(keeps)

    barrier = pltpu.get_barrier_semaphore()

    def greet(z, peer):
        pl.semaphore_signal(
            barrier, inc=1, device_id=(z, peer), device_id_type=pl.DeviceIdType.MESH
        )

    for d in range(1, n_z):
        greet(lax.rem(q + d, n_z), e)

    def greet_plane(d, _):
        greet(q, lax.rem(e + d, n_e))
        return 0

    lax.fori_loop(1, n_e, greet_plane, 0)

    @pl.when(moves)
    def _():
        greet(from_z, from_e)

    loads = basis_loads(basis_hbm, basis, basis_sem, q)
    for load in loads:
        load.start()
    table[...] = jnp.zeros_like(table)
    table[:, : coef_ref.shape[1]] = coef_ref[...]
    group_row[...] = jnp.zeros_like(group_row)
    group_row[:, : groups_ref.shape[1]] = groups_ref[...]
    place_metadata(
        q, e, src_ref, dst_ref, rel_ref, group_row, counts_ref, meta_ref, feat_ref.shape[0]
    )
    pre_self[...] = dot(feat_ref[...], w_ref[:, lanes])
    pl.semaphore_wait(barrier, n_z - 1 + n_e - 1 + moves.astype(I32))

    def meta_copy(d, slot):
        z = lax.rem(q + d, n_z)
        return remote(meta_ref, meta_z.at[slot], meta_send.at[d], meta_recv.at[slot], z, e)

    def tag_copy(peer, slot):
        return remote(
            meta_all.at[lax.div(peer, 2)],
            tags.at[slot],
            tag_send.at[peer],
            tag_recv.at[slot],
            q,
            peer,
        )

    def feed_copy(peer, slot):
        return remote(
            feed_out.at[peer], feed_in.at[slot], feed_send.at[peer], feed_recv.at[slot], q, peer
        )

    def start_all(copy):
        def go(d, _):
            copy(lax.rem(e + d, n_e), e).start()
            return 0

        lax.fori_loop(1, n_e, go, 0)

    def wait_all(copy):
        def go(d, _):
            peer = lax.rem(e + d, n_e)
            copy(peer, peer).wait_recv()
            return 0

        lax.fori_loop(1, n_e, go, 0)

    def sent_all(copy):
        def go(d, _):
            copy(lax.rem(e + d, n_e), e).wait_send()
            return 0

        lax.fori_loop(1, n_e, go, 0)

    for d in range(1, n_z):
        meta_copy(d, q).start()
    feat_t = feat_ref[:, lanes].T
    meta = meta_ref[...]
    for d in range(1, n_z):
        slot = lax.rem(q + d, n_z)
        meta_copy(d, slot).wait_recv()
        meta += meta_z[slot]
    meta_all[...] = meta
    start_all(tag_copy)
    tags[e] = meta_all[lax.div(e, 2)]
    n_ent = pick.shape[0]
    pairs = n_e // 2
    wide_lanes = meta_ref.shape[3]
    for t in range(pairs):
        line[:, t * wide_lanes : (t + 1) * wide_lanes] = meta_all[t, 0]
    pick_src[...] = one_hot(n_ent, line[...])
    feed = dot(feat_t, pick_src[...])
    feed_out[...] = feed.T.astype(BF).reshape(feed_out.shape)
    start_all(feed_copy)
    feed_in[e] = feed_out[e]
    wait_all(tag_copy)
    left = lax.broadcasted_iota(I32, (1, wide_lanes), 1) < wide_lanes // 2
    for f, out in ((1, line), (2, line_rel)):
        for t in range(pairs):
            even = tags[2 * t, f]
            odd = tags[2 * t + 1, f]
            even = jnp.where(core == 0, even, pltpu.roll(even, wide_lanes // 2, 1))
            odd = jnp.where(core == 0, pltpu.roll(odd, wide_lanes // 2, 1), odd)
            out[:, t * wide_lanes : (t + 1) * wide_lanes] = jnp.where(left, even, odd)
    which = one_hot(table.shape[1], line_rel[...])
    hi, mid, lo = split3(table[...])
    coef_t = dot(jnp.concatenate([hi, mid, lo], axis=0), which)
    coef_t = coef_t[:bases] + coef_t[bases : 2 * bases] + coef_t[2 * bases : 3 * bases]
    for p, b in enumerate(slot_order(bases)):
        coef_t_ref[p : p + 1, :] = coef_t[b : b + 1, :]
    pick[...] = one_hot(n_ent, line[...])
    degree = dot(pick[...], jnp.ones((pick.shape[1], part), BF))
    inv_ref[...] = 1.0 / jnp.maximum(degree, 1.0)
    sums_acc[...] = jnp.zeros_like(sums_acc)
    wait_all(feed_copy)
    rows_t[...] = feed_in[...].reshape(pick.shape[1], part).astype(F32).T
    for load in loads:
        load.wait()
    pair = 8
    chunk = n_ent // 2
    steps = bases // pair

    def forward_half(h, first, last):
        rows = pl.ds(h * chunk, chunk)

        def forward_step(i, _):
            at = i * pair
            mixed = jnp.concatenate(
                [
                    (rows_t[...] * coef_t_ref[pl.ds(at + g, 1), :]).astype(BF)
                    for g in range(pair)
                ],
                axis=0,
            )
            out = dot(pick[rows, :], mixed, ((1,), (1,)))
            weights = basis[pl.ds(at, pair)].reshape(pair * part, width)
            sums_acc[rows, :] += dot(out.astype(BF), weights)
            agg[pl.ds(at, pair), :, rows] = out.T.astype(BF).reshape(pair, part, chunk)
            return 0

        lax.fori_loop(first, last, forward_step, 0)

    agg_copy = remote(
        agg.at[pl.ds((1 - core) * half, half)], agg_sib, agg_send, agg_recv, q, sib
    )

    def sums_copy(d, slot, h):
        z = lax.rem(q + d, n_z)
        at = pl.ds(h * chunk, chunk)
        return remote(
            sums_ref.at[z, at],
            sums_in.at[slot, at],
            sums_send.at[d, h],
            sums_recv.at[slot, h],
            z,
            e,
        )

    def pre_copy(d, slot, h):
        z = lax.rem(q + d, n_z)
        at = pl.ds(h * chunk, chunk)
        return remote(
            pre_in.at[q, at], pre_in.at[slot, at], pre_send.at[d, h], pre_recv.at[slot, h], z, e
        )

    def sib_copy(h):
        at = pl.ds(h * chunk, chunk)
        return remote(
            scaled.at[at], scaled_sib.at[at], sib_send.at[h], sib_recv.at[h], q, sib
        )

    def send_sums(h):
        at = pl.ds(h * chunk, chunk)
        for r in range(n_z):
            sums_ref[r, at] = sums_acc[at, r * part : (r + 1) * part].astype(BF)
        for d in range(1, n_z):
            sums_copy(d, q, h).start()

    def activate(h):
        at = pl.ds(h * chunk, chunk)
        total = sums_ref[q, at].astype(F32)
        for d in range(1, n_z):
            slot = lax.rem(q + d, n_z)
            sums_copy(d, slot, h).wait_recv()
            total += sums_in[slot, at].astype(F32)
        pre = pre_self[at] + total * inv_ref[at]
        sig = jax.nn.sigmoid(pre)
        slope = sig * (1.0 + pre * (1.0 - sig))
        pre_in[q, at] = (cot_ref[at, lanes].astype(F32) * slope).astype(BF)
        for d in range(1, n_z):
            pre_copy(d, q, h).start()
        act_ref[at, lanes] = (pre * sig).astype(BF)

    forward_half(0, 0, steps)
    send_sums(0)
    forward_half(1, 0, steps - 1)
    activate(0)
    forward_half(1, steps - 1, steps)
    send_sums(1)
    agg_copy.start()
    activate(1)

    def act_copy(d, z_in):
        z = lax.rem(q + d, n_z)
        at = pl.ds(pl.multiple_of(z_in * part, part), part)
        return remote(
            act_ref.at[:, lanes], act_ref.at[:, at], act_send.at[d], act_recv.at[z_in], z, e
        )

    for h in range(2):
        at = pl.ds(h * chunk, chunk)
        for d in range(1, n_z):
            pre_copy(d, lax.rem(q + d, n_z), h).wait_recv()
        inverse = inv_ref[at]
        for z in range(n_z):
            part_in = pre_in[z, at].astype(F32) * inverse
            scaled[at, z * part : (z + 1) * part] = part_in.astype(BF)
        sib_copy(h).start()
    w_rows = w_ref[lanes, :]
    grad = dot(pre_in[0], w_rows[:, :part], ((1,), (1,)))
    for z in range(1, n_z):
        grad += dot(pre_in[z], w_rows[:, z * part : (z + 1) * part], ((1,), (1,)))
    group = 4

    def back_step(i, _):
        weights = basis[pl.ds(i * group, group)].reshape(group * part, width)
        back[i] = dot(weights, scaled[...], ((1,), (1,))).astype(BF)
        return 0

    lax.fori_loop(0, bases // group, back_step, 0)

    agg_copy.wait_recv()
    for h in range(2):
        sib_copy(h).wait_recv()
    wide = width // 2

    def x_first(d, slot):
        peer = lax.rem(x + d, 4)
        return remote(
            term_x.at[peer], x_in.at[slot], x_send.at[d], x_recv.at[slot], q, at_chip(y, peer)
        )

    def y_first(d, slot):
        peer = lax.rem(y + d, 4)
        return remote(
            term_y.at[peer], y_in.at[slot], y_send.at[d], y_recv.at[slot], q, at_chip(peer, x)
        )

    def x_then_y(d, slot):
        peer = lax.rem(y + d, 4)
        return remote(
            half_x.at[peer], xy_in.at[slot], xy_send.at[d], xy_recv.at[slot], q, at_chip(peer, x)
        )

    def y_then_x(d, slot):
        peer = lax.rem(x + d, 4)
        return remote(
            half_y.at[peer], yx_in.at[slot], yx_send.at[d], yx_recv.at[slot], q, at_chip(y, peer)
        )

    for d in (2, 1, 3, 0):
        at = lax.rem(x + d, 4)
        own = agg[pl.ds(core * half + at * group, group)].reshape(group * part, n_ent)
        other = agg_sib[pl.ds(at * group, group)].reshape(group * part, n_ent)
        terms = dot(own, scaled[...]) + dot(other, scaled_sib[...])
        terms = terms.astype(BF)
        term_x[at] = terms[:, :wide].reshape(group, part, wide)
        for g in range(group):
            term_y[g, at] = terms[g * part : (g + 1) * part, wide:]
        if d:
            x_first(d, x).start()
    for d in (2, 1, 3):
        y_first(d, y).start()
    for d in range(1, n_z):
        act_copy(d, q).start()
    seg = acc.shape[1]

    def spread(first):
        acc[...] = jnp.zeros_like(acc)

        def step(i, _):
            out = dot(back[i], pick[:, first : first + seg])
            rows = acc[...]
            for g in range(group):
                coef = coef_t_ref[pl.ds(i * group + g, 1), first : first + seg]
                rows += out[g * part : (g + 1) * part] * coef
            acc[...] = rows
            return 0

        lax.fori_loop(0, bases // group, step, 0)
        block = row_out.shape[1]
        rows = acc[...].T.astype(BF).reshape(seg // block, block, part)
        row_out[first // block : (first + seg) // block] = rows

    def row_copy(peer, slot):
        return remote(
            row_out.at[peer], row_in.at[slot], row_send.at[peer], row_recv.at[slot], q, peer
        )

    def row_start(peer, _):
        @pl.when(peer != e)
        def _():
            row_copy(peer, e).start()

        return 0

    per_seg = n_e * seg // pick.shape[1]
    for n in range(n_e // per_seg):
        spread(n * seg)
        lax.fori_loop(n * per_seg, (n + 1) * per_seg, row_start, 0)
    row_in[e] = row_out[e]

    def add_up(own, arrived, recv, me):
        total = own.astype(F32)
        for d in (1, 3, 2):
            slot = lax.rem(me + d, 4)
            recv(d, slot).wait_recv()
            total += arrived[slot].astype(F32)
        return total

    half_x[...] = add_up(term_x[x], x_in, x_first, x).astype(BF)
    for d in (2, 1, 3):
        x_then_y(d, y).start()
    half_y[...] = add_up(term_y[y], y_in, y_first, y).astype(BF)
    for d in (2, 1, 3):
        y_then_x(d, x).start()
    wait_all(row_copy)
    grad += dot(pick_src[...], row_in[...].reshape(pick_src.shape[1], part))
    gf_ref[:, lanes] = grad.astype(BF)

    def gf_copy(d, z_in):
        z = lax.rem(q + d, n_z)
        at = pl.ds(pl.multiple_of(z_in * part, part), part)
        return remote(
            gf_ref.at[:, lanes], gf_ref.at[:, at], gf_send.at[d], gf_recv.at[z_in], z, e
        )

    for d in range(1, n_z):
        gf_copy(d, q).start()

    done[:, :wide] = add_up(half_x[y], xy_in, x_then_y, y).astype(BF)
    done[:, wide:] = add_up(half_y[x], yx_in, y_then_x, x).astype(BF)
    move = remote(done, done_in, move_send, move_recv, to_z, to_e)

    @pl.when(keeps)
    def _():
        done_in[...] = done[...]

    @pl.when(moves)
    def _():
        move.start()
        move.wait_send()
        remote(done, done_in, move_send, move_recv, from_z, from_e).wait_recv()

    gb_ref[...] = done_in[...].astype(F32)

    for d in range(1, n_z):
        z = lax.rem(q + d, n_z)
        act_copy(d, z).wait_recv()
        gf_copy(d, z).wait_recv()
        for h in range(2):
            sums_copy(d, q, h).wait_send()
            pre_copy(d, q, h).wait_send()
        act_copy(d, q).wait_send()
        gf_copy(d, q).wait_send()
    agg_copy.wait_send()
    for h in range(2):
        sib_copy(h).wait_send()

    for d in (1, 2, 3):
        x_first(d, x).wait_send()
        y_first(d, y).wait_send()
        x_then_y(d, y).wait_send()
        y_then_x(d, x).wait_send()

    for d in range(1, n_z):
        meta_copy(d, q).wait_send()
    sent_all(tag_copy)
    sent_all(feed_copy)
    sent_all(row_copy)


def run_step(src, dst, rel, groups, counts, features, w_self, cotangent, coeffs, basis_mats):
    n_z = lax.axis_size("rel")
    n_e = lax.axis_size("ent")
    n_ent, width = features.shape
    bases = coeffs.shape[0]
    all_slots = src.shape[1] * n_z
    part = width // n_z
    half = bases // 2
    block = all_slots // n_e
    vm = pl.BlockSpec(memory_space=pltpu.VMEM)
    dma = pltpu.SemaphoreType.DMA
    return pl.pallas_call(
        functools.partial(step_kernel, n_z, n_e),
        out_shape=(
            jax.ShapeDtypeStruct((n_ent, width), BF),
            jax.ShapeDtypeStruct((n_ent, width), BF),
            jax.ShapeDtypeStruct((part, width), F32),
        ),
        in_specs=[vm] * 9 + [pl.BlockSpec(memory_space=pl.ANY)],
        out_specs=(vm, vm, vm),
        scratch_shapes=[
            pltpu.VMEM((1, 256), I32),
            pltpu.VMEM((n_e // 2, 3, 1, 128), I32),
            pltpu.VMEM((n_z, n_e // 2, 3, 1, 128), I32),
            pltpu.VMEM((n_e // 2, 3, 1, 128), I32),
            pltpu.VMEM((n_e, 3, 1, 128), I32),
            pltpu.VMEM((1, all_slots), I32),
            pltpu.VMEM((1, all_slots), I32),
            pltpu.VMEM((bases, 1024), F32),
            pltpu.VMEM((n_e, block, part), BF),
            pltpu.VMEM((n_e, block, part), BF),
            pltpu.VMEM((part, all_slots), F32),
            pltpu.VMEM((bases, all_slots), F32),
            pltpu.VMEM((n_ent, part), F32),
            pltpu.VMEM((n_ent, part), F32),
            pltpu.VMEM((n_ent, width), F32),
            pltpu.VMEM((n_z, n_ent, part), BF),
            pltpu.VMEM((bases, part, n_ent), BF),
            pltpu.VMEM((n_z, n_ent, part), BF),
            pltpu.VMEM((n_z, n_ent, part), BF),
            pltpu.VMEM((n_ent, width), BF),
            pltpu.VMEM((n_ent, width), BF),
            pltpu.VMEM((half, part, n_ent), BF),
            pltpu.VMEM((bases, part, width), BF),
            pltpu.VMEM((n_ent, all_slots), BF),
            pltpu.VMEM((n_ent, all_slots), BF),
            pltpu.VMEM((part, all_slots // 2), F32),
            pltpu.VMEM((bases // 4, 4 * part, n_ent), BF),
            pltpu.VMEM((4, 4, part, width // 2), BF),
            pltpu.VMEM((4, 4, part, width // 2), BF),
            pltpu.VMEM((4, 4, part, width // 2), BF),
            pltpu.VMEM((4, 4, part, width // 2), BF),
            pltpu.VMEM((4, part, width // 2), BF),
            pltpu.VMEM((4, part, width // 2), BF),
            pltpu.VMEM((4, part, width // 2), BF),
            pltpu.VMEM((4, part, width // 2), BF),
            pltpu.VMEM((part, width), BF),
            pltpu.VMEM((part, width), BF),
            pltpu.VMEM((n_e, block, part), BF),
            pltpu.VMEM((n_e, block, part), BF),
            dma((bases // 4,)),
            dma((n_z, 2)),
            dma((n_z, 2)),
            dma((n_z,)),
            dma((n_z,)),
            dma((n_z, 2)),
            dma((n_z, 2)),
            dma,
            dma,
            dma((2,)),
            dma((2,)),
            dma((4,)),
            dma((4,)),
            dma((4,)),
            dma((4,)),
            dma((4,)),
            dma((4,)),
            dma((4,)),
            dma((4,)),
            dma,
            dma,
            dma((n_e,)),
            dma((n_e,)),
            dma((n_z,)),
            dma((n_z,)),
            dma((n_z,)),
            dma((n_z,)),
            dma((n_e,)),
            dma((n_e,)),
            dma((n_e,)),
            dma((n_e,)),
        ],
        compiler_params=pltpu.CompilerParams(
            vmem_limit_bytes=56 * MIB, collective_id=0, has_side_effects=True
        ),
    )(
        src,
        dst,
        rel,
        groups,
        counts,
        features,
        w_self,
        cotangent,
        coeffs,
        basis_mats.reshape(2, 2, 4, 2, width, width),
    )


def store_kernel(a_in, b_in, c_in, a_out, b_out, c_out, sems):
    copies = [
        pltpu.make_async_copy(i, o, sems.at[n])
        for n, (i, o) in enumerate(((a_in, a_out), (b_in, b_out), (c_in, c_out)))
    ]
    for copy in copies:
        copy.start()
    for copy in copies:
        copy.wait()


def store(arrays):
    hbm = pl.BlockSpec(memory_space=pl.ANY)
    return pl.pallas_call(
        store_kernel,
        out_shape=tuple(jax.ShapeDtypeStruct(a.shape, a.dtype) for a in arrays),
        in_specs=[pl.BlockSpec(memory_space=pltpu.VMEM)] * 3,
        out_specs=(hbm,) * 3,
        scratch_shapes=[pltpu.SemaphoreType.DMA((3,))],
    )(*arrays)


def per_device(
    features,
    w_self,
    basis_mats,
    basis_coeffs,
    group_rels,
    rel_local,
    edge_src,
    edge_dst,
    block_counts,
    cotangent,
):
    outs = run_step(
        edge_src[None],
        edge_dst[None],
        rel_local[None],
        group_rels[None],
        block_counts[0],
        features,
        w_self,
        cotangent,
        basis_coeffs.T,
        basis_mats,
    )
    return store(outs)


def solution(mesh):
    placed = (
        P("ent", None),
        P(),
        P(),
        P(),
        P("rel"),
        P(("rel", "ent")),
        P(("rel", "ent")),
        P(("rel", "ent")),
        P("rel", "ent", None),
        P("ent", None),
    )
    return jax.shard_map(
        per_device,
        mesh=mesh,
        in_specs=placed,
        out_specs=(P("ent", None), P("ent", None), P(("rel", "ent"), None)),
        check_vma=False,
    )
```

```python
import functools

import jax
import jax.numpy as jnp
from jax import lax
from jax.experimental import pallas as pl
from jax.experimental.pallas import tpu as pltpu
from jax.sharding import PartitionSpec as P

BF = jnp.bfloat16
F32 = jnp.float32
I32 = jnp.int32
MIB = 1 << 20


def dot(a, b, dims=((1,), (0,))):
    return lax.dot_general(a, b, (dims, ((), ())), preferred_element_type=F32)


def one_hot(count, row):
    ids = lax.broadcasted_iota(I32, (count, row.shape[1]), 0)
    return (ids == row).astype(F32).astype(BF)


def split3(x):
    hi = x.astype(BF)
    rest = x - hi.astype(F32)
    mid = rest.astype(BF)
    lo = (rest - mid.astype(F32)).astype(BF)
    return hi, mid, lo


def slot_order(bases):
    half = bases // 2
    return [
        c * half + (x % 2) * 8 + y * 2 + x // 2
        for c in range(2)
        for x in range(4)
        for y in range(half // 4)
    ]


def basis_loads(basis_hbm, basis, sems, q):
    part = basis.shape[1]
    lanes = pl.ds(pl.multiple_of(q * part, part), part)
    loads = []
    for c in range(2):
        for x in range(4):
            at = c * 4 + x
            loads.append(
                pltpu.make_async_copy(
                    basis_hbm.at[c, x % 2, :, x // 2, lanes, :],
                    basis.at[pl.ds(at * 4, 4)],
                    sems.at[at],
                )
            )
    return loads


def remote(src, dst, send_sem, recv_sem, z, e):
    return pltpu.make_async_remote_copy(
        src_ref=src,
        dst_ref=dst,
        send_sem=send_sem,
        recv_sem=recv_sem,
        device_id=(z, e),
        device_id_type=pl.DeviceIdType.MESH,
    )


def place_metadata(q, e, src_ref, dst_ref, rel_ref, group_row, counts_ref, meta_ref, n_ent):
    slots = src_ref.shape[1]
    n_e = counts_ref.shape[1]
    pairs, fields, _, lanes = meta_ref.shape
    cap = slots // n_e
    spot = lax.broadcasted_iota(I32, (1, slots), 1)
    peer = lax.div(spot, cap)
    rows16 = lax.broadcasted_iota(I32, (pairs, slots), 0)

    def digits(v):
        return lax.div(v, 32).astype(F32), lax.rem(v, 32).astype(F32)

    hi, lo = digits(group_row[...])
    level = lax.broadcasted_iota(I32, (pairs, group_row.shape[1]), 0)
    table = jnp.where(level == 0, hi, jnp.where(level == 1, lo, 0.0)).astype(BF)
    rel_digits = dot(table, one_hot(group_row.shape[1], rel_ref[...]))
    counts = jnp.broadcast_to(counts_ref[...].astype(F32), (pairs, n_e)).astype(BF)
    limit = dot(counts, one_hot(n_e, peer))[:1]
    live = lax.rem(spot, cap).astype(F32) < limit
    dst = jnp.where(live, dst_ref[...] - peer * n_ent, n_ent)
    values = digits(src_ref[...] - e * n_ent) + digits(dst)
    values = values + (rel_digits[:1], rel_digits[1:2])
    here = rows16 == lax.div(peer, 2)
    stacked = jnp.concatenate([jnp.where(here, v, 0.0) for v in values], axis=0).astype(BF)
    index = lax.broadcasted_iota(I32, (slots, lanes), 0)
    lane = lax.broadcasted_iota(I32, (slots, lanes), 1)
    half = lax.rem(lax.div(index, cap), 2)
    target = half * (lanes // 2) + q * cap + lax.rem(index, cap)
    moved = dot(stacked, (target == lane).astype(F32).astype(BF))
    for f in range(fields):
        hi = moved[2 * f * pairs : (2 * f + 1) * pairs]
        lo = moved[(2 * f + 1) * pairs : (2 * f + 2) * pairs]
        field = (hi * 32.0 + lo + 0.5).astype(I32)
        for t in range(pairs):
            meta_ref[t, f] = field[t : t + 1, :]


def step_kernel(
    n_z,
    n_e,
    src_ref,
    dst_ref,
    rel_ref,
    groups_ref,
    counts_ref,
    feat_ref,
    w_ref,
    cot_ref,
    coef_ref,
    basis_hbm,
    act_ref,
    gf_ref,
    gb_ref,
    group_row,
    meta_ref,
    meta_z,
    meta_all,
    tags,
    line,
    line_rel,
    table,
    feed_out,
    feed_in,
    rows_t,
    coef_t_ref,
    inv_ref,
    pre_self,
    sums_acc,
    sums_ref,
    agg,
    sums_in,
    pre_in,
    scaled,
    scaled_sib,
    agg_sib,
    basis,
    pick,
    pick_src,
    acc,
    back,
    term_x,
    term_y,
    x_in,
    y_in,
    half_x,
    half_y,
    xy_in,
    yx_in,
    done,
    done_in,
    row_out,
    row_in,
    basis_sem,
    sums_send,
    sums_recv,
    act_send,
    act_recv,
    pre_send,
    pre_recv,
    agg_send,
    agg_recv,
    sib_send,
    sib_recv,
    x_send,
    x_recv,
    y_send,
    y_recv,
    xy_send,
    xy_recv,
    yx_send,
    yx_recv,
    move_send,
    move_recv,
    row_send,
    row_recv,
    gf_send,
    gf_recv,
    meta_send,
    meta_recv,
    tag_send,
    tag_recv,
    feed_send,
    feed_recv,
):
    q = lax.axis_index("rel")
    e = lax.axis_index("ent")
    core = lax.rem(e, 2)
    chip = lax.div(e, 2)
    sib = e + 1 - 2 * core
    bases, part, width = basis.shape
    half = bases // 2
    lanes = pl.ds(pl.multiple_of(q * part, part), part)
    x = lax.rem(chip, 4)
    y = lax.div(chip, 4)

    def at_chip(y_at, x_at):
        return (y_at * 4 + x_at) * 2 + core

    to_z = 2 * core + lax.rem(x, 2)
    to_e = (y * 4 + lax.div(x, 2) * 2 + lax.div(q, 2)) * 2 + lax.rem(q, 2)
    from_z = lax.rem(x, 2) * 2 + core
    from_e = (y * 4 + lax.div(x, 2) * 2 + lax.rem(q, 2)) * 2 + lax.div(q, 2)
    keeps = jnp.logical_and(to_z == q, to_e == e)
    moves = jnp.logical_not(keeps)

    barrier = pltpu.get_barrier_semaphore()

    def greet(z, peer):
        pl.semaphore_signal(
            barrier, inc=1, device_id=(z, peer), device_id_type=pl.DeviceIdType.MESH
        )

    for d in range(1, n_z):
        greet(lax.rem(q + d, n_z), e)

    def greet_plane(d, _):
        greet(q, lax.rem(e + d, n_e))
        return 0

    lax.fori_loop(1, n_e, greet_plane, 0)

    @pl.when(moves)
    def _():
        greet(from_z, from_e)

    loads = basis_loads(basis_hbm, basis, basis_sem, q)
    for load in loads:
        load.start()
    table[...] = jnp.zeros_like(table)
    table[:, : coef_ref.shape[1]] = coef_ref[...]
    group_row[...] = jnp.zeros_like(group_row)
    group_row[:, : groups_ref.shape[1]] = groups_ref[...]
    place_metadata(
        q, e, src_ref, dst_ref, rel_ref, group_row, counts_ref, meta_ref, feat_ref.shape[0]
    )
    pre_self[...] = dot(feat_ref[...], w_ref[:, lanes])
    pl.semaphore_wait(barrier, n_z - 1 + n_e - 1 + moves.astype(I32))

    def meta_copy(d, slot):
        z = lax.rem(q + d, n_z)
        return remote(meta_ref, meta_z.at[slot], meta_send.at[d], meta_recv.at[slot], z, e)

    def tag_copy(peer, slot):
        return remote(
            meta_all.at[lax.div(peer, 2)],
            tags.at[slot],
            tag_send.at[peer],
            tag_recv.at[slot],
            q,
            peer,
        )

    def feed_copy(peer, slot):
        return remote(
            feed_out.at[peer], feed_in.at[slot], feed_send.at[peer], feed_recv.at[slot], q, peer
        )

    def start_all(copy):
        def go(d, _):
            copy(lax.rem(e + d, n_e), e).start()
            return 0

        lax.fori_loop(1, n_e, go, 0)

    def wait_all(copy):
        def go(d, _):
            peer = lax.rem(e + d, n_e)
            copy(peer, peer).wait_recv()
            return 0

        lax.fori_loop(1, n_e, go, 0)

    def sent_all(copy):
        def go(d, _):
            copy(lax.rem(e + d, n_e), e).wait_send()
            return 0

        lax.fori_loop(1, n_e, go, 0)

    for d in range(1, n_z):
        meta_copy(d, q).start()
    feat_t = feat_ref[:, lanes].T
    meta = meta_ref[...]
    for d in range(1, n_z):
        slot = lax.rem(q + d, n_z)
        meta_copy(d, slot).wait_recv()
        meta += meta_z[slot]
    meta_all[...] = meta
    start_all(tag_copy)
    tags[e] = meta_all[lax.div(e, 2)]
    n_ent = pick.shape[0]
    pairs = n_e // 2
    wide_lanes = meta_ref.shape[3]
    for t in range(pairs):
        line[:, t * wide_lanes : (t + 1) * wide_lanes] = meta_all[t, 0]
    pick_src[...] = one_hot(n_ent, line[...])
    feed = dot(feat_t, pick_src[...])
    feed_out[...] = feed.T.astype(BF).reshape(feed_out.shape)
    start_all(feed_copy)
    feed_in[e] = feed_out[e]
    wait_all(tag_copy)
    left = lax.broadcasted_iota(I32, (1, wide_lanes), 1) < wide_lanes // 2
    for f, out in ((1, line), (2, line_rel)):
        for t in range(pairs):
            even = tags[2 * t, f]
            odd = tags[2 * t + 1, f]
            even = jnp.where(core == 0, even, pltpu.roll(even, wide_lanes // 2, 1))
            odd = jnp.where(core == 0, pltpu.roll(odd, wide_lanes // 2, 1), odd)
            out[:, t * wide_lanes : (t + 1) * wide_lanes] = jnp.where(left, even, odd)
    which = one_hot(table.shape[1], line_rel[...])
    hi, mid, lo = split3(table[...])
    coef_t = dot(jnp.concatenate([hi, mid, lo], axis=0), which)
    coef_t = coef_t[:bases] + coef_t[bases : 2 * bases] + coef_t[2 * bases : 3 * bases]
    for p, b in enumerate(slot_order(bases)):
        coef_t_ref[p : p + 1, :] = coef_t[b : b + 1, :]
    pick[...] = one_hot(n_ent, line[...])
    degree = dot(pick[...], jnp.ones((pick.shape[1], part), BF))
    inv_ref[...] = 1.0 / jnp.maximum(degree, 1.0)
    sums_acc[...] = jnp.zeros_like(sums_acc)
    wait_all(feed_copy)
    rows_t[...] = feed_in[...].reshape(pick.shape[1], part).astype(F32).T
    for load in loads:
        load.wait()
    pair = 8
    chunk = n_ent // 2
    steps = bases // pair

    def forward_half(h, first, last):
        rows = pl.ds(h * chunk, chunk)

        def forward_step(i, _):
            at = i * pair
            mixed = jnp.concatenate(
                [
                    (rows_t[...] * coef_t_ref[pl.ds(at + g, 1), :]).astype(BF)
                    for g in range(pair)
                ],
                axis=0,
            )
            out = dot(pick[rows, :], mixed, ((1,), (1,)))
            weights = basis[pl.ds(at, pair)].reshape(pair * part, width)
            sums_acc[rows, :] += dot(out.astype(BF), weights)
            agg[pl.ds(at, pair), :, rows] = out.T.astype(BF).reshape(pair, part, chunk)
            return 0

        lax.fori_loop(first, last, forward_step, 0)

    agg_copy = remote(
        agg.at[pl.ds((1 - core) * half, half)], agg_sib, agg_send, agg_recv, q, sib
    )

    def sums_copy(d, slot, h):
        z = lax.rem(q + d, n_z)
        at = pl.ds(h * chunk, chunk)
        return remote(
            sums_ref.at[z, at],
            sums_in.at[slot, at],
            sums_send.at[d, h],
            sums_recv.at[slot, h],
            z,
            e,
        )

    def pre_copy(d, slot, h):
        z = lax.rem(q + d, n_z)
        at = pl.ds(h * chunk, chunk)
        return remote(
            pre_in.at[q, at], pre_in.at[slot, at], pre_send.at[d, h], pre_recv.at[slot, h], z, e
        )

    def sib_copy(h):
        at = pl.ds(h * chunk, chunk)
        return remote(
            scaled.at[at], scaled_sib.at[at], sib_send.at[h], sib_recv.at[h], q, sib
        )

    def send_sums(h):
        at = pl.ds(h * chunk, chunk)
        for r in range(n_z):
            sums_ref[r, at] = sums_acc[at, r * part : (r + 1) * part].astype(BF)
        for d in range(1, n_z):
            sums_copy(d, q, h).start()

    def activate(h):
        at = pl.ds(h * chunk, chunk)
        total = sums_ref[q, at].astype(F32)
        for d in range(1, n_z):
            slot = lax.rem(q + d, n_z)
            sums_copy(d, slot, h).wait_recv()
            total += sums_in[slot, at].astype(F32)
        pre = pre_self[at] + total * inv_ref[at]
        sig = jax.nn.sigmoid(pre)
        slope = sig * (1.0 + pre * (1.0 - sig))
        pre_in[q, at] = (cot_ref[at, lanes].astype(F32) * slope).astype(BF)
        for d in range(1, n_z):
            pre_copy(d, q, h).start()
        act_ref[at, lanes] = (pre * sig).astype(BF)

    forward_half(0, 0, steps)
    send_sums(0)
    forward_half(1, 0, steps - 1)
    activate(0)
    forward_half(1, steps - 1, steps)
    send_sums(1)
    agg_copy.start()
    activate(1)

    def act_copy(d, z_in):
        z = lax.rem(q + d, n_z)
        at = pl.ds(pl.multiple_of(z_in * part, part), part)
        return remote(
            act_ref.at[:, lanes], act_ref.at[:, at], act_send.at[d], act_recv.at[z_in], z, e
        )

    for h in range(2):
        at = pl.ds(h * chunk, chunk)
        for d in range(1, n_z):
            pre_copy(d, lax.rem(q + d, n_z), h).wait_recv()
        inverse = inv_ref[at]
        for z in range(n_z):
            part_in = pre_in[z, at].astype(F32) * inverse
            scaled[at, z * part : (z + 1) * part] = part_in.astype(BF)
        sib_copy(h).start()
    w_rows = w_ref[lanes, :]
    grad = dot(pre_in[0], w_rows[:, :part], ((1,), (1,)))
    for z in range(1, n_z):
        grad += dot(pre_in[z], w_rows[:, z * part : (z + 1) * part], ((1,), (1,)))
    group = 4

    def back_step(i, _):
        weights = basis[pl.ds(i * group, group)].reshape(group * part, width)
        back[i] = dot(weights, scaled[...], ((1,), (1,))).astype(BF)
        return 0

    lax.fori_loop(0, bases // group, back_step, 0)

    agg_copy.wait_recv()
    for h in range(2):
        sib_copy(h).wait_recv()
    wide = width // 2

    def x_first(d, slot):
        peer = lax.rem(x + d, 4)
        return remote(
            term_x.at[peer], x_in.at[slot], x_send.at[d], x_recv.at[slot], q, at_chip(y, peer)
        )

    def y_first(d, slot):
        peer = lax.rem(y + d, 4)
        return remote(
            term_y.at[peer], y_in.at[slot], y_send.at[d], y_recv.at[slot], q, at_chip(peer, x)
        )

    def x_then_y(d, slot):
        peer = lax.rem(y + d, 4)
        return remote(
            half_x.at[peer], xy_in.at[slot], xy_send.at[d], xy_recv.at[slot], q, at_chip(peer, x)
        )

    def y_then_x(d, slot):
        peer = lax.rem(x + d, 4)
        return remote(
            half_y.at[peer], yx_in.at[slot], yx_send.at[d], yx_recv.at[slot], q, at_chip(y, peer)
        )

    for d in (2, 1, 3, 0):
        at = lax.rem(x + d, 4)
        own = agg[pl.ds(core * half + at * group, group)].reshape(group * part, n_ent)
        other = agg_sib[pl.ds(at * group, group)].reshape(group * part, n_ent)
        terms = dot(own, scaled[...]) + dot(other, scaled_sib[...])
        terms = terms.astype(BF)
        term_x[at] = terms[:, :wide].reshape(group, part, wide)
        for g in range(group):
            term_y[g, at] = terms[g * part : (g + 1) * part, wide:]
        if d:
            x_first(d, x).start()
    for d in (2, 1, 3):
        y_first(d, y).start()
    for d in range(1, n_z):
        act_copy(d, q).start()
    seg = acc.shape[1]

    def spread(n):
        at = pl.ds(pl.multiple_of(n * seg, seg), seg)
        acc[...] = jnp.zeros_like(acc)

        def step(i, _):
            out = dot(back[i], pick[:, at])
            rows = acc[...]
            for g in range(group):
                rows += out[g * part : (g + 1) * part] * coef_t_ref[pl.ds(i * group + g, 1), at]
            acc[...] = rows
            return 0

        lax.fori_loop(0, bases // group, step, 0)
        block = row_out.shape[1]
        rows = acc[...].T.astype(BF).reshape(seg // block, block, part)
        row_out[pl.ds(n * (seg // block), seg // block)] = rows

    def row_copy(peer, slot):
        return remote(
            row_out.at[peer], row_in.at[slot], row_send.at[peer], row_recv.at[slot], q, peer
        )

    def row_start(peer, _):
        @pl.when(peer != e)
        def _():
            row_copy(peer, e).start()

        return 0

    per_seg = n_e * seg // pick.shape[1]
    for d in (2, 1, 3, 0):
        n = lax.rem(y + d, n_e // per_seg)
        spread(n)
        lax.fori_loop(n * per_seg, (n + 1) * per_seg, row_start, 0)
    row_in[e] = row_out[e]

    def add_up(own, arrived, recv, me):
        total = own.astype(F32)
        for d in (1, 3, 2):
            slot = lax.rem(me + d, 4)
            recv(d, slot).wait_recv()
            total += arrived[slot].astype(F32)
        return total

    half_x[...] = add_up(term_x[x], x_in, x_first, x).astype(BF)
    for d in (2, 1, 3):
        x_then_y(d, y).start()
    half_y[...] = add_up(term_y[y], y_in, y_first, y).astype(BF)
    for d in (2, 1, 3):
        y_then_x(d, x).start()
    wait_all(row_copy)
    grad += dot(pick_src[...], row_in[...].reshape(pick_src.shape[1], part))
    gf_ref[:, lanes] = grad.astype(BF)

    def gf_copy(d, z_in):
        z = lax.rem(q + d, n_z)
        at = pl.ds(pl.multiple_of(z_in * part, part), part)
        return remote(
            gf_ref.at[:, lanes], gf_ref.at[:, at], gf_send.at[d], gf_recv.at[z_in], z, e
        )

    for d in range(1, n_z):
        gf_copy(d, q).start()
    done[:, :wide] = add_up(half_x[y], xy_in, x_then_y, y).astype(BF)
    done[:, wide:] = add_up(half_y[x], yx_in, y_then_x, x).astype(BF)
    move = remote(done, done_in, move_send, move_recv, to_z, to_e)

    @pl.when(keeps)
    def _():
        done_in[...] = done[...]

    @pl.when(moves)
    def _():
        move.start()

    for d in range(1, n_z):
        z = lax.rem(q + d, n_z)
        act_copy(d, z).wait_recv()
        act_copy(d, q).wait_send()
        meta_copy(d, q).wait_send()
        for h in range(2):
            sums_copy(d, q, h).wait_send()
            pre_copy(d, q, h).wait_send()
    agg_copy.wait_send()
    for h in range(2):
        sib_copy(h).wait_send()
    for d in (1, 2, 3):
        x_first(d, x).wait_send()
        y_first(d, y).wait_send()
        x_then_y(d, y).wait_send()
        y_then_x(d, x).wait_send()
    sent_all(tag_copy)
    sent_all(feed_copy)
    sent_all(row_copy)

    @pl.when(moves)
    def _():
        move.wait_send()
        remote(done, done_in, move_send, move_recv, from_z, from_e).wait_recv()

    gb_ref[...] = done_in[...].astype(F32)

    for d in range(1, n_z):
        z = lax.rem(q + d, n_z)
        gf_copy(d, z).wait_recv()
        gf_copy(d, q).wait_send()


def run_step(src, dst, rel, groups, counts, features, w_self, cotangent, coeffs, basis_mats):
    n_z = lax.axis_size("rel")
    n_e = lax.axis_size("ent")
    n_ent, width = features.shape
    bases = coeffs.shape[0]
    all_slots = src.shape[1] * n_z
    part = width // n_z
    half = bases // 2
    block = all_slots // n_e
    vm = pl.BlockSpec(memory_space=pltpu.VMEM)
    dma = pltpu.SemaphoreType.DMA
    return pl.pallas_call(
        functools.partial(step_kernel, n_z, n_e),
        out_shape=(
            jax.ShapeDtypeStruct((n_ent, width), BF),
            jax.ShapeDtypeStruct((n_ent, width), BF),
            jax.ShapeDtypeStruct((part, width), F32),
        ),
        in_specs=[vm] * 9 + [pl.BlockSpec(memory_space=pl.ANY)],
        out_specs=(vm, vm, vm),
        scratch_shapes=[
            pltpu.VMEM((1, 256), I32),
            pltpu.VMEM((n_e // 2, 3, 1, 128), I32),
            pltpu.VMEM((n_z, n_e // 2, 3, 1, 128), I32),
            pltpu.VMEM((n_e // 2, 3, 1, 128), I32),
            pltpu.VMEM((n_e, 3, 1, 128), I32),
            pltpu.VMEM((1, all_slots), I32),
            pltpu.VMEM((1, all_slots), I32),
            pltpu.VMEM((bases, 1024), F32),
            pltpu.VMEM((n_e, block, part), BF),
            pltpu.VMEM((n_e, block, part), BF),
            pltpu.VMEM((part, all_slots), F32),
            pltpu.VMEM((bases, all_slots), F32),
            pltpu.VMEM((n_ent, part), F32),
            pltpu.VMEM((n_ent, part), F32),
            pltpu.VMEM((n_ent, width), F32),
            pltpu.VMEM((n_z, n_ent, part), BF),
            pltpu.VMEM((bases, part, n_ent), BF),
            pltpu.VMEM((n_z, n_ent, part), BF),
            pltpu.VMEM((n_z, n_ent, part), BF),
            pltpu.VMEM((n_ent, width), BF),
            pltpu.VMEM((n_ent, width), BF),
            pltpu.VMEM((half, part, n_ent), BF),
            pltpu.VMEM((bases, part, width), BF),
            pltpu.VMEM((n_ent, all_slots), BF),
            pltpu.VMEM((n_ent, all_slots), BF),
            pltpu.VMEM((part, all_slots // 4), F32),
            pltpu.VMEM((bases // 4, 4 * part, n_ent), BF),
            pltpu.VMEM((4, 4, part, width // 2), BF),
            pltpu.VMEM((4, 4, part, width // 2), BF),
            pltpu.VMEM((4, 4, part, width // 2), BF),
            pltpu.VMEM((4, 4, part, width // 2), BF),
            pltpu.VMEM((4, part, width // 2), BF),
            pltpu.VMEM((4, part, width // 2), BF),
            pltpu.VMEM((4, part, width // 2), BF),
            pltpu.VMEM((4, part, width // 2), BF),
            pltpu.VMEM((part, width), BF),
            pltpu.VMEM((part, width), BF),
            pltpu.VMEM((n_e, block, part), BF),
            pltpu.VMEM((n_e, block, part), BF),
            dma((bases // 4,)),
            dma((n_z, 2)),
            dma((n_z, 2)),
            dma((n_z,)),
            dma((n_z,)),
            dma((n_z, 2)),
            dma((n_z, 2)),
            dma,
            dma,
            dma((2,)),
            dma((2,)),
            dma((4,)),
            dma((4,)),
            dma((4,)),
            dma((4,)),
            dma((4,)),
            dma((4,)),
            dma((4,)),
            dma((4,)),
            dma,
            dma,
            dma((n_e,)),
            dma((n_e,)),
            dma((n_z,)),
            dma((n_z,)),
            dma((n_z,)),
            dma((n_z,)),
            dma((n_e,)),
            dma((n_e,)),
            dma((n_e,)),
            dma((n_e,)),
        ],
        compiler_params=pltpu.CompilerParams(
            vmem_limit_bytes=56 * MIB, collective_id=0, has_side_effects=True
        ),
    )(
        src,
        dst,
        rel,
        groups,
        counts,
        features,
        w_self,
        cotangent,
        coeffs,
        basis_mats.reshape(2, 2, 4, 2, width, width),
    )


def store_kernel(a_in, b_in, c_in, a_out, b_out, c_out, sems):
    copies = [
        pltpu.make_async_copy(i, o, sems.at[n])
        for n, (i, o) in enumerate(((a_in, a_out), (b_in, b_out), (c_in, c_out)))
    ]
    for copy in copies:
        copy.start()
    for copy in copies:
        copy.wait()


def store(arrays):
    hbm = pl.BlockSpec(memory_space=pl.ANY)
    return pl.pallas_call(
        store_kernel,
        out_shape=tuple(jax.ShapeDtypeStruct(a.shape, a.dtype) for a in arrays),
        in_specs=[pl.BlockSpec(memory_space=pltpu.VMEM)] * 3,
        out_specs=(hbm,) * 3,
        scratch_shapes=[pltpu.SemaphoreType.DMA((3,))],
    )(*arrays)


def per_device(
    features,
    w_self,
    basis_mats,
    basis_coeffs,
    group_rels,
    rel_local,
    edge_src,
    edge_dst,
    block_counts,
    cotangent,
):
    outs = run_step(
        edge_src[None],
        edge_dst[None],
        rel_local[None],
        group_rels[None],
        block_counts[0],
        features,
        w_self,
        cotangent,
        basis_coeffs.T,
        basis_mats,
    )
    return store(outs)


def solution(mesh):
    placed = (
        P("ent", None),
        P(),
        P(),
        P(),
        P("rel"),
        P(("rel", "ent")),
        P(("rel", "ent")),
        P(("rel", "ent")),
        P("rel", "ent", None),
        P("ent", None),
    )
    return jax.shard_map(
        per_device,
        mesh=mesh,
        in_specs=placed,
        out_specs=(P("ent", None), P("ent", None), P(("rel", "ent"), None)),
        check_vma=False,
    )
```

```python
import functools

import jax
import jax.numpy as jnp
from jax import lax
from jax.experimental import pallas as pl
from jax.experimental.pallas import tpu as pltpu
from jax.sharding import PartitionSpec as P

BF = jnp.bfloat16
F32 = jnp.float32
I32 = jnp.int32
MIB = 1 << 20


def dot(a, b, dims=((1,), (0,))):
    return lax.dot_general(a, b, (dims, ((), ())), preferred_element_type=F32)


def one_hot(count, row):
    ids = lax.broadcasted_iota(I32, (count, row.shape[1]), 0)
    return (ids == row).astype(F32).astype(BF)


def split3(x):
    hi = x.astype(BF)
    rest = x - hi.astype(F32)
    mid = rest.astype(BF)
    lo = (rest - mid.astype(F32)).astype(BF)
    return hi, mid, lo


def slot_order(bases):
    half = bases // 2
    return [
        c * half + (x % 2) * 8 + y * 2 + x // 2
        for c in range(2)
        for x in range(4)
        for y in range(half // 4)
    ]


def basis_loads(basis_hbm, basis, sems, q):
    part = basis.shape[1]
    lanes = pl.ds(pl.multiple_of(q * part, part), part)
    loads = []
    for c in range(2):
        for x in range(4):
            at = c * 4 + x
            loads.append(
                pltpu.make_async_copy(
                    basis_hbm.at[c, x % 2, :, x // 2, lanes, :],
                    basis.at[pl.ds(at * 4, 4)],
                    sems.at[at],
                )
            )
    return loads


def remote(src, dst, send_sem, recv_sem, z, e):
    return pltpu.make_async_remote_copy(
        src_ref=src,
        dst_ref=dst,
        send_sem=send_sem,
        recv_sem=recv_sem,
        device_id=(z, e),
        device_id_type=pl.DeviceIdType.MESH,
    )


def place_metadata(q, e, src_ref, dst_ref, rel_ref, group_row, counts_ref, meta_ref, n_ent):
    slots = src_ref.shape[1]
    n_e = counts_ref.shape[1]
    pairs, fields, _, lanes = meta_ref.shape
    cap = slots // n_e
    spot = lax.broadcasted_iota(I32, (1, slots), 1)
    peer = lax.div(spot, cap)
    rows16 = lax.broadcasted_iota(I32, (pairs, slots), 0)

    def digits(v):
        return lax.div(v, 32).astype(F32), lax.rem(v, 32).astype(F32)

    hi, lo = digits(group_row[...])
    level = lax.broadcasted_iota(I32, (pairs, group_row.shape[1]), 0)
    table = jnp.where(level == 0, hi, jnp.where(level == 1, lo, 0.0)).astype(BF)
    rel_digits = dot(table, one_hot(group_row.shape[1], rel_ref[...]))
    counts = jnp.broadcast_to(counts_ref[...].astype(F32), (pairs, n_e)).astype(BF)
    limit = dot(counts, one_hot(n_e, peer))[:1]
    live = lax.rem(spot, cap).astype(F32) < limit
    dst = jnp.where(live, dst_ref[...] - peer * n_ent, n_ent)
    values = digits(src_ref[...] - e * n_ent) + digits(dst)
    values = values + (rel_digits[:1], rel_digits[1:2])
    here = rows16 == lax.div(peer, 2)
    stacked = jnp.concatenate([jnp.where(here, v, 0.0) for v in values], axis=0).astype(BF)
    index = lax.broadcasted_iota(I32, (slots, lanes), 0)
    lane = lax.broadcasted_iota(I32, (slots, lanes), 1)
    half = lax.rem(lax.div(index, cap), 2)
    target = half * (lanes // 2) + q * cap + lax.rem(index, cap)
    moved = dot(stacked, (target == lane).astype(F32).astype(BF))
    for f in range(fields):
        hi = moved[2 * f * pairs : (2 * f + 1) * pairs]
        lo = moved[(2 * f + 1) * pairs : (2 * f + 2) * pairs]
        field = (hi * 32.0 + lo + 0.5).astype(I32)
        for t in range(pairs):
            meta_ref[t, f] = field[t : t + 1, :]


def step_kernel(
    n_z,
    n_e,
    src_ref,
    dst_ref,
    rel_ref,
    groups_ref,
    counts_ref,
    feat_ref,
    w_ref,
    cot_ref,
    coef_ref,
    basis_hbm,
    act_ref,
    gf_ref,
    gb_ref,
    group_row,
    meta_ref,
    meta_z,
    meta_all,
    tags,
    line,
    line_rel,
    table,
    feed_out,
    feed_in,
    rows_t,
    coef_t_ref,
    inv_ref,
    pre_self,
    sums_acc,
    sums_ref,
    agg,
    sums_in,
    pre_in,
    scaled,
    scaled_sib,
    agg_sib,
    basis,
    pick,
    pick_src,
    acc,
    back,
    term_x,
    term_y,
    x_in,
    y_in,
    half_x,
    half_y,
    xy_in,
    yx_in,
    done,
    done_in,
    row_out,
    row_in,
    basis_sem,
    sums_send,
    sums_recv,
    act_send,
    act_recv,
    pre_send,
    pre_recv,
    agg_send,
    agg_recv,
    sib_send,
    sib_recv,
    x_send,
    x_recv,
    y_send,
    y_recv,
    xy_send,
    xy_recv,
    yx_send,
    yx_recv,
    move_send,
    move_recv,
    row_send,
    row_recv,
    gf_send,
    gf_recv,
    meta_send,
    meta_recv,
    tag_send,
    tag_recv,
    feed_send,
    feed_recv,
):
    q = lax.axis_index("rel")
    e = lax.axis_index("ent")
    core = lax.rem(e, 2)
    chip = lax.div(e, 2)
    sib = e + 1 - 2 * core
    bases, part, width = basis.shape
    half = bases // 2
    lanes = pl.ds(pl.multiple_of(q * part, part), part)
    x = lax.rem(chip, 4)
    y = lax.div(chip, 4)

    def at_chip(y_at, x_at):
        return (y_at * 4 + x_at) * 2 + core

    to_z = 2 * core + lax.rem(x, 2)
    to_e = (y * 4 + lax.div(x, 2) * 2 + lax.div(q, 2)) * 2 + lax.rem(q, 2)
    from_z = lax.rem(x, 2) * 2 + core
    from_e = (y * 4 + lax.div(x, 2) * 2 + lax.rem(q, 2)) * 2 + lax.div(q, 2)
    keeps = jnp.logical_and(to_z == q, to_e == e)
    moves = jnp.logical_not(keeps)

    barrier = pltpu.get_barrier_semaphore()

    def greet(z, peer):
        pl.semaphore_signal(
            barrier, inc=1, device_id=(z, peer), device_id_type=pl.DeviceIdType.MESH
        )

    for d in range(1, n_z):
        greet(lax.rem(q + d, n_z), e)

    def greet_plane(d, _):
        greet(q, lax.rem(e + d, n_e))
        return 0

    lax.fori_loop(1, n_e, greet_plane, 0)

    @pl.when(moves)
    def _():
        greet(from_z, from_e)

    loads = basis_loads(basis_hbm, basis, basis_sem, q)
    for load in loads:
        load.start()
    table[...] = jnp.zeros_like(table)
    table[:, : coef_ref.shape[1]] = coef_ref[...]
    group_row[...] = jnp.zeros_like(group_row)
    group_row[:, : groups_ref.shape[1]] = groups_ref[...]
    place_metadata(
        q, e, src_ref, dst_ref, rel_ref, group_row, counts_ref, meta_ref, feat_ref.shape[0]
    )
    pre_self[...] = dot(feat_ref[...], w_ref[:, lanes])
    pl.semaphore_wait(barrier, n_z - 1 + n_e - 1 + moves.astype(I32))

    def meta_copy(d, slot):
        z = lax.rem(q + d, n_z)
        return remote(meta_ref, meta_z.at[slot], meta_send.at[d], meta_recv.at[slot], z, e)

    def tag_copy(peer, slot):
        return remote(
            meta_all.at[lax.div(peer, 2)],
            tags.at[slot],
            tag_send.at[peer],
            tag_recv.at[slot],
            q,
            peer,
        )

    def feed_copy(peer, slot):
        return remote(
            feed_out.at[peer], feed_in.at[slot], feed_send.at[peer], feed_recv.at[slot], q, peer
        )

    def start_all(copy):
        def go(d, _):
            copy(lax.rem(e + d, n_e), e).start()
            return 0

        lax.fori_loop(1, n_e, go, 0)

    def wait_all(copy):
        def go(d, _):
            peer = lax.rem(e + d, n_e)
            copy(peer, peer).wait_recv()
            return 0

        lax.fori_loop(1, n_e, go, 0)

    def sent_all(copy):
        def go(d, _):
            copy(lax.rem(e + d, n_e), e).wait_send()
            return 0

        lax.fori_loop(1, n_e, go, 0)

    for d in range(1, n_z):
        meta_copy(d, q).start()
    feat_t = feat_ref[:, lanes].T
    meta = meta_ref[...]
    for d in range(1, n_z):
        slot = lax.rem(q + d, n_z)
        meta_copy(d, slot).wait_recv()
        meta += meta_z[slot]
    meta_all[...] = meta
    start_all(tag_copy)
    tags[e] = meta_all[lax.div(e, 2)]
    n_ent = pick.shape[0]
    pairs = n_e // 2
    wide_lanes = meta_ref.shape[3]
    for t in range(pairs):
        line[:, t * wide_lanes : (t + 1) * wide_lanes] = meta_all[t, 0]
    pick_src[...] = one_hot(n_ent, line[...])
    feed = dot(feat_t, pick_src[...])
    feed_out[...] = feed.T.astype(BF).reshape(feed_out.shape)
    start_all(feed_copy)
    feed_in[e] = feed_out[e]
    wait_all(tag_copy)
    left = lax.broadcasted_iota(I32, (1, wide_lanes), 1) < wide_lanes // 2
    for f, out in ((1, line), (2, line_rel)):
        for t in range(pairs):
            even = tags[2 * t, f]
            odd = tags[2 * t + 1, f]
            even = jnp.where(core == 0, even, pltpu.roll(even, wide_lanes // 2, 1))
            odd = jnp.where(core == 0, pltpu.roll(odd, wide_lanes // 2, 1), odd)
            out[:, t * wide_lanes : (t + 1) * wide_lanes] = jnp.where(left, even, odd)
    which = one_hot(table.shape[1], line_rel[...])
    hi, mid, lo = split3(table[...])
    coef_t = dot(jnp.concatenate([hi, mid, lo], axis=0), which)
    coef_t = coef_t[:bases] + coef_t[bases : 2 * bases] + coef_t[2 * bases : 3 * bases]
    for p, b in enumerate(slot_order(bases)):
        coef_t_ref[p : p + 1, :] = coef_t[b : b + 1, :]
    pick[...] = one_hot(n_ent, line[...])
    degree = dot(pick[...], jnp.ones((pick.shape[1], part), BF))
    inv_ref[...] = 1.0 / jnp.maximum(degree, 1.0)
    sums_acc[...] = jnp.zeros_like(sums_acc)
    wait_all(feed_copy)
    rows_t[...] = feed_in[...].reshape(pick.shape[1], part).astype(F32).T
    for load in loads:
        load.wait()
    pair = 8
    chunk = n_ent // 2
    steps = bases // pair

    def forward_half(h, first, last):
        rows = pl.ds(h * chunk, chunk)

        def forward_step(i, _):
            at = i * pair
            mixed = jnp.concatenate(
                [
                    (rows_t[...] * coef_t_ref[pl.ds(at + g, 1), :]).astype(BF)
                    for g in range(pair)
                ],
                axis=0,
            )
            out = dot(pick[rows, :], mixed, ((1,), (1,)))
            weights = basis[pl.ds(at, pair)].reshape(pair * part, width)
            sums_acc[rows, :] += dot(out.astype(BF), weights)
            agg[pl.ds(at, pair), :, rows] = out.T.astype(BF).reshape(pair, part, chunk)
            return 0

        lax.fori_loop(first, last, forward_step, 0)

    agg_copy = remote(
        agg.at[pl.ds((1 - core) * half, half)], agg_sib, agg_send, agg_recv, q, sib
    )

    def sums_copy(d, slot, h):
        z = lax.rem(q + d, n_z)
        at = pl.ds(h * chunk, chunk)
        return remote(
            sums_ref.at[z, at],
            sums_in.at[slot, at],
            sums_send.at[d, h],
            sums_recv.at[slot, h],
            z,
            e,
        )

    def pre_copy(d, slot, h):
        z = lax.rem(q + d, n_z)
        at = pl.ds(h * chunk, chunk)
        return remote(
            pre_in.at[q, at], pre_in.at[slot, at], pre_send.at[d, h], pre_recv.at[slot, h], z, e
        )

    def sib_copy(h):
        at = pl.ds(h * chunk, chunk)
        return remote(
            scaled.at[at], scaled_sib.at[at], sib_send.at[h], sib_recv.at[h], q, sib
        )

    def send_sums(h):
        at = pl.ds(h * chunk, chunk)
        for r in range(n_z):
            sums_ref[r, at] = sums_acc[at, r * part : (r + 1) * part].astype(BF)
        for d in range(1, n_z):
            sums_copy(d, q, h).start()

    def activate(h):
        at = pl.ds(h * chunk, chunk)
        total = sums_ref[q, at].astype(F32)
        for d in range(1, n_z):
            slot = lax.rem(q + d, n_z)
            sums_copy(d, slot, h).wait_recv()
            total += sums_in[slot, at].astype(F32)
        pre = pre_self[at] + total * inv_ref[at]
        sig = jax.nn.sigmoid(pre)
        slope = sig * (1.0 + pre * (1.0 - sig))
        pre_in[q, at] = (cot_ref[at, lanes].astype(F32) * slope).astype(BF)
        for d in range(1, n_z):
            pre_copy(d, q, h).start()
        act_ref[at, lanes] = (pre * sig).astype(BF)

    forward_half(0, 0, steps)
    send_sums(0)
    forward_half(1, 0, steps - 1)
    activate(0)
    forward_half(1, steps - 1, steps)
    send_sums(1)
    agg_copy.start()
    activate(1)

    def act_copy(d, z_in):
        z = lax.rem(q + d, n_z)
        at = pl.ds(pl.multiple_of(z_in * part, part), part)
        return remote(
            act_ref.at[:, lanes], act_ref.at[:, at], act_send.at[d], act_recv.at[z_in], z, e
        )

    for h in range(2):
        at = pl.ds(h * chunk, chunk)
        for d in range(1, n_z):
            pre_copy(d, lax.rem(q + d, n_z), h).wait_recv()
        inverse = inv_ref[at]
        for z in range(n_z):
            part_in = pre_in[z, at].astype(F32) * inverse
            scaled[at, z * part : (z + 1) * part] = part_in.astype(BF)
        sib_copy(h).start()
    w_rows = w_ref[lanes, :]
    grad = dot(pre_in[0], w_rows[:, :part], ((1,), (1,)))
    for z in range(1, n_z):
        grad += dot(pre_in[z], w_rows[:, z * part : (z + 1) * part], ((1,), (1,)))
    group = 4

    def back_step(i, _):
        weights = basis[pl.ds(i * group, group)].reshape(group * part, width)
        back[i] = dot(weights, scaled[...], ((1,), (1,))).astype(BF)
        return 0

    lax.fori_loop(0, bases // group, back_step, 0)

    agg_copy.wait_recv()
    for h in range(2):
        sib_copy(h).wait_recv()
    wide = width // 2

    def x_first(d, slot):
        peer = lax.rem(x + d, 4)
        return remote(
            term_x.at[peer], x_in.at[slot], x_send.at[d], x_recv.at[slot], q, at_chip(y, peer)
        )

    def y_first(d, slot):
        peer = lax.rem(y + d, 4)
        return remote(
            term_y.at[peer], y_in.at[slot], y_send.at[d], y_recv.at[slot], q, at_chip(peer, x)
        )

    def x_then_y(d, slot):
        peer = lax.rem(y + d, 4)
        return remote(
            half_x.at[peer], xy_in.at[slot], xy_send.at[d], xy_recv.at[slot], q, at_chip(peer, x)
        )

    def y_then_x(d, slot):
        peer = lax.rem(x + d, 4)
        return remote(
            half_y.at[peer], yx_in.at[slot], yx_send.at[d], yx_recv.at[slot], q, at_chip(y, peer)
        )

    for d in (2, 1, 3, 0):
        at = lax.rem(x + d, 4)
        own = agg[pl.ds(core * half + at * group, group)].reshape(group * part, n_ent)
        other = agg_sib[pl.ds(at * group, group)].reshape(group * part, n_ent)
        terms = dot(own, scaled[...]) + dot(other, scaled_sib[...])
        terms = terms.astype(BF)
        term_x[at] = terms[:, :wide].reshape(group, part, wide)
        for g in range(group):
            term_y[g, at] = terms[g * part : (g + 1) * part, wide:]
        if d:
            x_first(d, x).start()
    for d in (2, 1, 3):
        y_first(d, y).start()
    for d in range(1, n_z):
        act_copy(d, q).start()
    seg = acc.shape[1]

    def spread(n):
        at = pl.ds(pl.multiple_of(n * seg, seg), seg)
        acc[...] = jnp.zeros_like(acc)

        def step(i, _):
            out = dot(back[i], pick[:, at])
            rows = acc[...]
            for g in range(group):
                rows += out[g * part : (g + 1) * part] * coef_t_ref[pl.ds(i * group + g, 1), at]
            acc[...] = rows
            return 0

        lax.fori_loop(0, bases // group, step, 0)
        block = row_out.shape[1]
        rows = acc[...].T.astype(BF).reshape(seg // block, block, part)
        row_out[pl.ds(n * (seg // block), seg // block)] = rows

    def row_copy(peer, slot):
        return remote(
            row_out.at[peer], row_in.at[slot], row_send.at[peer], row_recv.at[slot], q, peer
        )

    def row_start(peer, _):
        @pl.when(peer != e)
        def _():
            row_copy(peer, e).start()

        return 0

    per_seg = n_e * seg // pick.shape[1]
    for d in (2, 1, 3, 0):
        n = lax.rem(y + d, n_e // per_seg)
        spread(n)
        lax.fori_loop(n * per_seg, (n + 1) * per_seg, row_start, 0)
    row_in[e] = row_out[e]

    def add_up(own, arrived, recv, me):
        total = own.astype(F32)
        for d in (1, 3, 2):
            slot = lax.rem(me + d, 4)
            recv(d, slot).wait_recv()
            total += arrived[slot].astype(F32)
        return total

    half_x[...] = add_up(term_x[x], x_in, x_first, x).astype(BF)
    for d in (2, 1, 3):
        x_then_y(d, y).start()
    half_y[...] = add_up(term_y[y], y_in, y_first, y).astype(BF)
    for d in (2, 1, 3):
        y_then_x(d, x).start()
    wait_all(row_copy)
    grad += dot(pick_src[...], row_in[...].reshape(pick_src.shape[1], part))
    gf_ref[:, lanes] = grad.astype(BF)

    def gf_copy(d, z_in):
        z = lax.rem(q + d, n_z)
        at = pl.ds(pl.multiple_of(z_in * part, part), part)
        return remote(
            gf_ref.at[:, lanes], gf_ref.at[:, at], gf_send.at[d], gf_recv.at[z_in], z, e
        )

    for d in range(1, n_z):
        gf_copy(d, q).start()
    done[:, :wide] = add_up(half_x[y], xy_in, x_then_y, y).astype(BF)
    done[:, wide:] = add_up(half_y[x], yx_in, y_then_x, x).astype(BF)
    move = remote(done, done_in, move_send, move_recv, to_z, to_e)

    @pl.when(keeps)
    def _():
        done_in[...] = done[...]

    @pl.when(moves)
    def _():
        move.start()

    for d in range(1, n_z):
        z = lax.rem(q + d, n_z)
        act_copy(d, z).wait_recv()
        act_copy(d, q).wait_send()
        meta_copy(d, q).wait_send()
        for h in range(2):
            sums_copy(d, q, h).wait_send()
            pre_copy(d, q, h).wait_send()
    agg_copy.wait_send()
    for h in range(2):
        sib_copy(h).wait_send()
    for d in (1, 2, 3):
        x_first(d, x).wait_send()
        y_first(d, y).wait_send()
        x_then_y(d, y).wait_send()
        y_then_x(d, x).wait_send()
    sent_all(tag_copy)
    sent_all(feed_copy)
    sent_all(row_copy)

    @pl.when(moves)
    def _():
        move.wait_send()
        remote(done, done_in, move_send, move_recv, from_z, from_e).wait_recv()

    gb_ref[...] = done_in[...].astype(F32)

    for d in range(1, n_z):
        z = lax.rem(q + d, n_z)
        gf_copy(d, z).wait_recv()
        gf_copy(d, q).wait_send()


def run_step(src, dst, rel, groups, counts, features, w_self, cotangent, coeffs, basis_mats):
    n_z = lax.axis_size("rel")
    n_e = lax.axis_size("ent")
    n_ent, width = features.shape
    bases = coeffs.shape[0]
    all_slots = src.shape[1] * n_z
    part = width // n_z
    half = bases // 2
    block = all_slots // n_e
    vm = pl.BlockSpec(memory_space=pltpu.VMEM)
    dma = pltpu.SemaphoreType.DMA
    return pl.pallas_call(
        functools.partial(step_kernel, n_z, n_e),
        out_shape=(
            jax.ShapeDtypeStruct((n_ent, width), BF),
            jax.ShapeDtypeStruct((n_ent, width), BF),
            jax.ShapeDtypeStruct((part, width), F32),
        ),
        in_specs=[vm] * 9 + [pl.BlockSpec(memory_space=pl.ANY)],
        out_specs=(vm, vm, vm),
        scratch_shapes=[
            pltpu.VMEM((1, 256), I32),
            pltpu.VMEM((n_e // 2, 3, 1, 128), I32),
            pltpu.VMEM((n_z, n_e // 2, 3, 1, 128), I32),
            pltpu.VMEM((n_e // 2, 3, 1, 128), I32),
            pltpu.VMEM((n_e, 3, 1, 128), I32),
            pltpu.VMEM((1, all_slots), I32),
            pltpu.VMEM((1, all_slots), I32),
            pltpu.VMEM((bases, 1024), F32),
            pltpu.VMEM((n_e, block, part), BF),
            pltpu.VMEM((n_e, block, part), BF),
            pltpu.VMEM((part, all_slots), F32),
            pltpu.VMEM((bases, all_slots), F32),
            pltpu.VMEM((n_ent, part), F32),
            pltpu.VMEM((n_ent, part), F32),
            pltpu.VMEM((n_ent, width), F32),
            pltpu.VMEM((n_z, n_ent, part), BF),
            pltpu.VMEM((bases, part, n_ent), BF),
            pltpu.VMEM((n_z, n_ent, part), BF),
            pltpu.VMEM((n_z, n_ent, part), BF),
            pltpu.VMEM((n_ent, width), BF),
            pltpu.VMEM((n_ent, width), BF),
            pltpu.VMEM((half, part, n_ent), BF),
            pltpu.VMEM((bases, part, width), BF),
            pltpu.VMEM((n_ent, all_slots), BF),
            pltpu.VMEM((n_ent, all_slots), BF),
            pltpu.VMEM((part, all_slots // 4), F32),
            pltpu.VMEM((bases // 4, 4 * part, n_ent), BF),
            pltpu.VMEM((4, 4, part, width // 2), BF),
            pltpu.VMEM((4, 4, part, width // 2), BF),
            pltpu.VMEM((4, 4, part, width // 2), BF),
            pltpu.VMEM((4, 4, part, width // 2), BF),
            pltpu.VMEM((4, part, width // 2), BF),
            pltpu.VMEM((4, part, width // 2), BF),
            pltpu.VMEM((4, part, width // 2), BF),
            pltpu.VMEM((4, part, width // 2), BF),
            pltpu.VMEM((part, width), BF),
            pltpu.VMEM((part, width), BF),
            pltpu.VMEM((n_e, block, part), BF),
            pltpu.VMEM((n_e, block, part), BF),
            dma((bases // 4,)),
            dma((n_z, 2)),
            dma((n_z, 2)),
            dma((n_z,)),
            dma((n_z,)),
            dma((n_z, 2)),
            dma((n_z, 2)),
            dma,
            dma,
            dma((2,)),
            dma((2,)),
            dma((4,)),
            dma((4,)),
            dma((4,)),
            dma((4,)),
            dma((4,)),
            dma((4,)),
            dma((4,)),
            dma((4,)),
            dma,
            dma,
            dma((n_e,)),
            dma((n_e,)),
            dma((n_z,)),
            dma((n_z,)),
            dma((n_z,)),
            dma((n_z,)),
            dma((n_e,)),
            dma((n_e,)),
            dma((n_e,)),
            dma((n_e,)),
        ],
        compiler_params=pltpu.CompilerParams(
            vmem_limit_bytes=56 * MIB, collective_id=0, has_side_effects=True
        ),
    )(
        src,
        dst,
        rel,
        groups,
        counts,
        features,
        w_self,
        cotangent,
        coeffs,
        basis_mats.reshape(2, 2, 4, 2, width, width),
    )


def store_kernel(a_in, b_in, c_in, a_out, b_out, c_out, a_mid, b_mid, c_mid, sems):
    arrays = ((c_in, c_mid, c_out), (a_in, a_mid, a_out), (b_in, b_mid, b_out))
    loads = [
        pltpu.make_async_copy(i, m, sems.at[0, n]) for n, (i, m, _) in enumerate(arrays)
    ]
    stores = [
        pltpu.make_async_copy(m, o, sems.at[1, n]) for n, (_, m, o) in enumerate(arrays)
    ]
    for load in loads:
        load.start()
    for load, save in zip(loads, stores):
        load.wait()
        save.start()
    for save in stores:
        save.wait()


def store(arrays):
    hbm = pl.BlockSpec(memory_space=pl.ANY)
    return pl.pallas_call(
        store_kernel,
        out_shape=tuple(jax.ShapeDtypeStruct(a.shape, a.dtype) for a in arrays),
        in_specs=[hbm] * 3,
        out_specs=(hbm,) * 3,
        scratch_shapes=[pltpu.VMEM(a.shape, a.dtype) for a in arrays]
        + [pltpu.SemaphoreType.DMA((2, 3))],
    )(*arrays)


def per_device(
    features,
    w_self,
    basis_mats,
    basis_coeffs,
    group_rels,
    rel_local,
    edge_src,
    edge_dst,
    block_counts,
    cotangent,
):
    outs = run_step(
        edge_src[None],
        edge_dst[None],
        rel_local[None],
        group_rels[None],
        block_counts[0],
        features,
        w_self,
        cotangent,
        basis_coeffs.T,
        basis_mats,
    )
    return store(outs)


def solution(mesh):
    placed = (
        P("ent", None),
        P(),
        P(),
        P(),
        P("rel"),
        P(("rel", "ent")),
        P(("rel", "ent")),
        P(("rel", "ent")),
        P("rel", "ent", None),
        P("ent", None),
    )
    return jax.shard_map(
        per_device,
        mesh=mesh,
        in_specs=placed,
        out_specs=(P("ent", None), P("ent", None), P(("rel", "ent"), None)),
        check_vma=False,
    )
```
